32 devices in a mesh: rep: 4 (over x, core), fsdp: 8 (over z, y).
Axes of the slice: x: 2, y: 2, z: 4, core: 2. Of those that a mesh axis runs over, the one named last changes fastest.
Arguments:
- inputs: bfloat16 [2, 8192, 1024], P(None, ('rep', 'fsdp')), may hold values from -6 to 6
- cotangent: bfloat16 [2, 8192, 1024], P(None, ('rep', 'fsdp')), may hold values from -6 to 6
- lengths: int32 [2, 32], replicated, may hold values from 128 to 256, as said below
- norm_one: bfloat16 [1024], P('fsdp'), may hold values from 0.5 to 1.5
- w_in: bfloat16 [1024, 3072], P('fsdp'), may hold values from -0.1875 to 0.1875
- conv_w: bfloat16 [3, 1024], P(None, 'fsdp'), may hold values from -3.5 to 3.5
- w_out: bfloat16 [1024, 1024], P('fsdp'), may hold values from -0.1875 to 0.1875
- norm_two: bfloat16 [1024], P('fsdp'), may hold values from 0.5 to 1.5
- w_gate: bfloat16 [1024, 4608], P('fsdp'), may hold values from -0.1875 to 0.1875
- w_up: bfloat16 [1024, 4608], P('fsdp'), may hold values from -0.1875 to 0.1875
- w_down: bfloat16 [4608, 1024], P('fsdp'), may hold values from -0.125 to 0.125
Outputs:
- outputs: float32 [2, 8192, 1024], P(None, ('rep', 'fsdp'))
- d_inputs: float32 [2, 8192, 1024], P(None, ('rep', 'fsdp'))
- d_norm_one: float32 [1024], P('fsdp')
- d_w_in: float32 [1024, 3072], P('fsdp')
- d_conv_w: float32 [3, 1024], P(None, 'fsdp')
- d_w_out: float32 [1024, 1024], P('fsdp')
- d_norm_two: float32 [1024], P('fsdp')
- d_w_gate: float32 [1024, 4608], P('fsdp')
- d_w_up: float32 [1024, 4608], P('fsdp')
- d_w_down: float32 [4608, 1024], P('fsdp')
The draws below stay inside these ranges and needn't reach their ends.
Inputs may be any that keep to these rules, and one draw needn't show every extreme that they name: `lengths`: in every micro-batch one slot holds exactly 256 live tokens and one exactly 128.
All inputs are finite; a program needn't handle non-finite values.
Results may differ from the reference program's by a relative error of at most 0.012.
Values may be sent and summed in bfloat16 or wider, within the bound.
A program may use at most 256 MiB of HBM per device.

```python
import jax
import jax.numpy as jnp
from jax import lax

D = 1024
FF = 4608
MICRO = 2
SLOT = 256
SLOTS = 32
ROWS = 8192


def draw_lengths(key, part):
    key_vals = jax.random.fold_in(key, 11)
    key_long = jax.random.fold_in(key, 23)
    key_short = jax.random.fold_in(key, 37)
    values = jax.random.randint(key_vals, (MICRO, SLOTS), SLOT // 2, SLOT + 1, dtype=jnp.int32)
    longest = jax.random.randint(key_long, (MICRO,), 0, SLOTS, dtype=jnp.int32)
    step_over = jax.random.randint(key_short, (MICRO,), 1, SLOTS, dtype=jnp.int32)
    shortest = (longest + step_over) % SLOTS
    column = jnp.arange(SLOTS, dtype=jnp.int32)[None, :]
    values = jnp.where(column == longest[:, None], SLOT, values)
    values = jnp.where(column == shortest[:, None], SLOT // 2, values)
    return values.astype(jnp.int32)


def spiked(values, key, source, target, blocks, factor):
    def block_of(axis_at):
        return (jnp.arange(values.shape[axis_at]) // (values.shape[axis_at] // blocks)).reshape((-1,) + (1,) * (values.ndim - 1 - axis_at))

    near = jax.random.permutation(key, blocks)[block_of(target)]
    far = (block_of(target) + blocks // 2) % blocks
    return jnp.where((block_of(source) == near) | (block_of(source) == far), factor * values, values)


def block_levels(key, dims, split, low, high):
    gain, own = 1.0, jax.random.fold_in(key, 6)
    for dim, blocks in split:
        heights = jnp.exp(jax.random.uniform(jax.random.fold_in(own, dim), (blocks,), jnp.float32, low / len(split), high / len(split)))
        gain = gain * jnp.repeat(heights, dims[dim] // blocks).reshape([-1 if axis == dim else 1 for axis in range(len(dims))])
    return gain


def centred(rng, dims, spread, most, pieces=(), held_as=jnp.bfloat16):
    entries = jax.random.normal(rng, dims, jnp.float32) * spread
    if len(pieces) > 0:
        entries = block_levels(rng, dims, pieces, -0.22, 0.18) * entries
    return jnp.clip(entries, min=-most, max=most).astype(held_as)


def noise_with(own_key, dims, deviation, most, shards, heavy, kind=jnp.bfloat16):
    entries = deviation * jax.random.normal(own_key, dims, jnp.float32)
    if shards:
        entries = entries * block_levels(own_key, dims, shards, -0.22, 0.18)
    return jnp.clip(spiked(entries, jax.random.fold_in(own_key, 3), *heavy), -most, most).astype(kind)


def setup_inputs(seed: int = 0) -> dict:
    seeds = jax.random.split(jax.random.key(seed), 12)
    return {
        "inputs": noise_with(seeds[0], (MICRO, ROWS, D), 1.0, 6.0, ((1, 32),), (1, 2, 32, 2.75)),
        "cotangent": noise_with(seeds[1], (MICRO, ROWS, D), 1.0, 6.0, ((1, 32),), (1, 2, 32, 2.75)),
        "lengths": draw_lengths(jax.random.fold_in(seeds[11], 71), 0),
        "norm_one": jnp.clip(1.0 + 0.1 * jax.random.normal(seeds[3], (D,), jnp.float32), 0.5, 1.5).astype(jnp.bfloat16),
        "w_in": centred(seeds[4], (D, 3 * D), D ** -0.5, 0.1875, ((0, 8),)),
        "conv_w": centred(seeds[5], (3, D), 3 ** -0.5, 3.5, ((1, 8),)),
        "w_out": centred(seeds[6], (D, D), D ** -0.5, 0.1875, ((0, 8),)),
        "norm_two": jnp.clip(1.0 + 0.1 * jax.random.normal(seeds[7], (D,), jnp.float32), 0.5, 1.5).astype(jnp.bfloat16),
        "w_gate": centred(seeds[8], (D, FF), D ** -0.5, 0.1875, ((0, 8),)),
        "w_up": centred(seeds[9], (D, FF), D ** -0.5, 0.1875, ((0, 8),)),
        "w_down": centred(seeds[10], (FF, D), (FF // 2) ** -0.5, 0.125, ((0, 8),)),
    }


EPSILON = 1e-05
HIGH = lax.Precision.HIGHEST

@jax.custom_vjp
def low(v):
    return lax.optimization_barrier(v.astype(jnp.bfloat16)).astype(jnp.float32)

@jax.custom_vjp
def low_back(v):
    return v

def low_keep(v):
    return (low(v), None)

def low_pass(kept, grad):
    return (grad,)

def back_keep(v):
    return (v, None)

def back_low(kept, grad):
    return (low(grad),)
low.defvjp(low_keep, low_pass)
low_back.defvjp(back_keep, back_low)

def block_forward(block_x, norm_one, w_in, conv_w, w_out, norm_two, w_gate, w_up, w_down):
    features = block_x.shape[-1]
    scale_one = lax.rsqrt(lax.optimization_barrier(jnp.mean(block_x * block_x, axis=-1, keepdims=True)) + EPSILON)
    act_one = low(block_x * scale_one * norm_one)
    projected = low_back(jnp.einsum('gsd,de->gse', act_one, w_in, precision=HIGH))
    part_b = projected[..., :features]
    part_c = projected[..., features:2 * features]
    part_x = projected[..., 2 * features:]
    product = part_b * part_x
    padded = jnp.pad(product, ((0, 0), (2, 0), (0, 0)))
    convolved = conv_w[0] * padded[:, :-2] + conv_w[1] * padded[:, 1:-1] + conv_w[2] * padded[:, 2:]
    mixer_in = low(part_c * convolved)
    hstate = block_x + low_back(jnp.einsum('gsd,de->gse', mixer_in, w_out, precision=HIGH))
    scale_two = lax.rsqrt(lax.optimization_barrier(jnp.mean(hstate * hstate, axis=-1, keepdims=True)) + EPSILON)
    act_two = low(hstate * scale_two * norm_two)
    gate_pre = low_back(jnp.einsum('gsd,df->gsf', act_two, w_gate, precision=HIGH))
    up_pre = low_back(jnp.einsum('gsd,df->gsf', act_two, w_up, precision=HIGH))
    hidden = low(jax.nn.silu(gate_pre) * up_pre)
    return hstate + jnp.einsum('gsf,fd->gsd', hidden, w_down, precision=HIGH)

def reference(inputs, cotangent, lengths, norm_one, w_in, conv_w, w_out, norm_two, w_gate, w_up, w_down):
    weights = tuple((w.astype(jnp.float32) for w in (norm_one, w_in, conv_w, w_out, norm_two, w_gate, w_up, w_down)))
    slots_all = MICRO * SLOTS
    limit = max(4096, SLOT)
    slots_block = max((c for c in range(1, slots_all + 1) if slots_all % c == 0 and c * SLOT <= limit))
    block_count = slots_all // slots_block
    position = jnp.arange(SLOT, dtype=jnp.int32)
    live_rows = (position[None, :] < lengths.reshape(slots_all).astype(jnp.int32)[:, None]).astype(jnp.float32)
    rows_x = inputs.astype(jnp.float32).reshape(slots_all, SLOT, D)
    cotan_rows = cotangent.astype(jnp.float32).reshape(slots_all, SLOT, D) * live_rows[:, :, None]
    rows_x = rows_x.reshape(block_count, slots_block, SLOT, D)
    cotan_rows = cotan_rows.reshape(block_count, slots_block, SLOT, D)

    def scan_step(totals, pair_in):
        block_x, block_cot = pair_in
        block_out, pullback = jax.vjp(block_forward, block_x, *weights)
        grads = pullback(block_cot)
        return (tuple((a + b for a, b in zip(totals, grads[1:]))), (block_out, grads[0]))
    start = tuple((jnp.zeros_like(w) for w in weights))
    totals, (outs_all, dx_all) = lax.scan(scan_step, start, (rows_x, cotan_rows))
    outputs = outs_all.reshape(MICRO, SLOTS * SLOT, D)
    d_inputs = dx_all.reshape(MICRO, SLOTS * SLOT, D)
    return (outputs, d_inputs, totals[0], totals[1], totals[2], totals[3], totals[4], totals[5], totals[6], totals[7])
```

```python
import jax
import jax.numpy as jnp
from jax import lax
from jax.sharding import PartitionSpec as P

EPSILON = 1e-05
LOW = jnp.bfloat16
F32 = jnp.float32


def hop(values, axis, bit):
    size = lax.axis_size(axis)
    return lax.ppermute(values, axis, [(at, at ^ bit) for at in range(size)])


def after(values, *earlier):
    return lax.optimization_barrier((values, *earlier))[0]


def gather_bits():
    size = lax.axis_size("fsdp")
    bits = [1 << k for k in range(size.bit_length() - 1)]
    return bits[1:] + bits[:1]


def gather_pieces(own):
    pieces = {0: own}
    for bit in gather_bits():
        for offset in list(pieces):
            pieces[offset ^ bit] = hop(pieces[offset], "fsdp", bit)
    return pieces


def put(target, block, index):
    return lax.dynamic_update_slice(target, block, index + (0,) * (target.ndim - len(index)))


def in_order(pieces, place):
    shards = len(pieces)
    whole = jnp.zeros((shards, *pieces[0].shape), pieces[0].dtype)
    for offset, piece in pieces.items():
        whole = put(whole, piece[None], (place ^ offset,))
    return whole


def reduce_pieces(whole, kind=LOW):
    place = lax.axis_index("fsdp")
    shards = whole.shape[0]
    bits = gather_bits()[::-1]
    top = shards.bit_length() - 1
    rest = whole.shape[1:]
    held = whole.reshape((2,) * top + rest)
    axes = [1 << k for k in reversed(range(top))]
    for bit in bits:
        axis = axes.index(bit)
        mine = jnp.where((place & bit) != 0, 1, 0)
        sent = lax.dynamic_index_in_dim(held, 1 - mine, axis, keepdims=False).astype(kind)
        kept = lax.dynamic_index_in_dim(held, mine, axis, keepdims=False).astype(F32)
        total = kept + hop(sent, "fsdp", bit).astype(F32)
        axes.pop(axis)
        held = total.astype(kind) if axes else total
    return held


def rms_scale(values):
    return lax.rsqrt(jnp.mean(values * values, axis=-1, keepdims=True) + EPSILON)


def dot(left, right):
    return jnp.dot(left, right, preferred_element_type=F32)


def dot_last(left, right):
    return lax.dot_general(left, right, (((1,), (1,)), ((), ())), preferred_element_type=F32)


def dot_first(left, right):
    return lax.dot_general(left, right, (((0,), (0,)), ((), ())), preferred_element_type=F32)


def norm_back(d_act, values, scale, gain):
    scaled = d_act * gain
    return scale * (
        scaled - values * scale * scale * jnp.mean(scaled * values, axis=-1, keepdims=True)
    )


def sum_over_rep(own_and_core, across):
    rows = own_and_core.shape[0] // 2
    near = hop(own_and_core[rows:].astype(LOW), "rep", 1).astype(F32)
    far = hop(across[rows:].astype(LOW), "rep", 1).astype(F32)
    own = own_and_core[:rows] + near
    other = (across[:rows] + far).astype(LOW)
    return own + hop(other, "rep", 2).astype(F32)


def spread_over_rep(values):
    near = hop(values, "rep", 1)
    across = hop(values, "rep", 2)
    return jnp.concatenate([values, near]), jnp.concatenate([across, hop(across, "rep", 1)])


def share_quarters(quarter):
    rep = lax.axis_index("rep")
    near = hop(quarter, "rep", 1)
    across = hop(quarter, "rep", 2)
    corner = hop(across, "rep", 1)
    whole = jnp.zeros((4, *quarter.shape), quarter.dtype)
    for offset, block in enumerate((quarter, near, across, corner)):
        whole = put(whole, block[None], (rep ^ offset,))
    return whole


def gather_full(weight, *earlier):
    rep = lax.axis_index("rep")
    place = lax.axis_index("fsdp")
    rows, cols = weight.shape
    quarter = rows // 4
    own = lax.dynamic_slice_in_dim(weight, rep * quarter, quarter, 0)
    pieces = gather_pieces(after(own, *earlier) if earlier else own)
    shards = len(pieces)
    whole = jnp.zeros((shards, 4, quarter, cols), weight.dtype)
    whole = put(whole, weight.reshape(1, 4, quarter, cols), (place,))
    for flip in (0, 1):
        group = {o: p for o, p in pieces.items() if o & 1 == flip and o}
        offsets = sorted(group)
        stacked = jnp.stack([group[o] for o in offsets])
        across = hop(stacked, "rep", 2)
        near = hop(stacked, "rep", 1)
        corner = hop(across, "rep", 1)
        for turn, block in enumerate((stacked, near, across, corner)):
            for at, offset in enumerate(offsets):
                whole = put(whole, block[at][None, None], (place ^ offset, rep ^ turn))
    return whole.reshape(shards * rows, cols), pieces


def reduce_full(grad):
    rep = lax.axis_index("rep")
    shards = lax.axis_size("fsdp")
    rows, cols = grad.shape
    quarter = rows // shards // 4
    held = grad.reshape(shards, 2, 2, quarter, cols)
    core, side = rep & 1, (rep >> 1) & 1
    sent = lax.dynamic_index_in_dim(held, 1 - core, 2, keepdims=False).astype(LOW)
    kept = lax.dynamic_index_in_dim(held, core, 2, keepdims=False)
    pair = (kept.astype(F32) + hop(sent, "rep", 1).astype(F32)).astype(LOW)
    sent = lax.dynamic_index_in_dim(pair, 1 - side, 1, keepdims=False)
    kept = lax.dynamic_index_in_dim(pair, side, 1, keepdims=False)
    four = kept.astype(F32) + hop(sent, "rep", 2).astype(F32)
    own = reduce_pieces(four).astype(LOW)
    return share_quarters(own).reshape(4 * quarter, cols).astype(F32)


def on_device(
    inputs, cotangent, lengths, norm_one, w_in, conv_w, w_out, norm_two, w_gate, w_up, w_down
):
    micro_count, tok_rows, features = inputs.shape
    shards = lax.axis_size("fsdp")
    place = lax.axis_index("fsdp")
    rep = lax.axis_index("rep")
    all_rows = micro_count * tok_rows
    hidden_own = w_down.shape[0]
    cut = hidden_own // 4
    part_ff = shards * cut

    small = jnp.concatenate([norm_one[None], norm_two[None], conv_w, jnp.zeros_like(conv_w)])
    small_all = in_order(gather_pieces(small), place)
    small_all = jnp.moveaxis(small_all, 0, 1).reshape(8, features).astype(F32)
    g_one, g_two, taps = small_all[0], small_all[1], small_all[2:5]

    m_in, in_pieces = gather_full(w_in)
    m_out, out_pieces = gather_full(w_out, in_pieces[2])
    gate_own = lax.dynamic_index_in_dim(
        w_gate.reshape(-1, shards, 4, cut), rep, 2, keepdims=False
    ).reshape(-1, part_ff)
    up_own = lax.dynamic_index_in_dim(
        w_up.reshape(-1, shards, 4, cut), rep, 2, keepdims=False
    ).reshape(-1, part_ff)
    down_own = lax.dynamic_slice_in_dim(w_down, rep * cut, cut, 0)
    gate_pieces = gather_pieces(after(gate_own, in_pieces[4]))
    up_pieces = gather_pieces(after(up_own, gate_pieces[4]))
    down_pieces = gather_pieces(after(down_own, up_pieces[4]))
    m_gate = in_order(gate_pieces, place).reshape(features, part_ff)
    m_up = in_order(up_pieces, place).reshape(features, part_ff)
    m_down = in_order(down_pieces, place).reshape(part_ff, features)

    slot_cols = jnp.arange(lengths.shape[1], dtype=jnp.int32)
    slot_id = rep * shards + place
    length_now = jnp.sum(jnp.where(slot_cols == slot_id, lengths, 0), axis=1)
    position = jnp.arange(tok_rows, dtype=jnp.int32)
    live = (position[None] < length_now[:, None]).astype(F32)[..., None]
    cotan_f = (cotangent.astype(F32) * live).reshape(all_rows, features)
    cotan_low = cotan_f.astype(LOW)
    cot_near, cot_far = spread_over_rep(after(cotan_low, in_pieces[1]))

    rows_f = inputs.reshape(all_rows, features).astype(F32)
    scale_one = rms_scale(rows_f)
    act_one = (rows_f * scale_one * g_one).astype(LOW)
    projected = dot(act_one, m_in)
    part_b = projected[:, :features]
    part_c = projected[:, features : 2 * features]
    part_x = projected[:, 2 * features :]
    product = (part_b * part_x).reshape(micro_count, tok_rows, features)
    padded = jnp.pad(product, ((0, 0), (2, 0), (0, 0)))
    convolved = (
        taps[0] * padded[:, :-2] + taps[1] * padded[:, 1:-1] + taps[2] * padded[:, 2:]
    ).reshape(all_rows, features)
    mixer_in = (part_c * convolved).astype(LOW)
    hstate = rows_f + dot(mixer_in, m_out)
    scale_two = rms_scale(hstate)
    act_two = (hstate * scale_two * g_two).astype(LOW)
    act_near, act_far = spread_over_rep(act_two)

    def units(act, cot):
        gate_pre = dot(act, m_gate)
        up_pre = dot(act, m_up)
        sigmoid_g = jax.nn.sigmoid(gate_pre)
        silu_g = gate_pre * sigmoid_g
        hidden = (silu_g * up_pre).astype(LOW)
        d_hidden = dot_last(cot, m_down)
        d_gate = (d_hidden * up_pre * sigmoid_g * (1.0 + gate_pre * (1.0 - sigmoid_g))).astype(LOW)
        d_up = (d_hidden * silu_g).astype(LOW)
        return hidden, d_gate, d_up

    hidden_n, d_gate_n, d_up_n = units(act_near, cot_near)
    hidden_f, d_gate_f, d_up_f = units(act_far, cot_far)
    grad_down = dot_first(hidden_n, cot_near) + dot_first(hidden_f, cot_far)
    d_act_two = sum_over_rep(
        dot_last(d_gate_n, m_gate) + dot_last(d_up_n, m_up),
        dot_last(d_gate_f, m_gate) + dot_last(d_up_f, m_up),
    )
    grad_gate = dot_first(act_near, d_gate_n) + dot_first(act_far, d_gate_f)
    grad_up = dot_first(act_near, d_up_n) + dot_first(act_far, d_up_f)
    ffn = sum_over_rep(dot(hidden_n, m_down), dot(hidden_f, m_down))
    outputs = (hstate + ffn).reshape(inputs.shape)

    sum_down = reduce_pieces(grad_down.reshape(shards, cut, features))
    sum_gate = reduce_pieces(grad_gate.reshape(shards, -1, part_ff))
    sum_up = reduce_pieces(grad_up.reshape(shards, -1, part_ff))
    all_down = share_quarters(sum_down.astype(LOW)).reshape(hidden_own, features).astype(F32)

    def unit_columns(total):
        quarters = share_quarters(total.astype(LOW)).reshape(4, -1, shards, cut)
        return quarters.transpose(1, 2, 0, 3).reshape(-1, 4 * part_ff).astype(F32)

    all_gate = unit_columns(sum_gate)
    all_up = unit_columns(sum_up)

    grad_two = jnp.sum(d_act_two * hstate * scale_two, axis=0)
    d_hstate = cotan_f + norm_back(d_act_two, hstate, scale_two, g_two)
    d_mixer = d_hstate.astype(LOW)
    grad_out = dot_first(mixer_in, d_mixer)
    d_mixin = dot_last(d_mixer, m_out)
    d_cpart = d_mixin * convolved
    d_conv = (d_mixin * part_c).reshape(micro_count, tok_rows, features)
    trailing = jnp.pad(d_conv, ((0, 0), (0, 2), (0, 0)))
    d_product = (
        taps[2] * d_conv + taps[1] * trailing[:, 1:-1] + taps[0] * trailing[:, 2:]
    ).reshape(all_rows, features)
    grad_conv = [
        jnp.sum(d_conv * padded[:, k : k + tok_rows], axis=(0, 1)) for k in range(3)
    ]
    d_projected = jnp.concatenate(
        [d_product * part_x, d_cpart, d_product * part_b], axis=1
    ).astype(LOW)
    grad_in = dot_first(act_one, d_projected)
    d_act_one = dot_last(d_projected, m_in)
    grad_one = jnp.sum(d_act_one * rows_f * scale_one, axis=0)
    d_rows = d_hstate + norm_back(d_act_one, rows_f, scale_one, g_one)
    d_inputs = d_rows.reshape(inputs.shape)

    all_out = reduce_full(grad_out)
    all_in = reduce_full(grad_in)

    zeros = jnp.zeros_like(grad_one)
    small_grads = jnp.stack([grad_one, grad_two, *grad_conv, zeros, zeros, zeros])
    small_grads = jnp.moveaxis(small_grads.reshape(8, shards, -1), 1, 0)
    small_own = reduce_pieces(small_grads, F32)
    small_own = small_own + hop(small_own, "rep", 1)
    small_own = small_own + hop(small_own, "rep", 2)

    return (
        outputs,
        d_inputs,
        small_own[0],
        all_in,
        small_own[2:5],
        all_out,
        small_own[1],
        all_gate,
        all_up,
        all_down,
    )


def solution(mesh):
    return jax.shard_map(
        on_device,
        mesh=mesh,
        in_specs=(
            P(None, ("rep", "fsdp"), None),
            P(None, ("rep", "fsdp"), None),
            P(),
            P("fsdp"),
            P("fsdp", None),
            P(None, "fsdp"),
            P("fsdp", None),
            P("fsdp"),
            P("fsdp", None),
            P("fsdp", None),
            P("fsdp", None),
        ),
        out_specs=(
            P(None, ("rep", "fsdp"), None),
            P(None, ("rep", "fsdp"), None),
            P("fsdp"),
            P("fsdp", None),
            P(None, "fsdp"),
            P("fsdp", None),
            P("fsdp"),
            P("fsdp", None),
            P("fsdp", None),
            P("fsdp", None),
        ),
        check_vma=False,
    )
```

```python
import functools

import jax
import jax.numpy as jnp
from jax import lax
from jax.experimental import pallas as pl
from jax.experimental.pallas import tpu as pltpu
from jax.sharding import PartitionSpec as P

EPSILON = 1e-05
LOW = jnp.bfloat16
F32 = jnp.float32
MESH = pl.DeviceIdType.MESH


def hop(values, axis, bit):
    size = lax.axis_size(axis)
    return lax.ppermute(values, axis, [(at, at ^ bit) for at in range(size)])


def after(values, *earlier):
    return lax.optimization_barrier((values, *earlier))[0]


def gather_bits():
    size = lax.axis_size("fsdp")
    bits = [1 << k for k in range(size.bit_length() - 1)]
    return bits[1:] + bits[:1]


def gather_pieces(own):
    pieces = {0: own}
    for bit in gather_bits():
        for offset in list(pieces):
            pieces[offset ^ bit] = hop(pieces[offset], "fsdp", bit)
    return pieces


def put(target, block, index):
    return lax.dynamic_update_slice(target, block, index + (0,) * (target.ndim - len(index)))


def in_order(pieces, place):
    shards = len(pieces)
    whole = jnp.zeros((shards, *pieces[0].shape), pieces[0].dtype)
    for offset, piece in pieces.items():
        whole = put(whole, piece[None], (place ^ offset,))
    return whole


def reduce_pieces(whole, kind=LOW):
    place = lax.axis_index("fsdp")
    shards = whole.shape[0]
    bits = gather_bits()[::-1]
    top = shards.bit_length() - 1
    rest = whole.shape[1:]
    held = whole.reshape((2,) * top + rest)
    axes = [1 << k for k in reversed(range(top))]
    for bit in bits:
        axis = axes.index(bit)
        mine = jnp.where((place & bit) != 0, 1, 0)
        sent = lax.dynamic_index_in_dim(held, 1 - mine, axis, keepdims=False).astype(kind)
        kept = lax.dynamic_index_in_dim(held, mine, axis, keepdims=False).astype(F32)
        total = kept + hop(sent, "fsdp", bit).astype(F32)
        axes.pop(axis)
        held = total.astype(kind) if axes else total
    return held


def rms_scale(values):
    return lax.rsqrt(jnp.mean(values * values, axis=-1, keepdims=True) + EPSILON)


def dot(left, right):
    return jnp.dot(left, right, preferred_element_type=F32)


def dot_last(left, right):
    return lax.dot_general(left, right, (((1,), (1,)), ((), ())), preferred_element_type=F32)


def dot_first(left, right):
    return lax.dot_general(left, right, (((0,), (0,)), ((), ())), preferred_element_type=F32)


def norm_back(d_act, values, scale, gain):
    scaled = d_act * gain
    return scale * (
        scaled - values * scale * scale * jnp.mean(scaled * values, axis=-1, keepdims=True)
    )


def sum_over_rep(own_and_core, across):
    rows = own_and_core.shape[0] // 2
    near = hop(own_and_core[rows:].astype(LOW), "rep", 1).astype(F32)
    far = hop(across[rows:].astype(LOW), "rep", 1).astype(F32)
    own = own_and_core[:rows] + near
    other = (across[:rows] + far).astype(LOW)
    return own + hop(other, "rep", 2).astype(F32)


def spread_over_rep(values):
    near = hop(values, "rep", 1)
    across = hop(values, "rep", 2)
    return jnp.concatenate([values, near]), jnp.concatenate([across, hop(across, "rep", 1)])


def share_quarters(quarter):
    rep = lax.axis_index("rep")
    near = hop(quarter, "rep", 1)
    across = hop(quarter, "rep", 2)
    corner = hop(across, "rep", 1)
    whole = jnp.zeros((4, *quarter.shape), quarter.dtype)
    for offset, block in enumerate((quarter, near, across, corner)):
        whole = put(whole, block[None], (rep ^ offset,))
    return whole


def gather_full(weight, *earlier):
    rep = lax.axis_index("rep")
    place = lax.axis_index("fsdp")
    rows, cols = weight.shape
    quarter = rows // 4
    own = lax.dynamic_slice_in_dim(weight, rep * quarter, quarter, 0)
    pieces = gather_pieces(after(own, *earlier) if earlier else own)
    shards = len(pieces)
    whole = jnp.zeros((shards, 4, quarter, cols), weight.dtype)
    whole = put(whole, weight.reshape(1, 4, quarter, cols), (place,))
    for flip in (0, 1):
        group = {o: p for o, p in pieces.items() if o & 1 == flip and o}
        offsets = sorted(group)
        stacked = jnp.stack([group[o] for o in offsets])
        across = hop(stacked, "rep", 2)
        near = hop(stacked, "rep", 1)
        corner = hop(across, "rep", 1)
        for turn, block in enumerate((stacked, near, across, corner)):
            for at, offset in enumerate(offsets):
                whole = put(whole, block[at][None, None], (place ^ offset, rep ^ turn))
    return whole.reshape(shards * rows, cols), pieces


def reduce_full(grad):
    rep = lax.axis_index("rep")
    shards = lax.axis_size("fsdp")
    rows, cols = grad.shape
    quarter = rows // shards // 4
    held = grad.reshape(shards, 2, 2, quarter, cols)
    core, side = rep & 1, (rep >> 1) & 1
    sent = lax.dynamic_index_in_dim(held, 1 - core, 2, keepdims=False).astype(LOW)
    kept = lax.dynamic_index_in_dim(held, core, 2, keepdims=False)
    pair = (kept.astype(F32) + hop(sent, "rep", 1).astype(F32)).astype(LOW)
    sent = lax.dynamic_index_in_dim(pair, 1 - side, 1, keepdims=False)
    kept = lax.dynamic_index_in_dim(pair, side, 1, keepdims=False)
    four = kept.astype(F32) + hop(sent, "rep", 2).astype(F32)
    own = reduce_pieces(four).astype(LOW)
    return share_quarters(own).reshape(4 * quarter, cols).astype(F32)


def flipped(index, offset):
    bit = 1
    while bit <= offset:
        if offset & bit:
            index = index + bit - 2 * bit * ((index // bit) % 2)
        bit *= 2
    return index


class Copies:
    def __init__(self, send_sems, recv_sems):
        self.sems = send_sems, recv_sems
        self.rep = lax.axis_index("rep")
        self.place = lax.axis_index("fsdp")
        self.started = []

    def peer(self, rep_bits, place_bits):
        return (flipped(self.rep, rep_bits), flipped(self.place, place_bits))

    def meet(self, peers):
        barrier = pltpu.get_barrier_semaphore()
        for bits in peers:
            pl.semaphore_signal(barrier, inc=1, device_id=self.peer(*bits), device_id_type=MESH)
        pl.semaphore_wait(barrier, len(peers))

    def send(self, source, target, rep_bits, place_bits):
        at = len(self.started)
        copy = pltpu.make_async_remote_copy(
            src_ref=source,
            dst_ref=target,
            send_sem=self.sems[0].at[at],
            recv_sem=self.sems[1].at[at],
            device_id=self.peer(rep_bits, place_bits),
            device_id_type=MESH,
        )
        copy.start()
        self.started.append(copy)
        return copy

    def close(self):
        for copy in self.started:
            copy.wait_send()


class Local:
    def __init__(self, sems):
        self.sems = sems
        self.started = []

    def copy(self, source, target):
        copy = pltpu.make_async_copy(source, target, self.sems.at[len(self.started)])
        copy.start()
        self.started.append(copy)
        return copy


class Spread:
    def __init__(self, copies, locals_, shards, source, target, at=None):
        self.copies = copies
        self.target = target
        self.at = at if at is not None else (lambda shard: target.at[shard])
        self.source = source
        self.locals = locals_
        self.far = list(range(2, shards, 2))
        self.near = [1] + [offset + 1 for offset in self.far]

    def start(self):
        copies = self.copies
        here = self.at(copies.place)
        self.arriving = {offset: copies.send(self.source, here, 0, offset) for offset in self.far}
        self.arriving[1] = copies.send(self.source, here, 0, 1)
        if self.locals is not None:
            self.own = self.locals.copy(self.source, here)

    def arrive(self, offset):
        self.arriving[offset].wait_recv()
        if offset % 2 == 0:
            block = self.at(flipped(self.copies.place, offset))
            self.arriving[offset + 1] = self.copies.send(block, block, 0, 1)

    def finish(self):
        for offset in self.near:
            self.arriving[offset].wait_recv()
        if self.locals is not None:
            self.own.wait()


class SpreadAll(Spread):
    def __init__(self, copies, locals_, shards, source, target, width):
        self.width = width
        self.whole = source
        self.local_all = locals_
        rep = copies.rep
        super().__init__(
            copies,
            None,
            shards,
            source.at[:, self.columns(rep)],
            target,
            lambda shard: target.at[shard, :, self.columns(rep)],
        )
        self.across = {}
        self.core = []

    def columns(self, rep):
        return pl.ds(pl.multiple_of(rep * self.width, self.width), self.width)

    def start(self):
        super().start()
        self.own = self.local_all.copy(self.whole, self.target.at[self.copies.place])

    def arrive(self, offset):
        super().arrive(offset)
        block = self.at(flipped(self.copies.place, offset))
        self.across[offset] = self.copies.send(block, block, 2, 0)
        self.core.append(self.copies.send(block, block, 1, 0))

    def cross(self, offset):
        copies = self.copies
        self.across[offset].wait_recv()
        shard = flipped(copies.place, offset)
        block = self.target.at[shard, :, self.columns(flipped(copies.rep, 2))]
        self.core.append(copies.send(block, block, 1, 0))

    def finish(self):
        for copy in self.core:
            copy.wait_recv()
        self.own.wait()


def row_loop(rows, step, body):
    @pl.loop(0, rows // step)
    def _(at):
        body(pl.ds(pl.multiple_of(at * step, step), step))


def normed(values, gain):
    return values * rms_scale(values) * gain


def shifted(values, by):
    rows = values.shape[0]
    at = lax.broadcasted_iota(jnp.int32, values.shape, 0)
    turned = pltpu.roll(values, by % rows, 0)
    kept = at >= by if by > 0 else at < rows + by
    return jnp.where(kept, turned, 0.0)


def mixer_columns(act, m_in, gains, at, width, features, slot):
    lanes = pl.ds(at, width)
    parts = []
    for base in (0, features, 2 * features):
        block = m_in[:, :, base + at : base + at + width].reshape(features, width)
        parts.append(dot(act, block))
    part_b, part_c, part_x = parts
    taps = [gains[2 + k : 3 + k, at : at + width] for k in range(3)]
    product = part_b * part_x
    convolved = []
    for start in range(0, act.shape[0], slot):
        rows = product[start : start + slot]
        convolved.append(
            taps[0] * shifted(rows, 2) + taps[1] * shifted(rows, 1) + taps[2] * rows
        )
    return part_b, part_c, part_x, product, jnp.concatenate(convolved)


def forward_kernel(
    slot,
    rows_ref, cot_ref, small_ref, in_ref, out_ref, gate_ref, up_ref, down_ref,
    all_in, all_out, all_gate, all_up, all_down, all_act, all_cot, gains_ref,
    small_all, v_in, v_out, act_one, mixer_in, act_two,
    send_sems, recv_sems, local_sems,
):
    rows, features = rows_ref.shape
    shards = all_gate.shape[0]
    copies = Copies(send_sems, recv_sems)
    local = Local(local_sems)
    far = list(range(2, shards, 2))
    copies.meet([(0, offset) for offset in [*far, 1]] + [(1, 0), (2, 0)])

    small = Spread(copies, local, shards, small_ref, small_all)
    w_in = SpreadAll(copies, local, shards, in_ref, v_in, in_ref.shape[1] // 4)
    w_out = SpreadAll(copies, local, shards, out_ref, v_out, out_ref.shape[1] // 4)
    gate = Spread(copies, local, shards, gate_ref, all_gate)
    up = Spread(copies, local, shards, up_ref, all_up)
    down = Spread(copies, local, shards, down_ref, all_down)

    small.start()
    w_in.start()
    w_out.start()
    own_cot = local.copy(cot_ref, all_cot.at[0])
    for offset in far:
        small.arrive(offset)
    small.finish()
    gains_ref[...] = jnp.sum(small_all[...], axis=0)
    gain_one = gains_ref[0:1]

    def first(at):
        act_one[at] = normed(rows_ref[at].astype(F32), gain_one).astype(LOW)

    w_in.arrive(far[0])
    w_in.arrive(1)
    row_loop(rows, 64, first)
    gate.start()
    for offset in far[1:]:
        w_in.arrive(offset)
    for offset in far:
        w_in.arrive(offset + 1)
    w_out.arrive(1)
    for offset in far:
        w_out.arrive(offset)
    for offset in far:
        w_out.arrive(offset + 1)
    up.start()
    cot_core = copies.send(cot_ref, all_cot.at[1], 1, 0)
    cot_across = copies.send(cot_ref, all_cot.at[2], 2, 0)
    order = [1, *far, *[offset + 1 for offset in far]]
    for offset in order:
        w_in.cross(offset)
    for offset in far:
        gate.arrive(offset)
    for offset in order:
        w_out.cross(offset)
    down.start()
    w_in.finish()

    width = features // 4
    for part in range(4):
        at = part * width
        _, part_c, _, _, convolved = mixer_columns(
            act_one[...], v_in, gains_ref, at, width, features, slot
        )
        mixer_in[:, at : at + width] = (part_c * convolved).astype(LOW)
        if part == 1:
            for offset in far:
                up.arrive(offset)
    keep_in = local.copy(v_in, all_in)
    w_out.finish()
    keep_out = local.copy(v_out, all_out)
    spread = []
    for start in range(0, rows, slot):
        held = slice(start, start + slot)
        hstate = rows_ref[held].astype(F32) + dot(
            mixer_in[held], v_out[...].reshape(features, features)
        )
        act_two[held] = normed(hstate, gains_ref[1:2]).astype(LOW)
        block = act_two.at[held]
        spread.append(
            (
                held,
                copies.send(block, all_act.at[2, held], 2, 0),
                copies.send(block, all_act.at[1, held], 1, 0),
                local.copy(block, all_act.at[0, held]),
            )
        )
    for offset in far:
        down.arrive(offset)
    cot_across.wait_recv()
    corner = [copies.send(all_cot.at[2], all_cot.at[3], 1, 0)]
    for held, across, _, _ in spread:
        across.wait_recv()
        corner.append(copies.send(all_act.at[2, held], all_act.at[3, held], 1, 0))
    gate.finish()
    up.finish()
    down.finish()
    cot_core.wait_recv()
    for _, _, core, own in spread:
        core.wait_recv()
        own.wait()
    for copy in corner:
        copy.wait_recv()
    own_cot.wait()
    keep_in.wait()
    keep_out.wait()
    copies.close()


def run_forward(rows, cot, small, w_in, w_out, gate, up, down, slot):
    shards = lax.axis_size("fsdp")
    count, features = rows.shape
    part = w_in.shape[0]
    shapes = [
        ((shards, *w_in.shape), LOW),
        ((shards, *w_out.shape), LOW),
        ((shards, *gate.shape), LOW),
        ((shards, *up.shape), LOW),
        ((shards, *down.shape), LOW),
        ((4, count, features), LOW),
        ((4, count, features), LOW),
    ]
    hbm = pl.BlockSpec(memory_space=pltpu.HBM)
    vmem = pl.BlockSpec(memory_space=pltpu.VMEM)
    hops = 12 * shards + 16
    return pl.pallas_call(
        functools.partial(forward_kernel, slot),
        out_shape=[jax.ShapeDtypeStruct(*shape) for shape in shapes]
        + [jax.ShapeDtypeStruct((8, features), F32)],
        in_specs=[vmem, hbm, vmem, hbm, hbm, hbm, hbm, hbm],
        out_specs=[hbm] * 7 + [vmem],
        scratch_shapes=[
            pltpu.VMEM((shards, 8, features), F32),
            pltpu.VMEM((shards, *w_in.shape), LOW),
            pltpu.VMEM((shards, *w_out.shape), LOW),
            pltpu.VMEM((count, features), LOW),
            pltpu.VMEM((count, features), LOW),
            pltpu.VMEM((count, features), LOW),
            pltpu.SemaphoreType.DMA((hops,)),
            pltpu.SemaphoreType.DMA((hops,)),
            pltpu.SemaphoreType.DMA((16,)),
        ],
        compiler_params=pltpu.CompilerParams(
            collective_id=0, has_side_effects=True, vmem_limit_bytes=56 << 20
        ),
        name="forward",
    )(rows, cot, small, w_in, w_out, gate, up, down)


def on_device(
    inputs, cotangent, lengths, norm_one, w_in, conv_w, w_out, norm_two, w_gate, w_up, w_down
):
    micro_count, tok_rows, features = inputs.shape
    shards = lax.axis_size("fsdp")
    place = lax.axis_index("fsdp")
    rep = lax.axis_index("rep")
    all_rows = micro_count * tok_rows
    hidden_own = w_down.shape[0]
    cut = hidden_own // 4
    part_ff = shards * cut

    slot_cols = jnp.arange(lengths.shape[1], dtype=jnp.int32)
    slot_id = rep * shards + place
    length_now = jnp.sum(jnp.where(slot_cols == slot_id, lengths, 0), axis=1)
    position = jnp.arange(tok_rows, dtype=jnp.int32)
    live = (position[None] < length_now[:, None]).astype(F32)[..., None]
    cotan_f = (cotangent.astype(F32) * live).reshape(all_rows, features)
    cotan_low = cotan_f.astype(LOW)

    small = jnp.concatenate([norm_one[None], norm_two[None], conv_w, jnp.zeros_like(conv_w)])
    small = lax.dynamic_update_slice(
        jnp.zeros((8, features), F32), small.astype(F32), (0, place * small.shape[1])
    )
    gate_own = lax.dynamic_index_in_dim(
        w_gate.reshape(-1, shards, 4, cut), rep, 2, keepdims=False
    ).reshape(-1, part_ff)
    up_own = lax.dynamic_index_in_dim(
        w_up.reshape(-1, shards, 4, cut), rep, 2, keepdims=False
    ).reshape(-1, part_ff)
    down_own = lax.dynamic_slice_in_dim(w_down, rep * cut, cut, 0)
    rows_low = inputs.reshape(all_rows, features)
    m_in, m_out, m_gate, m_up, m_down, act_all, cot_all, gains = run_forward(
        rows_low, cotan_low, small, w_in, w_out, gate_own, up_own, down_own, tok_rows
    )
    m_in = m_in.reshape(features, -1)
    m_out = m_out.reshape(features, -1)
    m_gate = m_gate.reshape(features, part_ff)
    m_up = m_up.reshape(features, part_ff)
    m_down = m_down.reshape(part_ff, features)
    g_one, g_two, taps = gains[0], gains[1], gains[2:5]
    act_near, act_far = act_all[:2].reshape(-1, features), act_all[2:].reshape(-1, features)
    cot_near, cot_far = cot_all[:2].reshape(-1, features), cot_all[2:].reshape(-1, features)

    rows_f = inputs.reshape(all_rows, features).astype(F32)
    scale_one = rms_scale(rows_f)
    act_one = (rows_f * scale_one * g_one).astype(LOW)
    projected = dot(act_one, m_in)
    part_b = projected[:, :features]
    part_c = projected[:, features : 2 * features]
    part_x = projected[:, 2 * features :]
    product = (part_b * part_x).reshape(micro_count, tok_rows, features)
    padded = jnp.pad(product, ((0, 0), (2, 0), (0, 0)))
    convolved = (
        taps[0] * padded[:, :-2] + taps[1] * padded[:, 1:-1] + taps[2] * padded[:, 2:]
    ).reshape(all_rows, features)
    mixer_in = (part_c * convolved).astype(LOW)
    hstate = rows_f + dot(mixer_in, m_out)
    scale_two = rms_scale(hstate)
    act_two = (hstate * scale_two * g_two).astype(LOW)

    def units(act, cot):
        gate_pre = dot(act, m_gate)
        up_pre = dot(act, m_up)
        sigmoid_g = jax.nn.sigmoid(gate_pre)
        silu_g = gate_pre * sigmoid_g
        hidden = (silu_g * up_pre).astype(LOW)
        d_hidden = dot_last(cot, m_down)
        d_gate = (d_hidden * up_pre * sigmoid_g * (1.0 + gate_pre * (1.0 - sigmoid_g))).astype(LOW)
        d_up = (d_hidden * silu_g).astype(LOW)
        return hidden, d_gate, d_up

    hidden_n, d_gate_n, d_up_n = units(act_near, cot_near)
    hidden_f, d_gate_f, d_up_f = units(act_far, cot_far)
    grad_down = dot_first(hidden_n, cot_near) + dot_first(hidden_f, cot_far)
    d_act_two = sum_over_rep(
        dot_last(d_gate_n, m_gate) + dot_last(d_up_n, m_up),
        dot_last(d_gate_f, m_gate) + dot_last(d_up_f, m_up),
    )
    grad_gate = dot_first(act_near, d_gate_n) + dot_first(act_far, d_gate_f)
    grad_up = dot_first(act_near, d_up_n) + dot_first(act_far, d_up_f)
    ffn = sum_over_rep(dot(hidden_n, m_down), dot(hidden_f, m_down))
    outputs = (hstate + ffn).reshape(inputs.shape)

    sum_down = reduce_pieces(grad_down.reshape(shards, cut, features))
    sum_gate = reduce_pieces(grad_gate.reshape(shards, -1, part_ff))
    sum_up = reduce_pieces(grad_up.reshape(shards, -1, part_ff))
    all_down = share_quarters(sum_down.astype(LOW)).reshape(hidden_own, features).astype(F32)

    def unit_columns(total):
        quarters = share_quarters(total.astype(LOW)).reshape(4, -1, shards, cut)
        return quarters.transpose(1, 2, 0, 3).reshape(-1, 4 * part_ff).astype(F32)

    all_gate = unit_columns(sum_gate)
    all_up = unit_columns(sum_up)

    grad_two = jnp.sum(d_act_two * hstate * scale_two, axis=0)
    d_hstate = cotan_f + norm_back(d_act_two, hstate, scale_two, g_two)
    d_mixer = d_hstate.astype(LOW)
    grad_out = dot_first(mixer_in, d_mixer)
    d_mixin = dot_last(d_mixer, m_out)
    d_cpart = d_mixin * convolved
    d_conv = (d_mixin * part_c).reshape(micro_count, tok_rows, features)
    trailing = jnp.pad(d_conv, ((0, 0), (0, 2), (0, 0)))
    d_product = (
        taps[2] * d_conv + taps[1] * trailing[:, 1:-1] + taps[0] * trailing[:, 2:]
    ).reshape(all_rows, features)
    grad_conv = [
        jnp.sum(d_conv * padded[:, k : k + tok_rows], axis=(0, 1)) for k in range(3)
    ]
    d_projected = jnp.concatenate(
        [d_product * part_x, d_cpart, d_product * part_b], axis=1
    ).astype(LOW)
    grad_in = dot_first(act_one, d_projected)
    d_act_one = dot_last(d_projected, m_in)
    grad_one = jnp.sum(d_act_one * rows_f * scale_one, axis=0)
    d_rows = d_hstate + norm_back(d_act_one, rows_f, scale_one, g_one)
    d_inputs = d_rows.reshape(inputs.shape)

    all_out = reduce_full(grad_out)
    all_in = reduce_full(grad_in)

    zeros = jnp.zeros_like(grad_one)
    small_grads = jnp.stack([grad_one, grad_two, *grad_conv, zeros, zeros, zeros])
    small_grads = jnp.moveaxis(small_grads.reshape(8, shards, -1), 1, 0)
    small_own = reduce_pieces(small_grads, F32)
    small_own = small_own + hop(small_own, "rep", 1)
    small_own = small_own + hop(small_own, "rep", 2)

    return (
        outputs,
        d_inputs,
        small_own[0],
        all_in,
        small_own[2:5],
        all_out,
        small_own[1],
        all_gate,
        all_up,
        all_down,
    )


def solution(mesh):
    return jax.shard_map(
        on_device,
        mesh=mesh,
        in_specs=(
            P(None, ("rep", "fsdp"), None),
            P(None, ("rep", "fsdp"), None),
            P(),
            P("fsdp"),
            P("fsdp", None),
            P(None, "fsdp"),
            P("fsdp", None),
            P("fsdp"),
            P("fsdp", None),
            P("fsdp", None),
            P("fsdp", None),
        ),
        out_specs=(
            P(None, ("rep", "fsdp"), None),
            P(None, ("rep", "fsdp"), None),
            P("fsdp"),
            P("fsdp", None),
            P(None, "fsdp"),
            P("fsdp", None),
            P("fsdp"),
            P("fsdp", None),
            P("fsdp", None),
            P("fsdp", None),
        ),
        check_vma=False,
    )
```

```python
import functools

import jax
import jax.numpy as jnp
from jax import lax
from jax.experimental import pallas as pl
from jax.experimental.pallas import tpu as pltpu
from jax.sharding import PartitionSpec as P

EPSILON = 1e-05
LOW = jnp.bfloat16
F32 = jnp.float32
MESH = pl.DeviceIdType.MESH


def rms_scale(values):
    return lax.rsqrt(jnp.mean(values * values, axis=-1, keepdims=True) + EPSILON)


def dot(left, right):
    return jnp.dot(left, right, preferred_element_type=F32)


def dot_last(left, right):
    return lax.dot_general(left, right, (((1,), (1,)), ((), ())), preferred_element_type=F32)


def dot_first(left, right):
    return lax.dot_general(left, right, (((0,), (0,)), ((), ())), preferred_element_type=F32)


def norm_back(d_act, values, scale, gain):
    scaled = d_act * gain
    return scale * (
        scaled - values * scale * scale * jnp.mean(scaled * values, axis=-1, keepdims=True)
    )


def flipped(index, offset):
    bit = 1
    while bit <= offset:
        if offset & bit:
            index = index + bit - 2 * bit * ((index // bit) % 2)
        bit *= 2
    return index


class Copies:
    def __init__(self, send_sems, recv_sems):
        self.sems = send_sems, recv_sems
        self.rep = lax.axis_index("rep")
        self.place = lax.axis_index("fsdp")
        self.started = []

    def peer(self, rep_bits, place_bits):
        return (flipped(self.rep, rep_bits), flipped(self.place, place_bits))

    def meet(self, peers):
        barrier = pltpu.get_barrier_semaphore()
        for bits in peers:
            pl.semaphore_signal(barrier, inc=1, device_id=self.peer(*bits), device_id_type=MESH)
        pl.semaphore_wait(barrier, len(peers))

    def send(self, source, target, rep_bits, place_bits):
        at = len(self.started)
        copy = pltpu.make_async_remote_copy(
            src_ref=source,
            dst_ref=target,
            send_sem=self.sems[0].at[at],
            recv_sem=self.sems[1].at[at],
            device_id=self.peer(rep_bits, place_bits),
            device_id_type=MESH,
        )
        copy.start()
        self.started.append(copy)
        return copy

    def close(self):
        for copy in self.started:
            copy.wait_send()


class Local:
    def __init__(self, sems):
        self.sems = sems
        self.started = []

    def copy(self, source, target):
        copy = pltpu.make_async_copy(source, target, self.sems.at[len(self.started)])
        copy.start()
        self.started.append(copy)
        return copy


class Spread:
    def __init__(self, copies, locals_, shards, source, target, at=None):
        self.copies = copies
        self.target = target
        self.at = at if at is not None else (lambda shard: target.at[shard])
        self.source = source
        self.locals = locals_
        self.far = list(range(2, shards, 2))
        self.near = [1] + [offset + 1 for offset in self.far]

    def start(self):
        copies = self.copies
        here = self.at(copies.place)
        self.arriving = {offset: copies.send(self.source, here, 0, offset) for offset in self.far}
        self.arriving[1] = copies.send(self.source, here, 0, 1)
        if self.locals is not None:
            self.own = self.locals.copy(self.source, here)

    def arrive(self, offset):
        self.arriving[offset].wait_recv()
        if offset % 2 == 0:
            block = self.at(flipped(self.copies.place, offset))
            self.arriving[offset + 1] = self.copies.send(block, block, 0, 1)

    def finish(self):
        for offset in self.near:
            self.arriving[offset].wait_recv()
        if self.locals is not None:
            self.own.wait()


class SpreadAll(Spread):
    def __init__(self, copies, locals_, shards, source, target, width):
        self.width = width
        self.whole = source
        self.local_all = locals_
        rep = copies.rep
        super().__init__(
            copies,
            None,
            shards,
            source.at[:, self.columns(rep)],
            target,
            lambda shard: target.at[shard, :, self.columns(rep)],
        )
        self.across = {}
        self.core = []

    def columns(self, rep):
        return pl.ds(pl.multiple_of(rep * self.width, self.width), self.width)

    def start(self):
        super().start()
        self.own = self.local_all.copy(self.whole, self.target.at[self.copies.place])

    def arrive(self, offset):
        super().arrive(offset)
        block = self.at(flipped(self.copies.place, offset))
        self.across[offset] = self.copies.send(block, block, 2, 0)
        self.core.append(self.copies.send(block, block, 1, 0))

    def cross(self, offset):
        copies = self.copies
        self.across[offset].wait_recv()
        shard = flipped(copies.place, offset)
        block = self.target.at[shard, :, self.columns(flipped(copies.rep, 2))]
        self.core.append(copies.send(block, block, 1, 0))

    def finish(self):
        for copy in self.core:
            copy.wait_recv()
        self.own.wait()


def row_loop(rows, step, body):
    @pl.loop(0, rows // step)
    def _(at):
        body(pl.ds(pl.multiple_of(at * step, step), step))


def normed(values, gain):
    return values * rms_scale(values) * gain


def shifted(values, by):
    rows = values.shape[0]
    at = lax.broadcasted_iota(jnp.int32, values.shape, 0)
    turned = pltpu.roll(values, by % rows, 0)
    kept = at >= by if by > 0 else at < rows + by
    return jnp.where(kept, turned, 0.0)


def mixer_columns(act, m_in, gains, at, width, features, slot):
    lanes = pl.ds(at, width)
    parts = []
    for base in (0, features, 2 * features):
        block = m_in[:, :, base + at : base + at + width].reshape(features, width)
        parts.append(dot(act, block))
    part_b, part_c, part_x = parts
    taps = [gains[2 + k : 3 + k, at : at + width] for k in range(3)]
    product = part_b * part_x
    convolved = []
    for start in range(0, act.shape[0], slot):
        rows = product[start : start + slot]
        convolved.append(
            taps[0] * shifted(rows, 2) + taps[1] * shifted(rows, 1) + taps[2] * rows
        )
    return part_b, part_c, part_x, product, jnp.concatenate(convolved)


def forward_kernel(
    slot,
    rows_ref, cot_ref, small_ref, in_ref, out_ref, gate_ref, up_ref, down_ref,
    all_in, all_out, all_gate, all_up, all_down, all_act, all_cot, gains_ref,
    small_all, v_in, v_out, act_one, mixer_in, act_two,
    send_sems, recv_sems, local_sems,
):
    rows, features = rows_ref.shape
    shards = all_gate.shape[0]
    copies = Copies(send_sems, recv_sems)
    local = Local(local_sems)
    far = list(range(2, shards, 2))
    copies.meet([(0, offset) for offset in [*far, 1]] + [(1, 0), (2, 0)])

    small = Spread(copies, local, shards, small_ref, small_all)
    w_in = SpreadAll(copies, local, shards, in_ref, v_in, in_ref.shape[1] // 4)
    w_out = SpreadAll(copies, local, shards, out_ref, v_out, out_ref.shape[1] // 4)
    gate = Spread(copies, local, shards, gate_ref, all_gate)
    up = Spread(copies, local, shards, up_ref, all_up)
    down = Spread(copies, local, shards, down_ref, all_down)

    small.start()
    w_in.start()
    w_out.start()
    own_cot = local.copy(cot_ref, all_cot.at[0])
    for offset in far:
        small.arrive(offset)
    small.finish()
    gains_ref[...] = jnp.sum(small_all[...], axis=0)
    gain_one = gains_ref[0:1]

    def first(at):
        act_one[at] = normed(rows_ref[at].astype(F32), gain_one).astype(LOW)

    w_in.arrive(far[0])
    w_in.arrive(1)
    row_loop(rows, 64, first)
    gate.start()
    for offset in far[1:]:
        w_in.arrive(offset)
    for offset in far:
        w_in.arrive(offset + 1)
    w_out.arrive(1)
    for offset in far:
        w_out.arrive(offset)
    for offset in far:
        w_out.arrive(offset + 1)
    up.start()
    cot_core = copies.send(cot_ref, all_cot.at[1], 1, 0)
    cot_across = copies.send(cot_ref, all_cot.at[2], 2, 0)
    order = [1, *far, *[offset + 1 for offset in far]]
    for offset in order:
        w_in.cross(offset)
    for offset in far:
        gate.arrive(offset)
    for offset in order:
        w_out.cross(offset)
    down.start()
    w_in.finish()

    width = features // 4
    for part in range(4):
        at = part * width
        _, part_c, _, _, convolved = mixer_columns(
            act_one[...], v_in, gains_ref, at, width, features, slot
        )
        mixer_in[:, at : at + width] = (part_c * convolved).astype(LOW)
        if part == 1:
            for offset in far:
                up.arrive(offset)
    keep_in = local.copy(v_in, all_in)
    w_out.finish()
    keep_out = local.copy(v_out, all_out)
    spread = []
    for start in range(0, rows, slot):
        held = slice(start, start + slot)
        hstate = rows_ref[held].astype(F32) + dot(
            mixer_in[held], v_out[...].reshape(features, features)
        )
        act_two[held] = normed(hstate, gains_ref[1:2]).astype(LOW)
        block = act_two.at[held]
        spread.append(
            (
                held,
                copies.send(block, all_act.at[2, held], 2, 0),
                copies.send(block, all_act.at[1, held], 1, 0),
                local.copy(block, all_act.at[0, held]),
            )
        )
    for offset in far:
        down.arrive(offset)
    cot_across.wait_recv()
    corner = [copies.send(all_cot.at[2], all_cot.at[3], 1, 0)]
    for held, across, _, _ in spread:
        across.wait_recv()
        corner.append(copies.send(all_act.at[2, held], all_act.at[3, held], 1, 0))
    gate.finish()
    up.finish()
    down.finish()
    cot_core.wait_recv()
    for _, _, core, own in spread:
        core.wait_recv()
        own.wait()
    for copy in corner:
        copy.wait_recv()
    own_cot.wait()
    keep_in.wait()
    keep_out.wait()
    copies.close()


def run_forward(rows, cot, small, w_in, w_out, gate, up, down, slot):
    shards = lax.axis_size("fsdp")
    count, features = rows.shape
    part = w_in.shape[0]
    shapes = [
        ((shards, *w_in.shape), LOW),
        ((shards, *w_out.shape), LOW),
        ((shards, *gate.shape), LOW),
        ((shards, *up.shape), LOW),
        ((shards, *down.shape), LOW),
        ((4, count, features), LOW),
        ((4, count, features), LOW),
    ]
    hbm = pl.BlockSpec(memory_space=pltpu.HBM)
    vmem = pl.BlockSpec(memory_space=pltpu.VMEM)
    hops = 12 * shards + 16
    return pl.pallas_call(
        functools.partial(forward_kernel, slot),
        out_shape=[jax.ShapeDtypeStruct(*shape) for shape in shapes]
        + [jax.ShapeDtypeStruct((8, features), F32)],
        in_specs=[vmem, hbm, vmem, hbm, hbm, hbm, hbm, hbm],
        out_specs=[hbm] * 7 + [vmem],
        scratch_shapes=[
            pltpu.VMEM((shards, 8, features), F32),
            pltpu.VMEM((shards, *w_in.shape), LOW),
            pltpu.VMEM((shards, *w_out.shape), LOW),
            pltpu.VMEM((count, features), LOW),
            pltpu.VMEM((count, features), LOW),
            pltpu.VMEM((count, features), LOW),
            pltpu.SemaphoreType.DMA((hops,)),
            pltpu.SemaphoreType.DMA((hops,)),
            pltpu.SemaphoreType.DMA((16,)),
        ],
        compiler_params=pltpu.CompilerParams(
            collective_id=0, has_side_effects=True, vmem_limit_bytes=56 << 20
        ),
        name="forward",
    )(rows, cot, small, w_in, w_out, gate, up, down)


def add_into(target, *others):
    rows = target.shape[-2]
    step = 16 if rows % 16 == 0 else rows
    lead = target.shape[:-2]

    @pl.loop(0, rows // step)
    def _(at):
        held = pl.ds(pl.multiple_of(at * step, step), step)
        index = (slice(None),) * len(lead) + (held,)
        total = target[index].astype(F32)
        for other in others:
            total = total + other[index].astype(F32)
        target[index] = total.astype(target.dtype)


class Collect:
    def __init__(self, copies, shards, sent_at, own_at, near_in, far_in):
        self.copies = copies
        self.sent_at, self.own_at = sent_at, own_at
        self.near_in, self.far_in = near_in, far_in
        self.order = [*range(2, shards, 2), 0]
        self.arriving = {}
        self.far = {}

    def near(self, offset):
        copies = self.copies
        self.arriving[offset] = copies.send(
            self.sent_at(offset + 1), self.near_in.at[offset // 2], 0, 1
        )

    def near_all(self):
        for offset in self.order:
            self.near(offset)

    def combine(self, offset):
        self.arriving[offset].wait_recv()
        own = self.own_at(offset)
        add_into(own, self.near_in.at[offset // 2])
        if offset:
            self.far[offset] = self.copies.send(
                own, self.far_in.at[offset // 2 - 1], 0, offset
            )

    def combine_all(self):
        for offset in self.order:
            self.combine(offset)

    def total(self):
        for copy in self.far.values():
            copy.wait_recv()
        own = self.own_at(0)
        add_into(own, *[self.far_in.at[k] for k in range(len(self.far))])
        return own


class Share:
    def __init__(self, copies, local, source, target_at):
        self.copies = copies
        self.target_at = target_at
        here = target_at(copies.rep)
        self.across = copies.send(source, here, 2, 0)
        self.core = [copies.send(source, here, 1, 0)]
        self.own = local.copy(source, here)

    def forward(self):
        self.across.wait_recv()
        block = self.target_at(flipped(self.copies.rep, 2))
        self.core.append(self.copies.send(block, block, 1, 0))

    def finish(self):
        for copy in self.core:
            copy.wait_recv()
        self.own.wait()


class CollectAll:
    def __init__(self, copies, shards, width, parts, core_in, cross_in, near_in, far_in):
        self.copies = copies
        self.width = width
        self.parts, self.core_in, self.cross_in = parts, core_in, cross_in
        place = copies.place
        self.collect = Collect(
            copies,
            shards,
            lambda offset: parts.at[0, flipped(place, offset)],
            lambda offset: parts.at[0, flipped(place, offset)],
            near_in,
            far_in,
        )
        self.core = {}
        self.cross = {}
        self.order = [o + 1 for o in self.collect.order] + self.collect.order

    def compute(self, turn, left, right):
        rep = flipped(self.copies.rep, turn)
        shards, rows, _ = self.parts.shape[1:]
        for at in range(0, self.width, 256):
            columns = pl.ds(pl.multiple_of(rep * self.width + at, 256), 256)
            block = dot_first(left[...], right[:, columns]).astype(LOW)
            self.parts[turn, :, :, at : at + 256] = block.reshape(shards, rows, 256)

    def to_core(self, turn):
        self.core[turn - 1] = self.copies.send(
            self.parts.at[turn], self.core_in.at[turn // 2], 1, 0
        )

    def to_cross(self):
        self.core[2].wait_recv()
        place = self.copies.place
        for offset in self.order:
            block = self.parts.at[2, flipped(place, offset)]
            add_into(block, self.core_in.at[1, flipped(place, offset)])
            self.cross[offset] = self.copies.send(
                block, self.cross_in.at[flipped(place, offset)], 2, 0
            )
        self.core[0].wait_recv()

    def arrive(self, offset):
        self.cross[offset].wait_recv()
        shard = flipped(self.copies.place, offset)
        add_into(self.parts.at[0, shard], self.core_in.at[0, shard], self.cross_in.at[shard])

    def near_all(self):
        for offset in self.collect.order:
            self.arrive(offset + 1)
            self.collect.near(offset)

    def combine_all(self):
        for offset in self.collect.order:
            self.arrive(offset)
            self.collect.combine(offset)


def backward_kernel(
    slot,
    rows_ref, cot_ref, gains_ref, in_ref, out_ref, d_act_ref, ffn_ref, down_ref, gate_ref, up_ref,
    outputs_ref, d_rows_ref, down_sum, gate_sum, up_sum, in_sum, out_sum, small_sum, ffn_in,
    v_in, v_out, act_one, part_b, part_c, part_x, mixer_in, hstate, d_act, d_core, d_cross,
    ffn_part, d_hstate, d_mixer, d_proj,
    down_own, down_near, down_far, gate_own, gate_near, gate_far, up_own, up_near, up_far,
    w_out_parts, w_out_core, w_out_cross, w_out_near, w_out_far,
    w_in_parts, w_in_core, w_in_cross, w_in_near, w_in_far,
    small, small_in, send_sems, recv_sems, local_sems,
):
    rows, features = rows_ref.shape
    shards = gate_ref.shape[0]
    copies = Copies(send_sems, recv_sems)
    local = Local(local_sems)
    place, rep = copies.place, copies.rep
    far = list(range(2, shards, 2))
    bits = [1 << k for k in range(1, shards.bit_length() - 1)]
    copies.meet([(0, offset) for offset in [*far, 1]] + [(1, 0), (2, 0)])

    d_near = [copies.send(d_act_ref.at[turn], d_core.at[turn // 2], 1, 0) for turn in (3, 1)]
    d_own = [local.copy(d_act_ref.at[turn], d_act.at[turn // 2]) for turn in (2, 0)]
    load_in = local.copy(in_ref, v_in)
    load_out = local.copy(out_ref, v_out)

    def collector(source, own, near, far_in):
        loads = [
            local.copy(source.at[flipped(place, offset)], own.at[offset // 2])
            for offset in range(0, shards, 2)
        ]
        return loads, Collect(
            copies,
            shards,
            lambda offset: source.at[flipped(place, offset)],
            lambda offset: own.at[offset // 2],
            near,
            far_in,
        )

    down_loads, down = collector(down_ref, down_own, down_near, down_far)
    gate_loads, gate = collector(gate_ref, gate_own, gate_near, gate_far)
    up_loads, up = collector(up_ref, up_own, up_near, up_far)
    down.near_all()
    gate.near_all()

    gain_one, gain_two = gains_ref[0:1], gains_ref[1:2]

    def first(at):
        act_one[at] = normed(rows_ref[at].astype(F32), gain_one).astype(LOW)

    d_own[0].wait()
    d_near[0].wait_recv()
    d_far = []
    for start in range(0, rows, slot):
        held = slice(start, start + slot)
        add_into(d_act.at[1, held], d_core.at[1, held])
        d_far.append(copies.send(d_act.at[1, held], d_cross.at[held], 2, 0))
    ffn_near = [copies.send(ffn_ref.at[turn], ffn_in.at[turn // 2], 1, 0) for turn in (3, 1)]
    ffn_own = local.copy(ffn_ref.at[2], ffn_part)
    row_loop(rows, 64, first)

    load_in.wait()
    width = features // 4
    for part in range(4):
        at = part * width
        lanes = slice(at, at + width)
        b_now, c_now, x_now, _, convolved = mixer_columns(
            act_one[...], v_in, gains_ref, at, width, features, slot
        )
        part_b[:, lanes] = b_now
        part_c[:, lanes] = c_now
        part_x[:, lanes] = x_now
        mixer_in[:, lanes] = (c_now * convolved).astype(LOW)
        if part == 1:
            for copy in down_loads:
                copy.wait()
            down.combine_all()
            up.near_all()
    load_out.wait()
    for start in range(0, rows, slot):
        held = slice(start, start + slot)
        hstate[held] = rows_ref[held].astype(F32) + dot(
            mixer_in[held], v_out[...].reshape(features, features)
        )

    ffn_own.wait()
    ffn_near[0].wait_recv()
    load = local.copy(ffn_in.at[1], d_mixer)
    load.wait()
    add_into(ffn_part, d_mixer)
    load_cot = local.copy(cot_ref, d_mixer)
    ffn_across = copies.send(ffn_part, ffn_in.at[2], 2, 0)
    for copy in gate_loads:
        copy.wait()
    gate.combine_all()

    d_own[1].wait()
    d_near[1].wait_recv()
    small[0] = jnp.zeros((8, features), F32)

    def second(at):
        d_now = (
            d_act[0, at].astype(F32) + d_core[0, at].astype(F32) + d_cross[at].astype(F32)
        )
        values = hstate[at]
        scale = rms_scale(values)
        small[0, 1:2] += jnp.sum(d_now * values * scale, axis=0, keepdims=True)
        d_values = d_mixer[at].astype(F32) + norm_back(d_now, values, scale, gain_two)
        d_hstate[at] = d_values
        d_mixer[at] = d_values.astype(LOW)

    for copy in d_far:
        copy.wait_recv()
    load_cot.wait()
    row_loop(rows, 64, second)

    w_out = CollectAll(
        copies, shards, features // 4, w_out_parts, w_out_core, w_out_cross, w_out_near, w_out_far
    )
    w_in = CollectAll(
        copies, shards, 3 * features // 4, w_in_parts, w_in_core, w_in_cross, w_in_near, w_in_far
    )
    for turn in (3, 1):
        w_out.compute(turn, mixer_in, d_mixer)
        w_out.to_core(turn)
    for turn in (2, 0):
        w_out.compute(turn, mixer_in, d_mixer)

    per = shards * width // features
    for part in range(4):
        at = part * width
        lanes = slice(at, at + width)
        block = v_out[part * per : (part + 1) * per].reshape(width, features)
        d_mixin = dot_last(d_mixer[...], block)
        taps = [gains_ref[2 + k : 3 + k, lanes] for k in range(3)]
        for start in range(0, rows, slot):
            held = slice(start, start + slot)
            d_mix = d_mixin[held]
            b_now, c_now, x_now = part_b[held, lanes], part_c[held, lanes], part_x[held, lanes]
            product = b_now * x_now
            before = [shifted(product, 2), shifted(product, 1), product]
            convolved = taps[0] * before[0] + taps[1] * before[1] + taps[2] * before[2]
            d_conv = d_mix * c_now
            for k in range(3):
                small[0, 2 + k : 3 + k, lanes] += jnp.sum(
                    d_conv * before[k], axis=0, keepdims=True
                )
            d_product = (
                taps[2] * d_conv + taps[1] * shifted(d_conv, -1) + taps[0] * shifted(d_conv, -2)
            )
            d_proj[held, lanes] = (d_product * x_now).astype(LOW)
            d_proj[held, features + at : features + at + width] = (d_mix * convolved).astype(LOW)
            d_proj[held, 2 * features + at : 2 * features + at + width] = (
                d_product * b_now
            ).astype(LOW)
        if part == 0:
            w_out.to_cross()
        if part == 1:
            for copy in up_loads:
                copy.wait()
            up.combine_all()

    for turn in (3, 1):
        w_in.compute(turn, act_one, d_proj)
        w_in.to_core(turn)
    for turn in (2, 0):
        w_in.compute(turn, act_one, d_proj)
    w_in.to_cross()
    down_share = Share(copies, local, down.total(), lambda at: down_sum.at[at])
    w_out.near_all()

    for start in range(0, rows, slot):
        held = slice(start, start + slot)
        d_now = dot_last(d_proj[held], v_in[...].reshape(features, 3 * features))
        values = rows_ref[held].astype(F32)
        scale = rms_scale(values)
        small[0, 0:1] += jnp.sum(d_now * values * scale, axis=0, keepdims=True)
        d_hstate[held] += norm_back(d_now, values, scale, gain_one)
    d_out = local.copy(d_hstate, d_rows_ref)
    gate_share = Share(copies, local, gate.total(), lambda at: gate_sum.at[at])
    w_out.combine_all()

    hops = [(0, 1), *[(0, bit) for bit in bits], (1, 0), (2, 0)]
    for step, (rep_bits, place_bits) in enumerate(hops):
        copies.send(small.at[step], small_in.at[step], rep_bits, place_bits).wait_recv()
        small[step + 1] = small[step] + small_in[step]
    small_sum[...] = small[len(hops)]

    ffn_near[1].wait_recv()
    up_share = Share(copies, local, up.total(), lambda at: up_sum.at[at])

    def columns(target, width):
        return lambda at: target.at[:, pl.ds(pl.multiple_of(at * width, width), width)]

    out_share = Share(
        copies, local, w_out.collect.total(), columns(out_sum, features // 4)
    )
    down_share.forward()
    gate_share.forward()
    w_in.near_all()
    w_in.combine_all()

    ffn_across.wait_recv()
    for source in (ffn_ref.at[0], ffn_in.at[0], ffn_in.at[2]):
        load = local.copy(source, d_act.at[0])
        load.wait()
        add_into(hstate, d_act.at[0])
    put_out = local.copy(hstate, outputs_ref)
    in_share = Share(
        copies, local, w_in.collect.total(), columns(in_sum, 3 * features // 4)
    )
    shares = [down_share, gate_share, up_share, out_share, in_share]
    for share in shares[2:]:
        share.forward()
    for share in shares:
        share.finish()
    put_out.wait()
    d_out.wait()
    copies.close()


def run_backward(rows, cot, gains, m_in, m_out, d_act, ffn, down, gate, up, slot):
    count, features = rows.shape
    shards, cut = down.shape[:2]
    part = m_in.shape[1]
    half = shards // 2
    hbm = pl.BlockSpec(memory_space=pltpu.HBM)
    vmem = pl.BlockSpec(memory_space=pltpu.VMEM)
    hops = 10 * shards + 40
    depth = shards.bit_length() + 1

    def blocks(shape):
        return [
            pltpu.VMEM((half, *shape), LOW),
            pltpu.VMEM((half, *shape), LOW),
            pltpu.VMEM((max(half - 1, 1), *shape), LOW),
        ]

    def quarters(width):
        return [
            pltpu.VMEM((4, shards, part, width), LOW),
            pltpu.VMEM((2, shards, part, width), LOW),
            pltpu.VMEM((shards, part, width), LOW),
            *blocks((part, width))[1:],
        ]

    whole = (count, features)
    return pl.pallas_call(
        functools.partial(backward_kernel, slot),
        out_shape=[
            jax.ShapeDtypeStruct(*shape)
            for shape in (
                (whole, F32),
                (whole, F32),
                ((4, *down.shape[1:]), LOW),
                ((4, *gate.shape[1:]), LOW),
                ((4, *up.shape[1:]), LOW),
                ((part, 3 * features), LOW),
                ((part, features), LOW),
                ((8, features), F32),
                ((3, *whole), LOW),
            )
        ],
        in_specs=[vmem, hbm, vmem] + [hbm] * 7,
        out_specs=[hbm] * 7 + [vmem, hbm],
        scratch_shapes=[
            pltpu.VMEM(m_in.shape, LOW),
            pltpu.VMEM(m_out.shape, LOW),
            pltpu.VMEM(whole, LOW),
            pltpu.VMEM(whole, F32),
            pltpu.VMEM(whole, F32),
            pltpu.VMEM(whole, F32),
            pltpu.VMEM(whole, LOW),
            pltpu.VMEM(whole, F32),
            pltpu.VMEM((2, *whole), LOW),
            pltpu.VMEM((2, *whole), LOW),
            pltpu.VMEM(whole, LOW),
            pltpu.VMEM(whole, LOW),
            pltpu.VMEM(whole, F32),
            pltpu.VMEM(whole, LOW),
            pltpu.VMEM((count, 3 * features), LOW),
            *blocks(down.shape[1:]),
            *blocks(gate.shape[1:]),
            *blocks(up.shape[1:]),
            *quarters(features // 4),
            *quarters(3 * features // 4),
            pltpu.VMEM((depth + 1, 8, features), F32),
            pltpu.VMEM((depth, 8, features), F32),
            pltpu.SemaphoreType.DMA((hops,)),
            pltpu.SemaphoreType.DMA((hops,)),
            pltpu.SemaphoreType.DMA((2 * shards + 24,)),
        ],
        compiler_params=pltpu.CompilerParams(
            collective_id=1, has_side_effects=True, vmem_limit_bytes=63 << 20
        ),
        name="backward",
    )(rows, cot, gains, m_in, m_out, d_act, ffn, down, gate, up)


def on_device(
    inputs, cotangent, lengths, norm_one, w_in, conv_w, w_out, norm_two, w_gate, w_up, w_down
):
    micro_count, tok_rows, features = inputs.shape
    shards = lax.axis_size("fsdp")
    place = lax.axis_index("fsdp")
    rep = lax.axis_index("rep")
    all_rows = micro_count * tok_rows
    cut = w_down.shape[0] // 4
    part = w_in.shape[0]
    part_ff = shards * cut

    slot_cols = jnp.arange(lengths.shape[1], dtype=jnp.int32)
    slot_id = rep * shards + place
    length_now = jnp.sum(jnp.where(slot_cols == slot_id, lengths, 0), axis=1)
    position = jnp.arange(tok_rows, dtype=jnp.int32)
    live = (position[None] < length_now[:, None])[..., None]
    cot = jnp.where(live, cotangent, jnp.zeros_like(cotangent)).reshape(all_rows, features)

    small = jnp.concatenate([norm_one[None], norm_two[None], conv_w, jnp.zeros_like(conv_w)])
    small = lax.dynamic_update_slice(
        jnp.zeros((8, features), F32), small.astype(F32), (0, place * part)
    )

    def unit_quarter(weight):
        return lax.dynamic_index_in_dim(
            weight.reshape(-1, shards, 4, cut), rep, 2, keepdims=False
        ).reshape(-1, part_ff)

    down_own = lax.dynamic_slice_in_dim(w_down, rep * cut, cut, 0)
    rows_low = inputs.reshape(all_rows, features)
    m_in, m_out, m_gate, m_up, m_down, act_all, cot_all, gains = run_forward(
        rows_low, cot, small, w_in, w_out, unit_quarter(w_gate), unit_quarter(w_up), down_own,
        tok_rows,
    )
    m_gate = m_gate.reshape(features, part_ff)
    m_up = m_up.reshape(features, part_ff)
    m_down = m_down.reshape(part_ff, features)
    act = act_all.reshape(-1, features)
    cots = cot_all.reshape(-1, features)

    gate_pre = dot(act, m_gate)
    up_pre = dot(act, m_up)
    sigmoid_g = jax.nn.sigmoid(gate_pre)
    silu_g = gate_pre * sigmoid_g
    hidden = (silu_g * up_pre).astype(LOW)
    d_hidden = dot_last(cots, m_down)
    d_gate = (d_hidden * up_pre * sigmoid_g * (1.0 + gate_pre * (1.0 - sigmoid_g))).astype(LOW)
    d_up = (d_hidden * silu_g).astype(LOW)
    d_act = (dot_last(d_gate, m_gate) + dot_last(d_up, m_up)).astype(LOW)
    ffn = dot(hidden, m_down).astype(LOW)
    grad_down = dot_first(hidden, cots).astype(LOW)
    grad_gate = dot_first(act, d_gate).astype(LOW)
    grad_up = dot_first(act, d_up).astype(LOW)

    outputs, d_rows, down_sum, gate_sum, up_sum, in_sum, out_sum, small_sum, _ = run_backward(
        rows_low, cot, gains, m_in, m_out,
        d_act.reshape(4, all_rows, features), ffn.reshape(4, all_rows, features),
        grad_down.reshape(shards, cut, features),
        grad_gate.reshape(shards, part, part_ff),
        grad_up.reshape(shards, part, part_ff),
        tok_rows,
    )

    def unit_columns(quarters):
        quarters = quarters.reshape(4, part, shards, cut)
        return quarters.transpose(1, 2, 0, 3).reshape(part, 4 * part_ff).astype(F32)

    small_own = lax.dynamic_slice_in_dim(small_sum, place * part, part, 1)
    return (
        outputs.reshape(inputs.shape),
        d_rows.reshape(inputs.shape),
        small_own[0],
        in_sum.astype(F32),
        small_own[2:5],
        out_sum.astype(F32),
        small_own[1],
        unit_columns(gate_sum),
        unit_columns(up_sum),
        down_sum.reshape(4 * cut, features).astype(F32),
    )


def solution(mesh):
    return jax.shard_map(
        on_device,
        mesh=mesh,
        in_specs=(
            P(None, ("rep", "fsdp"), None),
            P(None, ("rep", "fsdp"), None),
            P(),
            P("fsdp"),
            P("fsdp", None),
            P(None, "fsdp"),
            P("fsdp", None),
            P("fsdp"),
            P("fsdp", None),
            P("fsdp", None),
            P("fsdp", None),
        ),
        out_specs=(
            P(None, ("rep", "fsdp"), None),
            P(None, ("rep", "fsdp"), None),
            P("fsdp"),
            P("fsdp", None),
            P(None, "fsdp"),
            P("fsdp", None),
            P("fsdp"),
            P("fsdp", None),
            P("fsdp", None),
            P("fsdp", None),
        ),
        check_vma=False,
    )
```

```python
import functools

import jax
import jax.numpy as jnp
from jax import lax
from jax.experimental import pallas as pl
from jax.experimental.pallas import tpu as pltpu
from jax.sharding import PartitionSpec as P

EPSILON = 1e-05
LOW = jnp.bfloat16
F32 = jnp.float32
MESH = pl.DeviceIdType.MESH


def rms_scale(values):
    return lax.rsqrt(jnp.mean(values * values, axis=-1, keepdims=True) + EPSILON)


def dot(left, right):
    return jnp.dot(left, right, preferred_element_type=F32)


def dot_last(left, right):
    return lax.dot_general(left, right, (((1,), (1,)), ((), ())), preferred_element_type=F32)


def dot_first(left, right):
    return lax.dot_general(left, right, (((0,), (0,)), ((), ())), preferred_element_type=F32)


def norm_back(d_act, values, scale, gain):
    scaled = d_act * gain
    return scale * (
        scaled - values * scale * scale * jnp.mean(scaled * values, axis=-1, keepdims=True)
    )


def flipped(index, offset):
    bit = 1
    while bit <= offset:
        if offset & bit:
            index = index + bit - 2 * bit * ((index // bit) % 2)
        bit *= 2
    return index


class Copy:
    def __init__(self, copies, at, source, target, bits):
        self.copies, self.at, self.bits = copies, at, bits
        self.source, self.target = source, target

    def made(self):
        return pltpu.make_async_remote_copy(
            src_ref=self.source() if callable(self.source) else self.source,
            dst_ref=self.target() if callable(self.target) else self.target,
            send_sem=self.copies.sems[0].at[self.at],
            recv_sem=self.copies.sems[1].at[self.at],
            device_id=self.copies.peer(*self.bits),
            device_id_type=MESH,
        )

    def wait_recv(self):
        self.made().wait_recv()

    def wait_send(self):
        self.made().wait_send()


class Copies:
    def __init__(self, send_sems, recv_sems):
        self.sems = send_sems, recv_sems
        self.rep = lax.axis_index("rep")
        self.place = lax.axis_index("fsdp")
        self.started = []
        self.done = []

    def peer(self, rep_bits, place_bits):
        return (flipped(self.rep, rep_bits), flipped(self.place, place_bits))

    def meet(self, peers):
        barrier = pltpu.get_barrier_semaphore()
        for bits in peers:
            pl.semaphore_signal(barrier, inc=1, device_id=self.peer(*bits), device_id_type=MESH)
        pl.semaphore_wait(barrier, len(peers))

    def send(self, source, target, rep_bits, place_bits):
        copy = Copy(self, len(self.started), source, target, (rep_bits, place_bits))
        copy.made().start()
        self.started.append(copy)
        return copy

    def sent(self, copy):
        copy.wait_send()
        self.done.append(copy)

    def close(self):
        for copy in self.started:
            if not any(copy is other for other in self.done):
                copy.wait_send()


class Local:
    def __init__(self, sems):
        self.sems = sems
        self.started = []

    def copy(self, source, target):
        copy = pltpu.make_async_copy(source, target, self.sems.at[len(self.started)])
        copy.start()
        self.started.append(copy)
        return copy


class Spread:
    def __init__(self, copies, locals_, shards, source, target, at=None):
        self.copies = copies
        self.target = target
        self.at = at if at is not None else (lambda shard: target.at[shard])
        self.source = source
        self.locals = locals_
        self.far = list(range(2, shards, 2))
        self.near = [1] + [offset + 1 for offset in self.far]

    def start(self):
        copies = self.copies
        here = self.at(copies.place)
        self.arriving = {offset: copies.send(self.source, here, 0, offset) for offset in self.far}
        self.arriving[1] = copies.send(self.source, here, 0, 1)
        if self.locals is not None:
            self.own = self.locals.copy(self.source, here)

    def arrive(self, offset):
        self.arriving[offset].wait_recv()
        if offset % 2 == 0:
            block = self.at(flipped(self.copies.place, offset))
            self.arriving[offset + 1] = self.copies.send(block, block, 0, 1)

    def finish(self):
        for offset in self.near:
            self.arriving[offset].wait_recv()
        if self.locals is not None:
            self.own.wait()


class SpreadAll(Spread):
    def __init__(self, copies, locals_, shards, source, target, width):
        self.width = width
        self.whole = source
        self.local_all = locals_
        rep = copies.rep
        super().__init__(
            copies,
            None,
            shards,
            source.at[:, self.columns(rep)],
            target,
            lambda shard: target.at[shard, :, self.columns(rep)],
        )
        self.across = {}
        self.core = []

    def columns(self, rep):
        return pl.ds(pl.multiple_of(rep * self.width, self.width), self.width)

    def start(self):
        super().start()
        self.own = self.local_all.copy(self.whole, self.target.at[self.copies.place])

    def arrive(self, offset):
        super().arrive(offset)
        block = self.at(flipped(self.copies.place, offset))
        self.across[offset] = self.copies.send(block, block, 2, 0)
        self.core.append(self.copies.send(block, block, 1, 0))

    def cross(self, offset):
        copies = self.copies
        self.across[offset].wait_recv()
        shard = flipped(copies.place, offset)
        block = self.target.at[shard, :, self.columns(flipped(copies.rep, 2))]
        self.core.append(copies.send(block, block, 1, 0))

    def finish(self):
        for copy in self.core:
            copy.wait_recv()
        self.own.wait()


def row_loop(rows, step, body):
    @pl.loop(0, rows // step)
    def _(at):
        body(pl.ds(pl.multiple_of(at * step, step), step))


def normed(values, gain):
    return values * rms_scale(values) * gain


def shifted(values, by):
    rows = values.shape[0]
    at = lax.broadcasted_iota(jnp.int32, values.shape, 0)
    turned = pltpu.roll(values, by % rows, 0)
    kept = at >= by if by > 0 else at < rows + by
    return jnp.where(kept, turned, 0.0)


def mixer_columns(act, m_in, gains, at, width, features, slot):
    lanes = pl.ds(at, width)
    parts = []
    for base in (0, features, 2 * features):
        block = m_in[:, :, base + at : base + at + width].reshape(features, width)
        parts.append(dot(act, block))
    part_b, part_c, part_x = parts
    taps = [gains[2 + k : 3 + k, at : at + width] for k in range(3)]
    product = part_b * part_x
    convolved = []
    for start in range(0, act.shape[0], slot):
        rows = product[start : start + slot]
        convolved.append(
            taps[0] * shifted(rows, 2) + taps[1] * shifted(rows, 1) + taps[2] * rows
        )
    return part_b, part_c, part_x, product, jnp.concatenate(convolved)


def forward_kernel(
    slot,
    rows_ref, cot_ref, small_ref, in_ref, out_ref, units_ref, down_ref,
    all_in, all_out, all_units, all_down, all_act, all_cot, gains_ref,
    small_all, v_in, v_out, act_one, mixer_in, act_two,
    send_sems, recv_sems, local_sems,
):
    rows, features = rows_ref.shape
    shards = all_units.shape[0]
    copies = Copies(send_sems, recv_sems)
    local = Local(local_sems)
    far = list(range(2, shards, 2))
    copies.meet([(0, offset) for offset in [*far, 1]] + [(1, 0), (2, 0)])

    small = Spread(copies, local, shards, small_ref, small_all)
    w_in = SpreadAll(copies, local, shards, in_ref, v_in, in_ref.shape[1] // 4)
    w_out = SpreadAll(copies, local, shards, out_ref, v_out, out_ref.shape[1] // 4)
    units = Spread(copies, local, shards, units_ref, all_units)
    down = Spread(copies, local, shards, down_ref, all_down)

    small.start()
    w_in.start()
    w_out.start()
    own_cot = local.copy(cot_ref, all_cot.at[0])
    for offset in far:
        small.arrive(offset)
    small.finish()
    gains_ref[...] = jnp.sum(small_all[...], axis=0)
    gain_one = gains_ref[0:1]

    def first(at):
        act_one[at] = normed(rows_ref[at].astype(F32), gain_one).astype(LOW)

    w_in.arrive(far[0])
    w_in.arrive(1)
    row_loop(rows, 64, first)
    units.start()
    for offset in far[1:]:
        w_in.arrive(offset)
    for offset in far:
        w_in.arrive(offset + 1)
    w_out.arrive(1)
    for offset in far:
        w_out.arrive(offset)
    for offset in far:
        w_out.arrive(offset + 1)
    down.start()
    cot_core = copies.send(cot_ref, all_cot.at[1], 1, 0)
    cot_across = copies.send(cot_ref, all_cot.at[2], 2, 0)
    order = [1, *far, *[offset + 1 for offset in far]]
    for offset in order:
        w_in.cross(offset)
    for offset in far:
        units.arrive(offset)
    for offset in order:
        w_out.cross(offset)
    w_in.finish()

    width = features // 4
    for part in range(4):
        at = part * width
        _, part_c, _, _, convolved = mixer_columns(
            act_one[...], v_in, gains_ref, at, width, features, slot
        )
        mixer_in[:, at : at + width] = (part_c * convolved).astype(LOW)
    keep_in = local.copy(v_in, all_in)
    w_out.finish()
    keep_out = local.copy(v_out, all_out)
    spread = []
    for start in range(0, rows, slot):
        held = slice(start, start + slot)
        hstate = rows_ref[held].astype(F32) + dot(
            mixer_in[held], v_out[...].reshape(features, features)
        )
        act_two[held] = normed(hstate, gains_ref[1:2]).astype(LOW)
        block = act_two.at[held]
        spread.append(
            (
                held,
                copies.send(block, all_act.at[2, held], 2, 0),
                copies.send(block, all_act.at[1, held], 1, 0),
                local.copy(block, all_act.at[0, held]),
            )
        )
    for offset in far:
        down.arrive(offset)
    cot_across.wait_recv()
    corner = [copies.send(all_cot.at[2], all_cot.at[3], 1, 0)]
    for held, across, _, _ in spread:
        across.wait_recv()
        corner.append(copies.send(all_act.at[2, held], all_act.at[3, held], 1, 0))
    units.finish()
    down.finish()
    cot_core.wait_recv()
    for _, _, core, own in spread:
        core.wait_recv()
        own.wait()
    for copy in corner:
        copy.wait_recv()
    own_cot.wait()
    keep_in.wait()
    keep_out.wait()
    copies.close()


def run_forward(rows, cot, small, w_in, w_out, units, down, slot):
    shards = lax.axis_size("fsdp")
    count, features = rows.shape
    part = w_in.shape[0]
    shapes = [
        ((shards, *w_in.shape), LOW),
        ((shards, *w_out.shape), LOW),
        ((shards, *units.shape), LOW),
        ((shards, *down.shape), LOW),
        ((4, count, features), LOW),
        ((4, count, features), LOW),
    ]
    hbm = pl.BlockSpec(memory_space=pltpu.HBM)
    vmem = pl.BlockSpec(memory_space=pltpu.VMEM)
    hops = 12 * shards + 16
    return pl.pallas_call(
        functools.partial(forward_kernel, slot),
        out_shape=[jax.ShapeDtypeStruct(*shape) for shape in shapes]
        + [jax.ShapeDtypeStruct((8, features), F32)],
        in_specs=[vmem, hbm, vmem, hbm, hbm, hbm, hbm],
        out_specs=[hbm] * 6 + [vmem],
        scratch_shapes=[
            pltpu.VMEM((shards, 8, features), F32),
            pltpu.VMEM((shards, *w_in.shape), LOW),
            pltpu.VMEM((shards, *w_out.shape), LOW),
            pltpu.VMEM((count, features), LOW),
            pltpu.VMEM((count, features), LOW),
            pltpu.VMEM((count, features), LOW),
            pltpu.SemaphoreType.DMA((hops,)),
            pltpu.SemaphoreType.DMA((hops,)),
            pltpu.SemaphoreType.DMA((16,)),
        ],
        compiler_params=pltpu.CompilerParams(
            collective_id=0, has_side_effects=True, vmem_limit_bytes=56 << 20
        ),
        name="forward",
    )(rows, cot, small, w_in, w_out, units, down)


def add_into(target, *others):
    rows = target.shape[-2]
    step = 16 if rows % 16 == 0 else rows
    lead = target.shape[:-2]

    @pl.loop(0, rows // step)
    def _(at):
        held = pl.ds(pl.multiple_of(at * step, step), step)
        index = (slice(None),) * len(lead) + (held,)
        total = target[index].astype(F32)
        for other in others:
            total = total + other[index].astype(F32)
        target[index] = total.astype(target.dtype)


class Collect:
    def __init__(self, copies, shards, sent_at, own_at, near_in, far_in):
        self.copies = copies
        self.sent_at, self.own_at = sent_at, own_at
        self.near_in, self.far_in = near_in, far_in
        self.order = [*range(2, shards, 2), 0]
        self.arriving = {}
        self.far = {}

    def near(self, offset):
        copies = self.copies
        self.arriving[offset] = copies.send(
            lambda: self.sent_at(offset + 1), lambda: self.near_in.at[offset // 2], 0, 1
        )

    def near_all(self):
        for offset in self.order:
            self.near(offset)

    def combine(self, offset):
        self.arriving[offset].wait_recv()
        own = self.own_at(offset)
        add_into(own, self.near_in.at[offset // 2])
        if offset:
            self.far[offset] = self.copies.send(
                lambda: self.own_at(offset), lambda: self.far_in.at[offset // 2 - 1], 0, offset
            )

    def combine_all(self):
        for offset in self.order:
            self.combine(offset)

    def total(self):
        for copy in self.far.values():
            copy.wait_recv()
        own = self.own_at(0)
        add_into(own, *[self.far_in.at[k] for k in range(len(self.far))])
        return own


class Share:
    def __init__(self, copies, local, source, target_at):
        self.copies = copies
        self.target_at = target_at
        here = target_at(copies.rep)
        self.across = copies.send(source, here, 2, 0)
        self.core = [copies.send(source, here, 1, 0)]
        self.own = local.copy(source, here)

    def forward(self):
        self.across.wait_recv()
        block = self.target_at(flipped(self.copies.rep, 2))
        self.core.append(self.copies.send(block, block, 1, 0))

    def finish(self):
        for copy in self.core:
            copy.wait_recv()
        self.own.wait()


class CollectAll:
    def __init__(self, copies, shards, width, parts, core_in, cross_in, near_in, far_in):
        self.copies = copies
        self.width = width
        self.parts, self.core_in, self.cross_in = parts, core_in, cross_in
        place = copies.place
        self.collect = Collect(
            copies,
            shards,
            lambda offset: parts.at[0, flipped(place, offset)],
            lambda offset: parts.at[0, flipped(place, offset)],
            near_in,
            far_in,
        )
        self.core = {}
        self.cross = {}
        self.order = [o + 1 for o in self.collect.order] + self.collect.order

    def compute(self, turn, left, right):
        rep = flipped(self.copies.rep, turn)
        shards, rows, _ = self.parts.shape[1:]
        for at in range(0, self.width, 256):
            columns = pl.ds(pl.multiple_of(rep * self.width + at, 256), 256)
            block = dot_first(left[...], right[:, columns]).astype(LOW)
            self.parts[turn, :, :, at : at + 256] = block.reshape(shards, rows, 256)

    def to_core(self, turn):
        self.core[turn - 1] = self.copies.send(
            lambda: self.parts.at[turn], lambda: self.core_in.at[turn // 2], 1, 0
        )

    def to_cross(self):
        self.core[2].wait_recv()
        place = self.copies.place
        for offset in self.order:
            block = self.parts.at[2, flipped(place, offset)]
            add_into(block, self.core_in.at[1, flipped(place, offset)])
            self.cross_one(offset)
        self.core[0].wait_recv()

    def cross_one(self, offset):
        place = self.copies.place
        self.cross[offset] = self.copies.send(
            lambda: self.parts.at[2, flipped(place, offset)],
            lambda: self.cross_in.at[flipped(place, offset)],
            2,
            0,
        )

    def arrive(self, offset):
        self.cross[offset].wait_recv()
        shard = flipped(self.copies.place, offset)
        add_into(self.parts.at[0, shard], self.core_in.at[0, shard], self.cross_in.at[shard])

    def near_all(self):
        for offset in self.collect.order:
            self.arrive(offset + 1)
            self.collect.near(offset)

    def combine_all(self):
        for offset in self.collect.order:
            self.arrive(offset)
            self.collect.combine(offset)


def feed_forward_rows(act, cot, units, down, hidden, d_units, width):
    act_rows, cot_rows = act[...], cot[...]
    step = 256

    def columns(at, size):
        lanes, up_lanes = pl.ds(at, size), pl.ds(width + at, size)
        gate_pre = dot(act_rows, units[:, lanes])
        up_pre = dot(act_rows, units[:, up_lanes])
        d_hidden = dot_last(cot_rows, down[lanes])
        sigmoid_g = jax.nn.sigmoid(gate_pre)
        silu_g = gate_pre * sigmoid_g
        hidden[:, lanes] = (silu_g * up_pre).astype(LOW)
        d_units[:, lanes] = (
            d_hidden * up_pre * sigmoid_g * (1.0 + gate_pre * (1.0 - sigmoid_g))
        ).astype(LOW)
        d_units[:, up_lanes] = (d_hidden * silu_g).astype(LOW)

    @pl.loop(0, width // step)
    def _(at):
        columns(pl.multiple_of(at * step, 128), step)

    if width % step:
        columns(width - width % step, width % step)


def put_shards(target, columns, block):
    shards, rows = target.shape[:2]
    if rows % 16 == 0:
        target[:, :, columns] = block.reshape(shards, rows, block.shape[1])
    else:
        for shard in range(shards):
            target[shard, :, columns] = block[shard * rows : (shard + 1) * rows]


def backward_kernel(
    slot,
    all_rows_ref, gains_ref, in_ref, out_ref, units_ref, down_ref, act_ref, cot_ref,
    outputs_ref, d_rows_ref, down_sum, units_sum, in_sum, out_sum, small_sum, ffn_part, ffn_in,
    d_act, d_core, d_cross, down_grad, down_near, down_far, units_grad, units_near, units_far,
    w_out_core, w_out_cross, w_out_near, w_out_far,
    w_in_core, w_in_cross, w_in_near, w_in_far,
    small, small_in, send_sems, recv_sems, local_sems,
):
    rows, features = all_rows_ref.shape
    shards = units_grad.shape[0]
    units_width = down_ref.shape[0]
    copies = Copies(send_sems, recv_sems)
    local = Local(local_sems)
    place = copies.place
    far = list(range(2, shards, 2))
    bits = [1 << k for k in range(1, shards.bit_length() - 1)]
    copies.meet([(0, offset) for offset in [*far, 1]] + [(1, 0), (2, 0)])

    def collector(grad, near, far_in):
        at = lambda offset: grad.at[flipped(place, offset)]
        return Collect(copies, shards, at, at, near, far_in)

    down = collector(down_grad, down_near, down_far)
    units = collector(units_grad, units_near, units_far)
    d_near, d_far, ffn_near = {}, [], {}

    def feed_forward(m_units, m_down, act, cot, hidden, d_units):
        part = lambda ref, turn: ref.at[turn * rows : (turn + 1) * rows]
        loads = {"units": local.copy(units_ref, m_units)}
        for turn in (3, 2, 1, 0):
            loads[turn] = [
                local.copy(act_ref.at[turn], part(act, turn)),
                local.copy(cot_ref.at[turn], part(cot, turn)),
            ]
            if turn == 3:
                loads["down"] = local.copy(down_ref, m_down)

        def units_of(turn):
            for load in loads[turn]:
                load.wait()
            if turn == 3:
                loads["units"].wait()
                loads["down"].wait()
            feed_forward_rows(
                part(act, turn), part(cot, turn), m_units, m_down,
                part(hidden, turn), part(d_units, turn), units_width,
            )

        def d_act_of(turn):
            block = part(d_units, turn)
            d_act[turn] = dot_last(block[...], m_units[...]).astype(LOW)
            if turn % 2:
                d_near[turn] = copies.send(
                    lambda: d_act.at[turn], lambda: d_core.at[turn // 2], 1, 0
                )

        def send_across(held):
            return copies.send(lambda: d_act.at[2, held], lambda: d_cross.at[held], 2, 0)

        def send_ffn(turn):
            return copies.send(
                lambda: ffn_part.at[turn], lambda: ffn_in.at[turn // 2], 1, 0
            )

        puts = []

        def ffn_of(turn):
            block = part(hidden, turn)
            block[:, :features] = dot(block[...], m_down[...]).astype(LOW)
            puts.append(local.copy(block.at[:, :features], ffn_part.at[turn]))

        for turn in (3, 2):
            units_of(turn)
            d_act_of(turn)
        d_near[3].wait_recv()
        for start in range(0, rows, slot):
            held = slice(start, start + slot)
            add_into(d_act.at[2, held], d_core.at[1, held])
            d_far.append(send_across(held))
        for turn in (1, 0):
            units_of(turn)
        for at in range(0, features, 256):
            lanes = slice(at, at + 256)
            put_shards(down_grad, lanes, dot_first(hidden[...], cot[:, lanes]).astype(LOW))
        down.near_all()
        d_act_of(1)
        ffn_of(3)
        ffn_of(1)
        per = 256 * shards // features
        for at in range(0, features, 256):
            shard = at * shards // features
            block = dot_first(act[:, at : at + 256], d_units[...]).astype(LOW)
            units_grad[shard : shard + per] = block.reshape(per, -1, block.shape[1])
            if at == 0:
                for turn, put in zip((3, 1), puts):
                    put.wait()
                    ffn_near[turn] = send_ffn(turn)
        units.near_all()
        del puts[:]
        d_act_of(0)
        ffn_of(2)
        ffn_of(0)
        down.combine_all()
        for put in puts:
            put.wait()

    pl.run_scoped(
        feed_forward,
        pltpu.VMEM(units_ref.shape, LOW),
        pltpu.VMEM(down_ref.shape, LOW),
        pltpu.VMEM((4 * rows, features), LOW),
        pltpu.VMEM((4 * rows, features), LOW),
        pltpu.VMEM((4 * rows, units_width), LOW),
        pltpu.VMEM((4 * rows, 2 * units_width), LOW),
    )

    def mixer(
        rows_ref, v_in, v_out, act_one, mixer_in, hstate, d_hstate, d_mixer, d_proj, w_out_parts
    ):
        load_rows = local.copy(all_rows_ref, rows_ref)
        load_in = local.copy(in_ref, v_in)
        load_out = local.copy(out_ref, v_out)
        gain_one, gain_two = gains_ref[0:1], gains_ref[1:2]

        copies.sent(d_near[3])
        ffn_other = d_act.at[3]
        load = local.copy(ffn_part.at[2], ffn_other)
        load.wait()
        ffn_near[3].wait_recv()
        load = local.copy(ffn_in.at[1], d_mixer)
        load.wait()
        add_into(ffn_other, d_mixer)
        ffn_across = copies.send(ffn_other, ffn_in.at[2], 2, 0)
        load_cot = local.copy(cot_ref.at[0], d_mixer)

        def first(at):
            act_one[at] = normed(rows_ref[at].astype(F32), gain_one).astype(LOW)

        load_rows.wait()
        row_loop(rows, 64, first)
        load_in.wait()
        width = features // 4
        w_out = CollectAll(
            copies, shards, width, w_out_parts, w_out_core, w_out_cross, w_out_near, w_out_far
        )

        def columns_back(part_b, part_c, part_x):
            for part in range(4):
                at = part * width
                lanes = slice(at, at + width)
                b_now, c_now, x_now, _, convolved = mixer_columns(
                    act_one[...], v_in, gains_ref, at, width, features, slot
                )
                part_b[:, lanes] = b_now
                part_c[:, lanes] = c_now
                part_x[:, lanes] = x_now
                mixer_in[:, lanes] = (c_now * convolved).astype(LOW)
            load_out.wait()
            for start in range(0, rows, slot):
                held = slice(start, start + slot)
                hstate[held] = rows_ref[held].astype(F32) + dot(
                    mixer_in[held], v_out[...].reshape(features, features)
                )

            d_near[1].wait_recv()
            small[0] = jnp.zeros((8, features), F32)

            def second(at):
                d_now = (
                    d_act[0, at].astype(F32) + d_core[0, at].astype(F32) + d_cross[at].astype(F32)
                )
                values = hstate[at]
                scale = rms_scale(values)
                small[0, 1:2] += jnp.sum(d_now * values * scale, axis=0, keepdims=True)
                d_values = d_mixer[at].astype(F32) + norm_back(d_now, values, scale, gain_two)
                d_hstate[at] = d_values
                d_mixer[at] = d_values.astype(LOW)

            for copy in d_far:
                copy.wait_recv()
            load_cot.wait()
            row_loop(rows, 64, second)

            for turn in (3, 1):
                w_out.compute(turn, mixer_in, d_mixer)
                w_out.to_core(turn)
            for turn in (2, 0):
                w_out.compute(turn, mixer_in, d_mixer)

            per = shards * width // features
            for part in range(4):
                at = part * width
                lanes = slice(at, at + width)
                block = v_out[part * per : (part + 1) * per].reshape(width, features)
                d_mixin = dot_last(d_mixer[...], block)
                taps = [gains_ref[2 + k : 3 + k, lanes] for k in range(3)]
                for start in range(0, rows, slot):
                    held = slice(start, start + slot)
                    d_mix = d_mixin[held]
                    b_now, c_now, x_now = part_b[held, lanes], part_c[held, lanes], part_x[held, lanes]
                    product = b_now * x_now
                    before = [shifted(product, 2), shifted(product, 1), product]
                    convolved = taps[0] * before[0] + taps[1] * before[1] + taps[2] * before[2]
                    d_conv = d_mix * c_now
                    for k in range(3):
                        small[0, 2 + k : 3 + k, lanes] += jnp.sum(
                            d_conv * before[k], axis=0, keepdims=True
                        )
                    d_product = (
                        taps[2] * d_conv
                        + taps[1] * shifted(d_conv, -1)
                        + taps[0] * shifted(d_conv, -2)
                    )
                    d_proj[held, lanes] = (d_product * x_now).astype(LOW)
                    d_proj[held, features + at : features + at + width] = (d_mix * convolved).astype(LOW)
                    d_proj[held, 2 * features + at : 2 * features + at + width] = (
                        d_product * b_now
                    ).astype(LOW)
                if part == 0:
                    w_out.to_cross()

        pl.run_scoped(columns_back, *[pltpu.VMEM((rows, features), F32)] * 3)

        def finish(w_in_parts):
            w_in = CollectAll(
                copies, shards, 3 * width, w_in_parts, w_in_core, w_in_cross, w_in_near, w_in_far
            )
            for turn in (3, 1):
                w_in.compute(turn, act_one, d_proj)
                w_in.to_core(turn)
            units.combine(units.order[0])
            for turn in (2, 0):
                w_in.compute(turn, act_one, d_proj)
            w_in.to_cross()
            for offset in units.order[1:]:
                units.combine(offset)
            down_share = Share(copies, local, down.total(), lambda at: down_sum.at[at])
            w_out.near_all()

            for start in range(0, rows, slot):
                held = slice(start, start + slot)
                d_now = dot_last(d_proj[held], v_in[...].reshape(features, 3 * features))
                values = rows_ref[held].astype(F32)
                scale = rms_scale(values)
                small[0, 0:1] += jnp.sum(d_now * values * scale, axis=0, keepdims=True)
                d_hstate[held] += norm_back(d_now, values, scale, gain_one)
            d_out = local.copy(d_hstate, d_rows_ref)
            w_out.combine_all()

            hops = [(0, 1), *[(0, bit) for bit in bits], (1, 0), (2, 0)]
            for step, (rep_bits, place_bits) in enumerate(hops):
                copies.send(small.at[step], small_in.at[step], rep_bits, place_bits).wait_recv()
                small[step + 1] = small[step] + small_in[step]
            small_sum[...] = small[len(hops)]

            def columns(target, width):
                return lambda at: target.at[:, pl.ds(pl.multiple_of(at * width, width), width)]

            w_in.near_all()
            units_share = Share(copies, local, units.total(), lambda at: units_sum.at[at])
            out_share = Share(copies, local, w_out.collect.total(), columns(out_sum, width))
            down_share.forward()
            w_in.combine_all()

            ffn_near[1].wait_recv()
            ffn_across.wait_recv()
            for source in (ffn_part.at[0], ffn_in.at[0], ffn_in.at[2]):
                load = local.copy(source, d_act.at[0])
                load.wait()
                add_into(hstate, d_act.at[0])
            put_out = local.copy(hstate, outputs_ref)
            in_share = Share(copies, local, w_in.collect.total(), columns(in_sum, 3 * width))
            shares = [down_share, units_share, out_share, in_share]
            for share in shares[1:]:
                share.forward()
            for share in shares:
                share.finish()
            put_out.wait()
            d_out.wait()
            copies.close()

        pl.run_scoped(finish, pltpu.VMEM((4, shards, part_rows, 3 * width), LOW))

    whole = (rows, features)
    part_rows = in_ref.shape[1]
    pl.run_scoped(
        mixer,
        pltpu.VMEM(whole, LOW),
        pltpu.VMEM(in_ref.shape, LOW),
        pltpu.VMEM(out_ref.shape, LOW),
        pltpu.VMEM(whole, LOW),
        pltpu.VMEM(whole, LOW),
        pltpu.VMEM(whole, F32),
        pltpu.VMEM(whole, F32),
        pltpu.VMEM(whole, LOW),
        pltpu.VMEM((rows, 3 * features), LOW),
        pltpu.VMEM((4, shards, part_rows, features // 4), LOW),
    )


def run_backward(rows, gains, m_in, m_out, m_units, m_down, act, cot, slot):
    count, features = rows.shape
    shards, part = m_in.shape[:2]
    cut = m_down.shape[0] // shards
    units = m_units.shape[1]
    half = shards // 2
    hbm = pl.BlockSpec(memory_space=pltpu.HBM)
    vmem = pl.BlockSpec(memory_space=pltpu.VMEM)
    hops = 10 * shards + 40
    depth = shards.bit_length() + 1

    def blocks(*shape):
        return [
            pltpu.VMEM((half, *shape), LOW),
            pltpu.VMEM((max(half - 1, 1), *shape), LOW),
        ]

    def quarters(width):
        return [
            pltpu.VMEM((2, shards, part, width), LOW),
            pltpu.VMEM((shards, part, width), LOW),
            *blocks(part, width),
        ]

    whole = (count, features)
    return pl.pallas_call(
        functools.partial(backward_kernel, slot),
        out_shape=[
            jax.ShapeDtypeStruct(*shape)
            for shape in (
                (whole, F32),
                (whole, F32),
                ((4, cut, features), LOW),
                ((4, part, units), LOW),
                ((part, 3 * features), LOW),
                ((part, features), LOW),
                ((8, features), F32),
                ((4, *whole), LOW),
                ((3, *whole), LOW),
            )
        ],
        in_specs=[hbm, vmem] + [hbm] * 6,
        out_specs=[hbm] * 6 + [vmem, hbm, hbm],
        scratch_shapes=[
            pltpu.VMEM((4, *whole), LOW),
            pltpu.VMEM((2, *whole), LOW),
            pltpu.VMEM(whole, LOW),
            pltpu.VMEM((shards, cut, features), LOW),
            *blocks(cut, features),
            pltpu.VMEM((shards, part, units), LOW),
            *blocks(part, units),
            *quarters(features // 4),
            *quarters(3 * features // 4),
            pltpu.VMEM((depth + 1, 8, features), F32),
            pltpu.VMEM((depth, 8, features), F32),
            pltpu.SemaphoreType.DMA((hops,)),
            pltpu.SemaphoreType.DMA((hops,)),
            pltpu.SemaphoreType.DMA((48,)),
        ],
        compiler_params=pltpu.CompilerParams(
            collective_id=1, has_side_effects=True, vmem_limit_bytes=127 << 19
        ),
        name="backward",
    )(rows, gains, m_in, m_out, m_units, m_down, act, cot)


def on_device(
    inputs, cotangent, lengths, norm_one, w_in, conv_w, w_out, norm_two, w_gate, w_up, w_down
):
    micro_count, tok_rows, features = inputs.shape
    shards = lax.axis_size("fsdp")
    place = lax.axis_index("fsdp")
    rep = lax.axis_index("rep")
    all_rows = micro_count * tok_rows
    cut = w_down.shape[0] // 4
    part = w_in.shape[0]
    part_ff = shards * cut

    slot_cols = jnp.arange(lengths.shape[1], dtype=jnp.int32)
    slot_id = rep * shards + place
    length_now = jnp.sum(jnp.where(slot_cols == slot_id, lengths, 0), axis=1)
    position = jnp.arange(tok_rows, dtype=jnp.int32)
    live = (position[None] < length_now[:, None])[..., None]
    cot = jnp.where(live, cotangent, jnp.zeros_like(cotangent)).reshape(all_rows, features)

    small = jnp.concatenate([norm_one[None], norm_two[None], conv_w, jnp.zeros_like(conv_w)])
    small = lax.dynamic_update_slice(
        jnp.zeros((8, features), F32), small.astype(F32), (0, place * part)
    )

    def unit_quarter(weight):
        return lax.dynamic_index_in_dim(
            weight.reshape(-1, shards, 4, cut), rep, 2, keepdims=False
        ).reshape(-1, part_ff)

    down_own = lax.dynamic_slice_in_dim(w_down, rep * cut, cut, 0)
    rows_low = inputs.reshape(all_rows, features)
    units_own = jnp.concatenate([unit_quarter(w_gate), unit_quarter(w_up)], axis=1)
    m_in, m_out, m_units, m_down, act_all, cot_all, gains = run_forward(
        rows_low, cot, small, w_in, w_out, units_own, down_own, tok_rows
    )

    outputs, d_rows, down_sum, units_sum, in_sum, out_sum, small_sum, _, _ = run_backward(
        rows_low, gains, m_in, m_out, m_units.reshape(features, 2 * part_ff),
        m_down.reshape(part_ff, features), act_all, cot_all, tok_rows,
    )

    def unit_columns(quarters):
        quarters = quarters.reshape(4, part, shards, cut)
        return quarters.transpose(1, 2, 0, 3).reshape(part, 4 * part_ff).astype(F32)

    small_own = lax.dynamic_slice_in_dim(small_sum, place * part, part, 1)
    return (
        outputs.reshape(inputs.shape),
        d_rows.reshape(inputs.shape),
        small_own[0],
        in_sum.astype(F32),
        small_own[2:5],
        out_sum.astype(F32),
        small_own[1],
        unit_columns(units_sum[:, :, :part_ff]),
        unit_columns(units_sum[:, :, part_ff:]),
        down_sum.reshape(4 * cut, features).astype(F32),
    )


def solution(mesh):
    return jax.shard_map(
        on_device,
        mesh=mesh,
        in_specs=(
            P(None, ("rep", "fsdp"), None),
            P(None, ("rep", "fsdp"), None),
            P(),
            P("fsdp"),
            P("fsdp", None),
            P(None, "fsdp"),
            P("fsdp", None),
            P("fsdp"),
            P("fsdp", None),
            P("fsdp", None),
            P("fsdp", None),
        ),
        out_specs=(
            P(None, ("rep", "fsdp"), None),
            P(None, ("rep", "fsdp"), None),
            P("fsdp"),
            P("fsdp", None),
            P(None, "fsdp"),
            P("fsdp", None),
            P("fsdp"),
            P("fsdp", None),
            P("fsdp", None),
            P("fsdp", None),
        ),
        check_vma=False,
    )
```

```python
import functools

import jax
import jax.numpy as jnp
from jax import lax
from jax.experimental import pallas as pl
from jax.experimental.pallas import tpu as pltpu
from jax.sharding import PartitionSpec as P

EPSILON = 1e-05
LOW = jnp.bfloat16
F32 = jnp.float32
MESH = pl.DeviceIdType.MESH


def rms_scale(values):
    return lax.rsqrt(jnp.mean(values * values, axis=-1, keepdims=True) + EPSILON)


def dot(left, right):
    return jnp.dot(left, right, preferred_element_type=F32)


def dot_last(left, right):
    return lax.dot_general(left, right, (((1,), (1,)), ((), ())), preferred_element_type=F32)


def dot_first(left, right):
    return lax.dot_general(left, right, (((0,), (0,)), ((), ())), preferred_element_type=F32)


def norm_back(d_act, values, scale, gain):
    scaled = d_act * gain
    return scale * (
        scaled - values * scale * scale * jnp.mean(scaled * values, axis=-1, keepdims=True)
    )


def flipped(index, offset):
    bit = 1
    while bit <= offset:
        if offset & bit:
            index = index + bit - 2 * bit * ((index // bit) % 2)
        bit *= 2
    return index


class Copy:
    def __init__(self, copies, at, source, target, bits):
        self.copies, self.at, self.bits = copies, at, bits
        self.source, self.target = source, target

    def made(self):
        return pltpu.make_async_remote_copy(
            src_ref=self.source() if callable(self.source) else self.source,
            dst_ref=self.target() if callable(self.target) else self.target,
            send_sem=self.copies.sems[0].at[self.at],
            recv_sem=self.copies.sems[1].at[self.at],
            device_id=self.copies.peer(*self.bits),
            device_id_type=MESH,
        )

    def wait_recv(self):
        self.made().wait_recv()

    def wait_send(self):
        self.made().wait_send()


class Copies:
    def __init__(self, send_sems, recv_sems):
        self.sems = send_sems, recv_sems
        self.rep = lax.axis_index("rep")
        self.place = lax.axis_index("fsdp")
        self.started = []
        self.done = []

    def peer(self, rep_bits, place_bits):
        return (flipped(self.rep, rep_bits), flipped(self.place, place_bits))

    def meet(self, peers):
        barrier = pltpu.get_barrier_semaphore()
        for bits in peers:
            pl.semaphore_signal(barrier, inc=1, device_id=self.peer(*bits), device_id_type=MESH)
        pl.semaphore_wait(barrier, len(peers))

    def send(self, source, target, rep_bits, place_bits):
        copy = Copy(self, len(self.started), source, target, (rep_bits, place_bits))
        copy.made().start()
        self.started.append(copy)
        return copy

    def sent(self, copy):
        copy.wait_send()
        copy.source = copy.target
        self.done.append(copy)

    def close(self):
        for copy in self.started:
            if not any(copy is other for other in self.done):
                copy.wait_send()


class Local:
    def __init__(self, sems):
        self.sems = sems
        self.started = []

    def copy(self, source, target):
        copy = pltpu.make_async_copy(source, target, self.sems.at[len(self.started)])
        copy.start()
        self.started.append(copy)
        return copy


class Spread:
    def __init__(self, copies, locals_, shards, source, target, at=None):
        self.copies = copies
        self.target = target
        self.at = at if at is not None else (lambda shard: target.at[shard])
        self.source = source
        self.locals = locals_
        self.far = list(range(2, shards, 2))
        self.near = [1] + [offset + 1 for offset in self.far]

    def start(self):
        copies = self.copies
        here = self.at(copies.place)
        self.arriving = {offset: copies.send(self.source, here, 0, offset) for offset in self.far}
        self.arriving[1] = copies.send(self.source, here, 0, 1)
        if self.locals is not None:
            self.own = self.locals.copy(self.source, here)

    def arrive(self, offset):
        self.arriving[offset].wait_recv()
        if offset % 2 == 0:
            block = self.at(flipped(self.copies.place, offset))
            self.arriving[offset + 1] = self.copies.send(block, block, 0, 1)

    def finish(self):
        for offset in self.near:
            self.arriving[offset].wait_recv()
        if self.locals is not None:
            self.own.wait()


class SpreadAll(Spread):
    def __init__(self, copies, locals_, shards, source, target, width):
        self.width = width
        self.whole = source
        self.local_all = locals_
        rep = copies.rep
        super().__init__(
            copies,
            None,
            shards,
            source.at[:, self.columns(rep)],
            target,
            lambda shard: target.at[shard, :, self.columns(rep)],
        )
        self.across = {}
        self.core = []

    def columns(self, rep):
        return pl.ds(pl.multiple_of(rep * self.width, self.width), self.width)

    def start(self):
        super().start()
        self.own = self.local_all.copy(self.whole, self.target.at[self.copies.place])

    def arrive(self, offset):
        super().arrive(offset)
        block = self.at(flipped(self.copies.place, offset))
        self.across[offset] = self.copies.send(block, block, 2, 0)
        self.core.append(self.copies.send(block, block, 1, 0))

    def cross(self, offset):
        copies = self.copies
        self.across[offset].wait_recv()
        shard = flipped(copies.place, offset)
        block = self.target.at[shard, :, self.columns(flipped(copies.rep, 2))]
        self.core.append(copies.send(block, block, 1, 0))

    def finish(self):
        for copy in self.core:
            copy.wait_recv()
        self.own.wait()


def row_loop(rows, step, body):
    @pl.loop(0, rows // step)
    def _(at):
        body(pl.ds(pl.multiple_of(at * step, step), step))


def normed(values, gain):
    return values * rms_scale(values) * gain


def shifted(values, by):
    rows = values.shape[0]
    at = lax.broadcasted_iota(jnp.int32, values.shape, 0)
    turned = pltpu.roll(values, by % rows, 0)
    kept = at >= by if by > 0 else at < rows + by
    return jnp.where(kept, turned, 0.0)


def mixer_columns(act, m_in, gains, at, width, features, slot):
    lanes = pl.ds(at, width)
    parts = []
    for base in (0, features, 2 * features):
        block = m_in[:, :, base + at : base + at + width].reshape(features, width)
        parts.append(dot(act, block))
    part_b, part_c, part_x = parts
    taps = [gains[2 + k : 3 + k, at : at + width] for k in range(3)]
    product = part_b * part_x
    convolved = []
    for start in range(0, act.shape[0], slot):
        rows = product[start : start + slot]
        convolved.append(
            taps[0] * shifted(rows, 2) + taps[1] * shifted(rows, 1) + taps[2] * rows
        )
    return part_b, part_c, part_x, product, jnp.concatenate(convolved)


def own_columns(rep, wide, target):
    half = target.shape[1] // 2
    shards = lax.axis_size("fsdp")
    cut = half // shards

    def lay(quarter):
        for at in range(shards):
            start = (4 * at + quarter) * cut
            for side in range(2):
                target[:, side * half + at * cut : side * half + (at + 1) * cut] = wide[
                    side, :, start : start + cut
                ]

    for quarter in range(4):
        pl.when(rep == quarter)(functools.partial(lay, quarter))


def forward_kernel(
    slot,
    lengths_ref, rows_ref, cot_ref, small_ref, in_ref, out_ref, gate_ref, up_ref, down_ref,
    all_in, all_out, all_units, all_down, all_act, all_cot, gains_ref,
    small_all, v_in, v_out, act_one, mixer_in, act_two, cot_live, wide, units_own, down_own,
    send_sems, recv_sems, local_sems,
):
    rows, features = rows_ref.shape
    shards = all_units.shape[0]
    copies = Copies(send_sems, recv_sems)
    local = Local(local_sems)
    far = list(range(2, shards, 2))
    copies.meet([(0, offset) for offset in [*far, 1]] + [(1, 0), (2, 0)])

    small = Spread(copies, local, shards, small_ref, small_all)
    w_in = SpreadAll(copies, local, shards, in_ref, v_in, in_ref.shape[1] // 4)
    w_out = SpreadAll(copies, local, shards, out_ref, v_out, out_ref.shape[1] // 4)
    units = Spread(copies, local, shards, units_own, all_units)
    down = Spread(copies, local, shards, down_own, all_down)

    small.start()
    w_in.start()
    w_out.start()
    loads = [local.copy(gate_ref, wide.at[0]), local.copy(up_ref, wide.at[1])]
    loads.append(local.copy(down_ref.at[copies.rep], down_own))

    slot_id = copies.rep * shards + copies.place
    for micro in range(rows // slot):
        length = lengths_ref[micro, slot_id]
        for start in range(0, slot, 64):
            held = slice(micro * slot + start, micro * slot + start + 64)
            at = start + lax.broadcasted_iota(jnp.int32, (64, features), 0)
            cot_live[held] = jnp.where(at < length, cot_ref[held].astype(F32), 0.0).astype(LOW)
    own_cot = local.copy(cot_live, all_cot.at[0])

    for load in loads:
        load.wait()
    own_columns(copies.rep, wide, units_own)
    for offset in far:
        small.arrive(offset)
    small.finish()
    gains_ref[...] = jnp.concatenate([small_all[at] for at in range(shards)], axis=1)
    gain_one = gains_ref[0:1]

    def first(at):
        act_one[at] = normed(rows_ref[at].astype(F32), gain_one).astype(LOW)

    w_in.arrive(far[0])
    w_in.arrive(1)
    row_loop(rows, 64, first)
    units.start()
    for offset in far[1:]:
        w_in.arrive(offset)
    for offset in far:
        w_in.arrive(offset + 1)
    w_out.arrive(1)
    for offset in far:
        w_out.arrive(offset)
    for offset in far:
        w_out.arrive(offset + 1)
    down.start()
    cot_core = copies.send(cot_live, all_cot.at[1], 1, 0)
    cot_across = copies.send(cot_live, all_cot.at[2], 2, 0)
    order = [1, *far, *[offset + 1 for offset in far]]
    for offset in order:
        w_in.cross(offset)
    for offset in far:
        units.arrive(offset)
    for offset in order:
        w_out.cross(offset)
    w_in.finish()

    width = features // 4
    for part in range(4):
        at = part * width
        _, part_c, _, _, convolved = mixer_columns(
            act_one[...], v_in, gains_ref, at, width, features, slot
        )
        mixer_in[:, at : at + width] = (part_c * convolved).astype(LOW)
    keep_in = local.copy(v_in, all_in)
    w_out.finish()
    keep_out = local.copy(v_out, all_out)
    spread = []
    for start in range(0, rows, slot):
        held = slice(start, start + slot)
        hstate = rows_ref[held].astype(F32) + dot(
            mixer_in[held], v_out[...].reshape(features, features)
        )
        act_two[held] = normed(hstate, gains_ref[1:2]).astype(LOW)
        block = act_two.at[held]
        spread.append(
            (
                held,
                copies.send(block, all_act.at[2, held], 2, 0),
                copies.send(block, all_act.at[1, held], 1, 0),
                local.copy(block, all_act.at[0, held]),
            )
        )
    for offset in far:
        down.arrive(offset)
    cot_across.wait_recv()
    corner = [copies.send(all_cot.at[2], all_cot.at[3], 1, 0)]
    for held, across, _, _ in spread:
        across.wait_recv()
        corner.append(copies.send(all_act.at[2, held], all_act.at[3, held], 1, 0))
    units.finish()
    down.finish()
    cot_core.wait_recv()
    for _, _, core, own in spread:
        core.wait_recv()
        own.wait()
    for copy in corner:
        copy.wait_recv()
    own_cot.wait()
    keep_in.wait()
    keep_out.wait()
    copies.close()


def run_forward(lengths, rows, cot, small, w_in, w_out, w_gate, w_up, w_down, slot):
    shards = lax.axis_size("fsdp")
    count, features = rows.shape
    part = w_in.shape[0]
    down = w_down.shape[1:]
    units = (part, 2 * shards * down[0])
    shapes = [
        (shards, *w_in.shape),
        (shards, *w_out.shape),
        (shards, *units),
        (shards, *down),
        (4, count, features),
        (4, count, features),
    ]
    hbm = pl.BlockSpec(memory_space=pltpu.HBM)
    vmem = pl.BlockSpec(memory_space=pltpu.VMEM)
    smem = pl.BlockSpec(memory_space=pltpu.SMEM)
    hops = 12 * shards + 16
    return pl.pallas_call(
        functools.partial(forward_kernel, slot),
        out_shape=[jax.ShapeDtypeStruct(shape, LOW) for shape in shapes]
        + [jax.ShapeDtypeStruct((8, features), F32)],
        in_specs=[smem, vmem, vmem, vmem, hbm, hbm, hbm, hbm, hbm],
        out_specs=[hbm] * 6 + [vmem],
        scratch_shapes=[
            pltpu.VMEM((shards, 8, part), F32),
            pltpu.VMEM((shards, *w_in.shape), LOW),
            pltpu.VMEM((shards, *w_out.shape), LOW),
            pltpu.VMEM((count, features), LOW),
            pltpu.VMEM((count, features), LOW),
            pltpu.VMEM((count, features), LOW),
            pltpu.VMEM((count, features), LOW),
            pltpu.VMEM((2, *w_gate.shape), LOW),
            pltpu.VMEM(units, LOW),
            pltpu.VMEM(down, LOW),
            pltpu.SemaphoreType.DMA((hops,)),
            pltpu.SemaphoreType.DMA((hops,)),
            pltpu.SemaphoreType.DMA((24,)),
        ],
        compiler_params=pltpu.CompilerParams(
            collective_id=0, has_side_effects=True, vmem_limit_bytes=56 << 20
        ),
        name="forward",
    )(lengths, rows, cot, small, w_in, w_out, w_gate, w_up, w_down)


def add_into(target, *others):
    rows = target.shape[-2]
    step = next((size for size in (64, 48, 16) if rows % size == 0), rows)
    kind = target.dtype if len(others) == 1 else F32

    @pl.loop(0, rows // step)
    def _(at):
        held = pl.ds(pl.multiple_of(at * step, step), step)
        total = target[held].astype(kind)
        for other in others:
            total = total + other[held].astype(kind)
        target[held] = total.astype(target.dtype)


class Collect:
    def __init__(self, copies, shards, sent_at, own_at, near_in, far_in):
        self.copies = copies
        self.sent_at, self.own_at = sent_at, own_at
        self.near_in, self.far_in = near_in, far_in
        self.order = [*range(4, shards, 2), 2, 0]
        self.arriving = {}
        self.far = {}

    def near(self, offset):
        copies = self.copies
        self.arriving[offset] = copies.send(
            lambda: self.sent_at(offset + 1), lambda: self.near_in.at[offset // 2], 0, 1
        )

    def near_all(self):
        for offset in self.order:
            self.near(offset)

    def combine(self, offset):
        self.arriving[offset].wait_recv()
        own = self.own_at(offset)
        add_into(own, self.near_in.at[offset // 2])
        if offset:
            self.far[offset] = self.copies.send(
                lambda: self.own_at(offset), lambda: self.far_in.at[offset // 2 - 1], 0, offset
            )

    def combine_all(self):
        for offset in self.order:
            self.combine(offset)

    def total(self):
        for copy in self.far.values():
            copy.wait_recv()
        own = self.own_at(0)
        add_into(own, *[self.far_in.at[k] for k in range(len(self.far))])
        return own


class Share:
    def __init__(self, copies, local, source, target_at):
        self.copies = copies
        self.target_at = target_at
        here = target_at(copies.rep)
        self.across = copies.send(source, here, 2, 0)
        self.core = [copies.send(source, here, 1, 0)]
        self.own = local.copy(source, here)

    def forward(self):
        self.across.wait_recv()
        block = self.target_at(flipped(self.copies.rep, 2))
        self.core.append(self.copies.send(block, block, 1, 0))

    def finish(self):
        for copy in self.core:
            copy.wait_recv()
        self.own.wait()


class CollectAll:
    def __init__(self, copies, shards, width, parts, core_in, cross_in, near_in, far_in):
        self.copies = copies
        self.width = width
        self.parts, self.core_in, self.cross_in = parts, core_in, cross_in
        place = copies.place
        self.collect = Collect(
            copies,
            shards,
            lambda offset: parts.at[0, flipped(place, offset)],
            lambda offset: parts.at[0, flipped(place, offset)],
            near_in,
            far_in,
        )
        self.core = {}
        self.cross = {}
        self.order = [o + 1 for o in self.collect.order] + self.collect.order

    def compute(self, turn, left, right):
        rep = flipped(self.copies.rep, turn)
        shards, rows, _ = self.parts.shape[1:]
        for at in range(0, self.width, 256):
            columns = pl.ds(pl.multiple_of(rep * self.width + at, 256), 256)
            block = dot_first(left[...], right[:, columns]).astype(LOW)
            self.parts[turn, :, :, at : at + 256] = block.reshape(shards, rows, 256)

    def to_core(self, turn):
        self.core[turn - 1] = self.copies.send(
            lambda: self.parts.at[turn], lambda: self.core_in.at[turn // 2], 1, 0
        )

    def to_cross(self):
        self.core[2].wait_recv()
        place = self.copies.place
        for offset in self.order:
            block = self.parts.at[2, flipped(place, offset)]
            add_into(block, self.core_in.at[1, flipped(place, offset)])
            self.cross_one(offset)
        self.core[0].wait_recv()

    def cross_one(self, offset):
        place = self.copies.place
        self.cross[offset] = self.copies.send(
            lambda: self.parts.at[2, flipped(place, offset)],
            lambda: self.cross_in.at[flipped(place, offset)],
            2,
            0,
        )

    def arrive(self, offset):
        self.cross[offset].wait_recv()
        shard = flipped(self.copies.place, offset)
        add_into(self.parts.at[0, shard], self.core_in.at[0, shard], self.cross_in.at[shard])

    def near_all(self):
        for offset in self.collect.order:
            self.arrive(offset + 1)
            self.collect.near(offset)

    def combine_all(self):
        for offset in self.collect.order:
            self.arrive(offset)
            self.collect.combine(offset)


def feed_forward_rows(act, cot, units, down, hidden, d_units, width):
    act_rows, cot_rows = act[...], cot[...]
    step = 256

    def columns(at, size):
        lanes, up_lanes = pl.ds(at, size), pl.ds(width + at, size)
        gate_pre = dot(act_rows, units[:, lanes])
        up_pre = dot(act_rows, units[:, up_lanes])
        d_hidden = dot_last(cot_rows, down[lanes])
        sigmoid_g = jax.nn.sigmoid(gate_pre)
        silu_g = gate_pre * sigmoid_g
        hidden[:, lanes] = (silu_g * up_pre).astype(LOW)
        d_units[:, lanes] = (
            d_hidden * up_pre * sigmoid_g * (1.0 + gate_pre * (1.0 - sigmoid_g))
        ).astype(LOW)
        d_units[:, up_lanes] = (d_hidden * silu_g).astype(LOW)

    @pl.loop(0, width // step)
    def _(at):
        columns(pl.multiple_of(at * step, 128), step)

    if width % step:
        columns(width - width % step, width % step)


def put_shards(target, columns, block):
    shards, rows = target.shape[:2]
    if rows % 16 == 0:
        target[:, :, columns] = block.reshape(shards, rows, block.shape[1])
    else:
        for shard in range(shards):
            target[shard, :, columns] = block[shard * rows : (shard + 1) * rows]


def backward_kernel(
    slot,
    all_rows_ref, gains_ref, in_ref, out_ref, units_ref, down_ref, act_ref, cot_ref,
    outputs_ref, d_rows_ref, down_sum, units_sum, in_sum, out_sum, small_sum, ffn_in,
    d_act, d_core, d_cross, down_grad, down_near, down_far, units_grad, units_near, units_far,
    w_out_core, w_out_cross, w_out_near, w_out_far,
    w_in_core, w_in_cross, w_in_near, w_in_far,
    small, small_in, send_sems, recv_sems, local_sems,
):
    rows, features = all_rows_ref.shape
    shards = units_grad.shape[0]
    units_width = down_ref.shape[0]
    copies = Copies(send_sems, recv_sems)
    local = Local(local_sems)
    place = copies.place
    far = list(range(2, shards, 2))
    bits = [1 << k for k in range(1, shards.bit_length() - 1)]
    copies.meet([(0, offset) for offset in [*far, 1]] + [(1, 0), (2, 0)])

    def collector(grad, near, far_in):
        at = lambda offset: grad.at[flipped(place, offset)]
        return Collect(copies, shards, at, at, near, far_in)

    down = collector(down_grad, down_near, down_far)
    units = collector(units_grad, units_near, units_far)
    d_near, d_far, ffn_near = {}, [], {}

    def feed_forward(m_units, m_down, act, cot, hidden, d_units):
        part = lambda ref, turn: ref.at[turn * rows : (turn + 1) * rows]
        loads = {"units": local.copy(units_ref, m_units)}
        for turn in (3, 2, 1, 0):
            loads[turn] = [
                local.copy(act_ref.at[turn], part(act, turn)),
                local.copy(cot_ref.at[turn], part(cot, turn)),
            ]
            if turn == 3:
                loads["down"] = local.copy(down_ref, m_down)

        def units_of(turn):
            for load in loads[turn]:
                load.wait()
            if turn == 3:
                loads["units"].wait()
                loads["down"].wait()
            feed_forward_rows(
                part(act, turn), part(cot, turn), m_units, m_down,
                part(hidden, turn), part(d_units, turn), units_width,
            )

        def d_act_of(turn):
            block = part(d_units, turn)
            d_act[turn] = dot_last(block[...], m_units[...]).astype(LOW)
            if turn % 2:
                d_near[turn] = copies.send(
                    lambda: d_act.at[turn], lambda: d_core.at[turn // 2], 1, 0
                )

        def send_across(held):
            return copies.send(lambda: d_act.at[2, held], lambda: d_cross.at[held], 2, 0)

        def ffn_of(turn):
            block = part(hidden, turn)
            block[:, :features] = dot(block[...], m_down[...]).astype(LOW)
            if turn % 2:
                ffn_near[turn] = copies.send(
                    lambda: part(hidden, turn).at[:, :features],
                    lambda: ffn_in.at[turn // 2],
                    1,
                    0,
                )

        per = 256 * shards // features

        def units_grad_of(chunk):
            base = flipped(place // per, chunk) * per
            lanes = pl.ds(pl.multiple_of(base * (features // shards), 256), 256)
            block = dot_first(act[:, lanes], d_units[...]).astype(LOW)
            units_grad[pl.ds(base, per)] = block.reshape(per, -1, block.shape[1])
            for offset in units.order:
                if offset // per == chunk:
                    units.near(offset)

        for turn in (3, 2):
            units_of(turn)
            d_act_of(turn)
        d_near[3].wait_recv()
        for start in range(0, rows, slot):
            held = slice(start, start + slot)
            add_into(d_act.at[2, held], d_core.at[1, held])
            d_far.append(send_across(held))
        for turn in (1, 0):
            units_of(turn)
        for at in range(0, features, 256):
            lanes = slice(at, at + 256)
            put_shards(down_grad, lanes, dot_first(hidden[...], cot[:, lanes]).astype(LOW))
        down.near_all()
        ffn_of(3)
        ffn_of(2)
        chunks = [*range(2, features // 256), 1, 0]
        units_grad_of(chunks[0])

        copies.sent(d_near[3])
        ffn_near[3].wait_recv()
        load = local.copy(ffn_in.at[1], d_act.at[3])
        units_grad_of(chunks[1])
        load.wait()
        add_into(d_act.at[3], part(hidden, 2).at[:, :features])
        across = copies.send(lambda: d_act.at[3], lambda: ffn_in.at[2], 2, 0)
        ffn_near[2] = across
        for chunk in chunks[2:]:
            units_grad_of(chunk)
        d_act_of(1)
        d_act_of(0)
        ffn_of(1)
        copies.sent(d_near[1])
        d_act[1] = dot(part(hidden, 0)[...], m_down[...]).astype(LOW)
        down.combine_all()
        copies.sent(ffn_near[3])
        copies.sent(ffn_near[1])

    pl.run_scoped(
        feed_forward,
        pltpu.VMEM(units_ref.shape, LOW),
        pltpu.VMEM(down_ref.shape, LOW),
        pltpu.VMEM((4 * rows, features), LOW),
        pltpu.VMEM((4 * rows, features), LOW),
        pltpu.VMEM((4 * rows, units_width), LOW),
        pltpu.VMEM((4 * rows, 2 * units_width), LOW),
    )

    def mixer(
        rows_ref, v_in, v_out, act_one, mixer_in, hstate, d_hstate, d_mixer, d_proj, w_out_parts
    ):
        load_rows = local.copy(all_rows_ref, rows_ref)
        load_in = local.copy(in_ref, v_in)
        load_out = local.copy(out_ref, v_out)
        gain_one, gain_two = gains_ref[0:1], gains_ref[1:2]

        load_cot = local.copy(cot_ref.at[0], d_mixer)

        def first(at):
            act_one[at] = normed(rows_ref[at].astype(F32), gain_one).astype(LOW)

        load_rows.wait()
        row_loop(rows, 64, first)
        load_in.wait()
        width = features // 4
        w_out = CollectAll(
            copies, shards, width, w_out_parts, w_out_core, w_out_cross, w_out_near, w_out_far
        )

        def columns_back(part_b, part_c, part_x):
            for part in range(4):
                at = part * width
                lanes = slice(at, at + width)
                b_now, c_now, x_now, _, convolved = mixer_columns(
                    act_one[...], v_in, gains_ref, at, width, features, slot
                )
                part_b[:, lanes] = b_now
                part_c[:, lanes] = c_now
                part_x[:, lanes] = x_now
                mixer_in[:, lanes] = (c_now * convolved).astype(LOW)
            load_out.wait()
            for start in range(0, rows, slot):
                held = slice(start, start + slot)
                hstate[held] = rows_ref[held].astype(F32) + dot(
                    mixer_in[held], v_out[...].reshape(features, features)
                )

            units.combine(units.order[0])

            d_near[1].wait_recv()
            small[0] = jnp.zeros((8, features), F32)

            def second(at):
                d_now = (
                    d_act[0, at].astype(F32) + d_core[0, at].astype(F32) + d_cross[at].astype(F32)
                )
                values = hstate[at]
                scale = rms_scale(values)
                small[0, 1:2] += jnp.sum(d_now * values * scale, axis=0, keepdims=True)
                d_values = d_mixer[at].astype(F32) + norm_back(d_now, values, scale, gain_two)
                d_hstate[at] = d_values
                d_mixer[at] = d_values.astype(LOW)

            for copy in d_far:
                copy.wait_recv()
            load_cot.wait()
            row_loop(rows, 64, second)

            for turn in (3, 1):
                w_out.compute(turn, mixer_in, d_mixer)
                w_out.to_core(turn)
            for turn in (2, 0):
                w_out.compute(turn, mixer_in, d_mixer)

            per = shards * width // features
            for part in range(4):
                at = part * width
                lanes = slice(at, at + width)
                block = v_out[part * per : (part + 1) * per].reshape(width, features)
                d_mixin = dot_last(d_mixer[...], block)
                taps = [gains_ref[2 + k : 3 + k, lanes] for k in range(3)]
                for start in range(0, rows, slot):
                    held = slice(start, start + slot)
                    d_mix = d_mixin[held]
                    b_now, c_now, x_now = part_b[held, lanes], part_c[held, lanes], part_x[held, lanes]
                    product = b_now * x_now
                    before = [shifted(product, 2), shifted(product, 1), product]
                    convolved = taps[0] * before[0] + taps[1] * before[1] + taps[2] * before[2]
                    d_conv = d_mix * c_now
                    for k in range(3):
                        small[0, 2 + k : 3 + k, lanes] += jnp.sum(
                            d_conv * before[k], axis=0, keepdims=True
                        )
                    d_product = (
                        taps[2] * d_conv
                        + taps[1] * shifted(d_conv, -1)
                        + taps[0] * shifted(d_conv, -2)
                    )
                    d_proj[held, lanes] = (d_product * x_now).astype(LOW)
                    d_proj[held, features + at : features + at + width] = (d_mix * convolved).astype(LOW)
                    d_proj[held, 2 * features + at : 2 * features + at + width] = (
                        d_product * b_now
                    ).astype(LOW)
                if part == 0:
                    w_out.to_cross()
                if part == 2:
                    units.combine(units.order[1])

        pl.run_scoped(columns_back, *[pltpu.VMEM((rows, features), F32)] * 3)

        def finish(w_in_parts):
            w_in = CollectAll(
                copies, shards, 3 * width, w_in_parts, w_in_core, w_in_cross, w_in_near, w_in_far
            )
            for turn in (3, 1):
                w_in.compute(turn, act_one, d_proj)
                w_in.to_core(turn)
            for turn in (2, 0):
                w_in.compute(turn, act_one, d_proj)
            w_in.to_cross()
            units.combine(units.order[2])

            def rows_back(start):
                held = slice(start, start + slot)
                d_now = dot_last(d_proj[held], v_in[...].reshape(features, 3 * features))
                values = rows_ref[held].astype(F32)
                scale = rms_scale(values)
                small[0, 0:1] += jnp.sum(d_now * values * scale, axis=0, keepdims=True)
                d_hstate[held] += norm_back(d_now, values, scale, gain_one)

            hops = [(0, 1), *[(0, bit) for bit in bits], (1, 0), (2, 0)]
            flight, summed = [], []

            def small_hop():
                step = len(flight)
                if len(summed) < step:
                    flight[-1].wait_recv()
                    small[step] = small[step - 1] + small_in[step - 1]
                    summed.append(step)
                if step < len(hops):
                    flight.append(copies.send(small.at[step], small_in.at[step], *hops[step]))

            def columns(target, width):
                return lambda at: target.at[:, pl.ds(pl.multiple_of(at * width, width), width)]

            starts = list(range(0, rows, slot))
            for start in starts[:-1]:
                rows_back(start)
            w_out.near_all()
            rows_back(starts[-1])
            d_out = local.copy(d_hstate, d_rows_ref)
            small_hop()
            down_share = Share(copies, local, down.total(), lambda at: down_sum.at[at])

            ffn_near[1].wait_recv()
            ffn_near[2].wait_recv()
            for copy in d_far:
                copies.sent(copy)
            loads = [
                local.copy(ffn_in.at[0], d_act.at[0]),
                local.copy(ffn_in.at[2], d_act.at[2]),
            ]
            for load in loads:
                load.wait()
            small_hop()
            add_into(hstate, d_act.at[1], d_act.at[0], d_act.at[2])
            put_out = local.copy(hstate, outputs_ref)
            small_hop()
            for offset in units.order[3:]:
                units.combine(offset)
            w_out.combine_all()
            small_hop()
            for offset in w_in.collect.order:
                w_in.arrive(offset + 1)
                w_in.collect.near(offset)
            small_hop()
            down_share.forward()
            units_share = Share(copies, local, units.total(), lambda at: units_sum.at[at])
            out_share = Share(copies, local, w_out.collect.total(), columns(out_sum, width))
            small_hop()
            w_in.combine_all()
            while len(summed) < len(hops):
                small_hop()
            small_sum[...] = small[len(hops)]
            units_share.forward()
            out_share.forward()
            in_share = Share(copies, local, w_in.collect.total(), columns(in_sum, 3 * width))
            in_share.forward()
            for share in (down_share, units_share, out_share, in_share):
                share.finish()
            put_out.wait()
            d_out.wait()
            copies.close()

        pl.run_scoped(finish, pltpu.VMEM((4, shards, part_rows, 3 * width), LOW))

    whole = (rows, features)
    part_rows = in_ref.shape[1]
    pl.run_scoped(
        mixer,
        pltpu.VMEM(whole, LOW),
        pltpu.VMEM(in_ref.shape, LOW),
        pltpu.VMEM(out_ref.shape, LOW),
        pltpu.VMEM(whole, LOW),
        pltpu.VMEM(whole, LOW),
        pltpu.VMEM(whole, F32),
        pltpu.VMEM(whole, F32),
        pltpu.VMEM(whole, LOW),
        pltpu.VMEM((rows, 3 * features), LOW),
        pltpu.VMEM((4, shards, part_rows, features // 4), LOW),
    )


def run_backward(rows, gains, m_in, m_out, m_units, m_down, act, cot, slot):
    count, features = rows.shape
    shards, part = m_in.shape[:2]
    cut = m_down.shape[0] // shards
    units = m_units.shape[1]
    half = shards // 2
    hbm = pl.BlockSpec(memory_space=pltpu.HBM)
    vmem = pl.BlockSpec(memory_space=pltpu.VMEM)
    hops = 10 * shards + 40
    depth = shards.bit_length() + 1

    def blocks(*shape):
        return [
            pltpu.VMEM((half, *shape), LOW),
            pltpu.VMEM((max(half - 1, 1), *shape), LOW),
        ]

    def quarters(width):
        return [
            pltpu.VMEM((2, shards, part, width), LOW),
            pltpu.VMEM((shards, part, width), LOW),
            *blocks(part, width),
        ]

    whole = (count, features)
    return pl.pallas_call(
        functools.partial(backward_kernel, slot),
        out_shape=[
            jax.ShapeDtypeStruct(*shape)
            for shape in (
                (whole, F32),
                (whole, F32),
                ((4, cut, features), LOW),
                ((4, part, units), LOW),
                ((part, 3 * features), LOW),
                ((part, features), LOW),
                ((8, features), F32),
                ((3, *whole), LOW),
            )
        ],
        in_specs=[hbm, vmem] + [hbm] * 6,
        out_specs=[hbm] * 6 + [vmem, hbm],
        scratch_shapes=[
            pltpu.VMEM((4, *whole), LOW),
            pltpu.VMEM((2, *whole), LOW),
            pltpu.VMEM(whole, LOW),
            pltpu.VMEM((shards, cut, features), LOW),
            *blocks(cut, features),
            pltpu.VMEM((shards, part, units), LOW),
            *blocks(part, units),
            *quarters(features // 4),
            *quarters(3 * features // 4),
            pltpu.VMEM((depth + 1, 8, features), F32),
            pltpu.VMEM((depth, 8, features), F32),
            pltpu.SemaphoreType.DMA((hops,)),
            pltpu.SemaphoreType.DMA((hops,)),
            pltpu.SemaphoreType.DMA((48,)),
        ],
        compiler_params=pltpu.CompilerParams(
            collective_id=1, has_side_effects=True, vmem_limit_bytes=127 << 19
        ),
        name="backward",
    )(rows, gains, m_in, m_out, m_units, m_down, act, cot)


def finish_kernel(
    cut, units_ref, down_ref, in_ref, out_ref, rows_ref, d_rows_ref,
    gate_out, up_out, down_out, in_out, out_out, rows_out, d_rows_out,
):
    half = units_ref.shape[2] // 2
    for side, target in enumerate((gate_out, up_out)):
        for at in range(half // cut):
            for quarter in range(4):
                start = (4 * at + quarter) * cut
                target[:, start : start + cut] = units_ref[
                    quarter, :, side * half + at * cut : side * half + (at + 1) * cut
                ].astype(F32)
    down_out[...] = down_ref[...].astype(F32)
    in_out[...] = in_ref[...].astype(F32)
    out_out[...] = out_ref[...].astype(F32)
    rows_out[...] = rows_ref[...]
    d_rows_out[...] = d_rows_ref[...]


def run_finish(units, down, w_in, w_out, outputs, d_rows):
    part, columns = units.shape[1:]
    cut, features = down.shape[1:]
    down = down.reshape(4 * cut, features)
    steps = 4 if part % 64 == 0 and cut % 16 == 0 else 1

    def rows(array):
        return pl.BlockSpec((array.shape[0] // steps, array.shape[1]), lambda at: (at, 0))

    wide = jax.ShapeDtypeStruct((part, 2 * columns), F32)
    narrow = (down, w_in, w_out, outputs, d_rows)
    outs = [wide, wide, *[jax.ShapeDtypeStruct(array.shape, F32) for array in narrow]]
    return pl.pallas_call(
        functools.partial(finish_kernel, cut),
        grid=(steps,),
        out_shape=outs,
        in_specs=[
            pl.BlockSpec((4, part // steps, columns), lambda at: (0, at, 0)),
            *[rows(array) for array in narrow],
        ],
        out_specs=[rows(out) for out in outs],
        compiler_params=pltpu.CompilerParams(vmem_limit_bytes=62 << 20),
        name="finish",
    )(units, *narrow)


def on_device(
    inputs, cotangent, lengths, norm_one, w_in, conv_w, w_out, norm_two, w_gate, w_up, w_down
):
    micro_count, tok_rows, features = inputs.shape
    shards = lax.axis_size("fsdp")
    place = lax.axis_index("fsdp")
    all_rows = micro_count * tok_rows
    cut = w_down.shape[0] // 4
    part = w_in.shape[0]
    part_ff = shards * cut

    small = jnp.concatenate([norm_one[None], norm_two[None], conv_w, jnp.zeros_like(conv_w)])
    rows_low = inputs.reshape(all_rows, features)
    m_in, m_out, m_units, m_down, act_all, cot_all, gains = run_forward(
        lengths, rows_low, cotangent.reshape(all_rows, features), small.astype(F32),
        w_in, w_out, w_gate, w_up, w_down.reshape(4, cut, features), tok_rows,
    )

    outputs, d_rows, down_sum, units_sum, in_sum, out_sum, small_sum, _ = run_backward(
        rows_low, gains, m_in, m_out, m_units.reshape(features, 2 * part_ff),
        m_down.reshape(part_ff, features), act_all, cot_all, tok_rows,
    )
    d_gate, d_up, d_down, d_in, d_out, outputs, d_rows = run_finish(
        units_sum, down_sum, in_sum, out_sum, outputs, d_rows
    )
    small_own = lax.dynamic_slice_in_dim(small_sum, place * part, part, 1)
    return (
        outputs.reshape(inputs.shape),
        d_rows.reshape(inputs.shape),
        small_own[0],
        d_in,
        small_own[2:5],
        d_out,
        small_own[1],
        d_gate,
        d_up,
        d_down,
    )


def solution(mesh):
    return jax.shard_map(
        on_device,
        mesh=mesh,
        in_specs=(
            P(None, ("rep", "fsdp"), None),
            P(None, ("rep", "fsdp"), None),
            P(),
            P("fsdp"),
            P("fsdp", None),
            P(None, "fsdp"),
            P("fsdp", None),
            P("fsdp"),
            P("fsdp", None),
            P("fsdp", None),
            P("fsdp", None),
        ),
        out_specs=(
            P(None, ("rep", "fsdp"), None),
            P(None, ("rep", "fsdp"), None),
            P("fsdp"),
            P("fsdp", None),
            P(None, "fsdp"),
            P("fsdp", None),
            P("fsdp"),
            P("fsdp", None),
            P("fsdp", None),
            P("fsdp", None),
        ),
        check_vma=False,
    )
```

```python
import functools

import jax
import jax.numpy as jnp
from jax import lax
from jax.experimental import pallas as pl
from jax.experimental.pallas import tpu as pltpu
from jax.sharding import PartitionSpec as P

EPSILON = 1e-05
LOW = jnp.bfloat16
F32 = jnp.float32
MESH = pl.DeviceIdType.MESH


def rms_scale(values):
    return lax.rsqrt(jnp.mean(values * values, axis=-1, keepdims=True) + EPSILON)


def dot(left, right):
    return jnp.dot(left, right, preferred_element_type=F32)


def dot_last(left, right):
    return lax.dot_general(left, right, (((1,), (1,)), ((), ())), preferred_element_type=F32)


def dot_first(left, right):
    return lax.dot_general(left, right, (((0,), (0,)), ((), ())), preferred_element_type=F32)


def norm_back(d_act, values, scale, gain):
    scaled = d_act * gain
    return scale * (
        scaled - values * scale * scale * jnp.mean(scaled * values, axis=-1, keepdims=True)
    )


def flipped(index, offset):
    bit = 1
    while bit <= offset:
        if offset & bit:
            index = index + bit - 2 * bit * ((index // bit) % 2)
        bit *= 2
    return index


class Copy:
    def __init__(self, copies, at, source, target, bits):
        self.copies, self.at, self.bits = copies, at, bits
        self.source, self.target = source, target

    def made(self):
        return pltpu.make_async_remote_copy(
            src_ref=self.source() if callable(self.source) else self.source,
            dst_ref=self.target() if callable(self.target) else self.target,
            send_sem=self.copies.sems[0].at[self.at],
            recv_sem=self.copies.sems[1].at[self.at],
            device_id=self.copies.peer(*self.bits),
            device_id_type=MESH,
        )

    def start(self):
        if self.only is None:
            self.made().start()
        else:
            pl.when(self.only)(lambda: self.made().start())

    def wait_recv(self):
        self.made().wait_recv()

    def wait_send(self):
        if self.only is None:
            self.made().wait_send()
        else:
            pl.when(self.only)(lambda: self.made().wait_send())


class Copies:
    def __init__(self, send_sems, recv_sems):
        self.sems = send_sems, recv_sems
        self.rep = lax.axis_index("rep")
        self.place = lax.axis_index("fsdp")
        self.started = []
        self.done = []
        self.relays = lax.axis_size("fsdp") == 8
        inner = ((self.place // 2 + 1) // 2) % 2
        self.inner, self.outer = inner == 1, inner == 0

    def peer(self, rep_bits, place_bits):
        return (flipped(self.rep, rep_bits), flipped(self.place, place_bits))

    def meet(self, peers):
        barrier = pltpu.get_barrier_semaphore()
        for bits in peers:
            pl.semaphore_signal(barrier, inc=1, device_id=self.peer(*bits), device_id_type=MESH)
        pl.semaphore_wait(barrier, len(peers))

    def send(self, source, target, rep_bits, place_bits):
        copy = self.plan(source, target, rep_bits, place_bits, None)
        copy.start()
        return copy

    def plan(self, source, target, rep_bits, place_bits, only):
        copy = Copy(self, len(self.started), source, target, (rep_bits, place_bits))
        copy.only = only
        self.started.append(copy)
        return copy

    def sent(self, copy):
        copy.wait_send()
        copy.source = copy.target
        self.done.append(copy)

    def close(self):
        for copy in self.started:
            if not any(copy is other for other in self.done):
                copy.wait_send()


class Local:
    def __init__(self, sems):
        self.sems = sems
        self.started = []

    def copy(self, source, target):
        copy = pltpu.make_async_copy(source, target, self.sems.at[len(self.started)])
        copy.start()
        self.started.append(copy)
        return copy


class Spread:
    def __init__(self, copies, locals_, shards, source, target, at=None):
        self.copies = copies
        self.target = target
        self.at = at if at is not None else (lambda shard: target.at[shard])
        self.source = source
        self.locals = locals_
        self.far = list(range(2, shards, 2))
        self.near = [1] + [offset + 1 for offset in self.far]

    def start(self):
        copies = self.copies
        here = self.at(copies.place)
        self.arriving = {}
        for offset in self.far:
            only = copies.inner if copies.relays and offset == 6 else None
            self.arriving[offset] = copies.plan(self.source, here, 0, offset, only)
            self.arriving[offset].start()
        self.arriving[1] = copies.send(self.source, here, 0, 1)
        if copies.relays:
            block = lambda: self.at(flipped(copies.place, 4))
            self.relay = copies.plan(block, block, 0, 2, copies.inner)
        if self.locals is not None:
            self.own = self.locals.copy(self.source, here)

    def arrive(self, offset):
        copies = self.copies
        if copies.relays and offset == 6:
            pl.when(copies.inner)(lambda: self.arriving[6].wait_recv())
            pl.when(copies.outer)(lambda: self.relay.wait_recv())
        else:
            self.arriving[offset].wait_recv()
        if copies.relays and offset == 4:
            self.relay.start()
        if offset % 2 == 0:
            block = self.at(flipped(copies.place, offset))
            self.arriving[offset + 1] = copies.send(block, block, 0, 1)

    def finish(self):
        for offset in self.near:
            self.arriving[offset].wait_recv()
        if self.locals is not None:
            self.own.wait()


class SpreadAll(Spread):
    def __init__(self, copies, locals_, shards, source, target, width):
        self.width = width
        self.whole = source
        self.local_all = locals_
        rep = copies.rep
        super().__init__(
            copies,
            None,
            shards,
            source.at[:, self.columns(rep)],
            target,
            lambda shard: target.at[shard, :, self.columns(rep)],
        )
        self.across = {}
        self.core = []

    def columns(self, rep):
        return pl.ds(pl.multiple_of(rep * self.width, self.width), self.width)

    def start(self):
        super().start()
        self.own = self.local_all.copy(self.whole, self.target.at[self.copies.place])

    def arrive(self, offset):
        super().arrive(offset)
        block = self.at(flipped(self.copies.place, offset))
        self.across[offset] = self.copies.send(block, block, 2, 0)
        self.core.append(self.copies.send(block, block, 1, 0))

    def cross(self, offset):
        copies = self.copies
        self.across[offset].wait_recv()
        shard = flipped(copies.place, offset)
        block = self.target.at[shard, :, self.columns(flipped(copies.rep, 2))]
        self.core.append(copies.send(block, block, 1, 0))

    def finish(self):
        for copy in self.core:
            copy.wait_recv()
        self.own.wait()


def row_loop(rows, step, body):
    @pl.loop(0, rows // step)
    def _(at):
        body(pl.ds(pl.multiple_of(at * step, step), step))


def normed(values, gain):
    return values * rms_scale(values) * gain


def shifted(values, by):
    rows = values.shape[0]
    at = lax.broadcasted_iota(jnp.int32, values.shape, 0)
    turned = pltpu.roll(values, by % rows, 0)
    kept = at >= by if by > 0 else at < rows + by
    return jnp.where(kept, turned, 0.0)


def mixer_columns(act, m_in, gains, at, width, features, slot):
    lanes = pl.ds(at, width)
    parts = []
    for base in (0, features, 2 * features):
        block = m_in[:, :, base + at : base + at + width].reshape(features, width)
        parts.append(dot(act, block))
    part_b, part_c, part_x = parts
    taps = [gains[2 + k : 3 + k, at : at + width] for k in range(3)]
    product = part_b * part_x
    convolved = []
    for start in range(0, act.shape[0], slot):
        rows = product[start : start + slot]
        convolved.append(
            taps[0] * shifted(rows, 2) + taps[1] * shifted(rows, 1) + taps[2] * rows
        )
    return part_b, part_c, part_x, product, jnp.concatenate(convolved)


def own_columns(rep, wide, target):
    half = target.shape[1] // 2
    shards = lax.axis_size("fsdp")
    cut = half // shards

    def lay(quarter):
        for at in range(shards):
            start = (4 * at + quarter) * cut
            for side in range(2):
                target[:, side * half + at * cut : side * half + (at + 1) * cut] = wide[
                    side, :, start : start + cut
                ]

    for quarter in range(4):
        pl.when(rep == quarter)(functools.partial(lay, quarter))


def forward_kernel(
    slot,
    lengths_ref, rows_ref, cot_ref, small_ref, in_ref, out_ref, gate_ref, up_ref, down_ref,
    all_in, all_out, all_units, all_down, all_act, all_cot, gains_ref,
    small_all, v_in, v_out, act_one, mixer_in, act_two, cot_live, wide, units_own, down_own,
    send_sems, recv_sems, local_sems,
):
    rows, features = rows_ref.shape
    shards = all_units.shape[0]
    copies = Copies(send_sems, recv_sems)
    local = Local(local_sems)
    far = list(range(2, shards, 2))
    copies.meet([(0, offset) for offset in [*far, 1]] + [(1, 0), (2, 0)])

    small = Spread(copies, local, shards, small_ref, small_all)
    w_in = SpreadAll(copies, local, shards, in_ref, v_in, in_ref.shape[1] // 4)
    w_out = SpreadAll(copies, local, shards, out_ref, v_out, out_ref.shape[1] // 4)
    units = Spread(copies, local, shards, units_own, all_units)
    down = Spread(copies, local, shards, down_own, all_down)

    small.start()
    w_in.start()
    w_out.start()
    loads = [local.copy(gate_ref, wide.at[0]), local.copy(up_ref, wide.at[1])]
    loads.append(local.copy(down_ref.at[copies.rep], down_own))

    slot_id = copies.rep * shards + copies.place
    for micro in range(rows // slot):
        length = lengths_ref[micro, slot_id]
        for start in range(0, slot, 64):
            held = slice(micro * slot + start, micro * slot + start + 64)
            at = start + lax.broadcasted_iota(jnp.int32, (64, features), 0)
            cot_live[held] = jnp.where(at < length, cot_ref[held].astype(F32), 0.0).astype(LOW)
    own_cot = local.copy(cot_live, all_cot.at[0])

    for load in loads:
        load.wait()
    own_columns(copies.rep, wide, units_own)
    for offset in far:
        small.arrive(offset)
    small.finish()
    gains_ref[...] = jnp.concatenate([small_all[at] for at in range(shards)], axis=1)
    gain_one = gains_ref[0:1]

    def first(at):
        act_one[at] = normed(rows_ref[at].astype(F32), gain_one).astype(LOW)

    w_in.arrive(1)
    w_in.arrive(far[0])
    row_loop(rows, 64, first)
    units.start()
    for offset in far[1:]:
        w_in.arrive(offset)
    for offset in far:
        w_in.arrive(offset + 1)
    w_out.arrive(1)
    for offset in far:
        w_out.arrive(offset)
    for offset in far:
        w_out.arrive(offset + 1)
    down.start()
    cot_core = copies.send(cot_live, all_cot.at[1], 1, 0)
    cot_across = copies.send(cot_live, all_cot.at[2], 2, 0)
    order = [1, *far, *[offset + 1 for offset in far]]
    for offset in order:
        w_in.cross(offset)
    for offset in far:
        units.arrive(offset)
    for offset in order:
        w_out.cross(offset)
    w_in.finish()

    width = features // 4
    for part in range(4):
        at = part * width
        _, part_c, _, _, convolved = mixer_columns(
            act_one[...], v_in, gains_ref, at, width, features, slot
        )
        mixer_in[:, at : at + width] = (part_c * convolved).astype(LOW)
    keep_in = local.copy(v_in, all_in)
    w_out.finish()
    keep_out = local.copy(v_out, all_out)
    spread = []
    for start in range(0, rows, slot):
        held = slice(start, start + slot)
        hstate = rows_ref[held].astype(F32) + dot(
            mixer_in[held], v_out[...].reshape(features, features)
        )
        act_two[held] = normed(hstate, gains_ref[1:2]).astype(LOW)
        block = act_two.at[held]
        spread.append(
            (
                held,
                copies.send(block, all_act.at[2, held], 2, 0),
                copies.send(block, all_act.at[1, held], 1, 0),
                local.copy(block, all_act.at[0, held]),
            )
        )
    for offset in far:
        down.arrive(offset)
    cot_across.wait_recv()
    corner = [copies.send(all_cot.at[2], all_cot.at[3], 1, 0)]
    for held, across, _, _ in spread:
        across.wait_recv()
        corner.append(copies.send(all_act.at[2, held], all_act.at[3, held], 1, 0))
    units.finish()
    down.finish()
    cot_core.wait_recv()
    for _, _, core, own in spread:
        core.wait_recv()
        own.wait()
    for copy in corner:
        copy.wait_recv()
    own_cot.wait()
    keep_in.wait()
    keep_out.wait()
    copies.close()


def run_forward(lengths, rows, cot, small, w_in, w_out, w_gate, w_up, w_down, slot):
    shards = lax.axis_size("fsdp")
    count, features = rows.shape
    part = w_in.shape[0]
    down = w_down.shape[1:]
    units = (part, 2 * shards * down[0])
    shapes = [
        (shards, *w_in.shape),
        (shards, *w_out.shape),
        (shards, *units),
        (shards, *down),
        (4, count, features),
        (4, count, features),
    ]
    hbm = pl.BlockSpec(memory_space=pltpu.HBM)
    vmem = pl.BlockSpec(memory_space=pltpu.VMEM)
    smem = pl.BlockSpec(memory_space=pltpu.SMEM)
    hops = 12 * shards + 24
    return pl.pallas_call(
        functools.partial(forward_kernel, slot),
        out_shape=[jax.ShapeDtypeStruct(shape, LOW) for shape in shapes]
        + [jax.ShapeDtypeStruct((8, features), F32)],
        in_specs=[smem, vmem, vmem, vmem, hbm, hbm, hbm, hbm, hbm],
        out_specs=[hbm] * 6 + [vmem],
        scratch_shapes=[
            pltpu.VMEM((shards, 8, part), F32),
            pltpu.VMEM((shards, *w_in.shape), LOW),
            pltpu.VMEM((shards, *w_out.shape), LOW),
            pltpu.VMEM((count, features), LOW),
            pltpu.VMEM((count, features), LOW),
            pltpu.VMEM((count, features), LOW),
            pltpu.VMEM((count, features), LOW),
            pltpu.VMEM((2, *w_gate.shape), LOW),
            pltpu.VMEM(units, LOW),
            pltpu.VMEM(down, LOW),
            pltpu.SemaphoreType.DMA((hops,)),
            pltpu.SemaphoreType.DMA((hops,)),
            pltpu.SemaphoreType.DMA((24,)),
        ],
        compiler_params=pltpu.CompilerParams(
            collective_id=0, has_side_effects=True, vmem_limit_bytes=56 << 20
        ),
        name="forward",
    )(lengths, rows, cot, small, w_in, w_out, w_gate, w_up, w_down)


def add_into(target, *others):
    rows = target.shape[-2]
    step = next((size for size in (64, 48, 16) if rows % size == 0), rows)
    kind = target.dtype if len(others) == 1 else F32

    @pl.loop(0, rows // step)
    def _(at):
        held = pl.ds(pl.multiple_of(at * step, step), step)
        total = target[held].astype(kind)
        for other in others:
            total = total + other[held].astype(kind)
        target[held] = total.astype(target.dtype)


class Collect:
    def __init__(self, copies, shards, sent_at, own_at, near_in, far_in):
        self.copies = copies
        self.sent_at, self.own_at = sent_at, own_at
        self.near_in, self.far_in = near_in, far_in
        self.order = list(range(shards - 2, -1, -2))
        self.arriving = {}
        self.far = {}

    def near(self, offset):
        copies = self.copies
        self.arriving[offset] = copies.send(
            lambda: self.sent_at(offset + 1), lambda: self.near_in.at[offset // 2], 0, 1
        )

    def near_all(self):
        for offset in self.order:
            self.near(offset)

    def combine(self, offset):
        copies = self.copies
        self.arriving[offset].wait_recv()
        own = self.own_at(offset)
        add_into(own, self.near_in.at[offset // 2])
        if not offset:
            return
        source = lambda: self.own_at(offset)
        target = lambda: self.far_in.at[offset // 2 - 1]
        if copies.relays and offset == 6:
            self.far[6] = copies.plan(source, target, 0, 6, copies.inner)
            self.relay = copies.plan(source, lambda: self.far_in.at[3], 0, 2, copies.outer)
            self.far[6].start()
            self.relay.start()
            return
        if copies.relays and offset == 4:

            @pl.when(copies.inner)
            def _():
                self.relay.wait_recv()
                add_into(self.own_at(4), self.far_in.at[3])

        self.far[offset] = copies.send(source, target, 0, offset)

    def combine_all(self):
        for offset in self.order:
            self.combine(offset)

    def total(self):
        copies = self.copies
        relayed = [6] if copies.relays else []
        for offset, copy in self.far.items():
            if offset not in relayed:
                copy.wait_recv()
        if not relayed:
            add_into(self.own_at(0), *[self.far_in.at[k] for k in range(len(self.far))])
            return self.own_at(0)

        @pl.when(copies.inner)
        def _():
            self.far[6].wait_recv()
            add_into(self.own_at(0), *[self.far_in.at[k] for k in range(3)])

        @pl.when(copies.outer)
        def _():
            add_into(self.own_at(0), *[self.far_in.at[k] for k in range(2)])

        return self.own_at(0)


class Share:
    def __init__(self, copies, local, collect, target_at):
        self.copies = copies
        self.target_at = target_at
        collect.total()
        source = lambda: collect.own_at(0)
        here = lambda: target_at(copies.rep)
        self.across = copies.send(source, here, 2, 0)
        self.core = [copies.send(source, here, 1, 0)]
        self.own = local.copy(source(), here())

    def settle(self):
        self.own.wait()
        self.own = None

    def forward(self):
        self.across.wait_recv()
        block = lambda: self.target_at(flipped(self.copies.rep, 2))
        self.core.append(self.copies.send(block, block, 1, 0))

    def finish(self):
        for copy in self.core:
            copy.wait_recv()
        if self.own is not None:
            self.own.wait()


class CollectAll:
    def __init__(self, copies, shards, width, parts, core_in, cross_in, near_in, far_in):
        self.copies = copies
        self.width = width
        self.parts, self.core_in, self.cross_in = parts, core_in, cross_in
        place = copies.place
        self.collect = Collect(
            copies,
            shards,
            lambda offset: parts.at[0, flipped(place, offset)],
            lambda offset: parts.at[0, flipped(place, offset)],
            near_in,
            far_in,
        )
        self.core = {}
        self.cross = {}
        self.order = [o + 1 for o in self.collect.order] + self.collect.order

    def compute(self, turn, left, right):
        rep = flipped(self.copies.rep, turn)
        shards, rows, _ = self.parts.shape[1:]
        for at in range(0, self.width, 256):
            columns = pl.ds(pl.multiple_of(rep * self.width + at, 256), 256)
            block = dot_first(left[...], right[:, columns]).astype(LOW)
            self.parts[turn, :, :, at : at + 256] = block.reshape(shards, rows, 256)

    def to_core(self, turn):
        self.core[turn - 1] = self.copies.send(
            lambda: self.parts.at[turn], lambda: self.core_in.at[turn // 2], 1, 0
        )

    def to_cross(self):
        self.core[2].wait_recv()
        place = self.copies.place
        for offset in self.order:
            block = self.parts.at[2, flipped(place, offset)]
            add_into(block, self.core_in.at[1, flipped(place, offset)])
            self.cross_one(offset)
        self.core[0].wait_recv()

    def cross_one(self, offset):
        place = self.copies.place
        self.cross[offset] = self.copies.send(
            lambda: self.parts.at[2, flipped(place, offset)],
            lambda: self.cross_in.at[flipped(place, offset)],
            2,
            0,
        )

    def arrive(self, offset):
        self.cross[offset].wait_recv()
        shard = flipped(self.copies.place, offset)
        add_into(self.parts.at[0, shard], self.core_in.at[0, shard], self.cross_in.at[shard])

    def near_all(self):
        for offset in self.collect.order:
            self.arrive(offset + 1)
            self.collect.near(offset)

    def combine_all(self):
        for offset in self.collect.order:
            self.arrive(offset)
            self.collect.combine(offset)


def feed_forward_rows(act, cot, units, down, hidden, d_units, width):
    act_rows, cot_rows = act[...], cot[...]
    step = 256

    def columns(at, size):
        lanes, up_lanes = pl.ds(at, size), pl.ds(width + at, size)
        gate_pre = dot(act_rows, units[:, lanes])
        up_pre = dot(act_rows, units[:, up_lanes])
        d_hidden = dot_last(cot_rows, down[lanes])
        sigmoid_g = jax.nn.sigmoid(gate_pre)
        silu_g = gate_pre * sigmoid_g
        hidden[:, lanes] = (silu_g * up_pre).astype(LOW)
        d_units[:, lanes] = (
            d_hidden * up_pre * sigmoid_g * (1.0 + gate_pre * (1.0 - sigmoid_g))
        ).astype(LOW)
        d_units[:, up_lanes] = (d_hidden * silu_g).astype(LOW)

    @pl.loop(0, width // step)
    def _(at):
        columns(pl.multiple_of(at * step, 128), step)

    if width % step:
        columns(width - width % step, width % step)


def put_shards(target, columns, block):
    shards, rows = target.shape[:2]
    if rows % 16 == 0:
        target[:, :, columns] = block.reshape(shards, rows, block.shape[1])
    else:
        for shard in range(shards):
            target[shard, :, columns] = block[shard * rows : (shard + 1) * rows]


def backward_kernel(
    slot,
    all_rows_ref, gains_ref, in_ref, out_ref, units_ref, down_ref, act_ref, cot_ref,
    outputs_ref, d_rows_ref, down_sum, units_sum, in_sum, out_sum, small_sum, ffn_in,
    d_act, d_core, d_cross, down_grad, down_near, down_far, units_grad, units_near, units_far,
    w_out_core, w_out_cross, w_out_near, w_out_far,
    w_in_core, w_in_cross, w_in_near, w_in_far,
    small, small_in, send_sems, recv_sems, local_sems,
):
    rows, features = all_rows_ref.shape
    shards = units_grad.shape[0]
    units_width = down_ref.shape[0]
    copies = Copies(send_sems, recv_sems)
    local = Local(local_sems)
    place = copies.place
    far = list(range(2, shards, 2))
    bits = [1 << k for k in range(1, shards.bit_length() - 1)]
    copies.meet([(0, offset) for offset in [*far, 1]] + [(1, 0), (2, 0)])

    def collector(grad, near, far_in):
        at = lambda offset: grad.at[flipped(place, offset)]
        return Collect(copies, shards, at, at, near, far_in)

    down = collector(down_grad, down_near, down_far)
    units = collector(units_grad, units_near, units_far)
    d_near, d_far, ffn_near, down_share = {}, [], {}, []

    def feed_forward(m_units, m_down, act, cot, hidden, d_units):
        part = lambda ref, turn: ref.at[turn * rows : (turn + 1) * rows]
        loads = {"units": local.copy(units_ref, m_units)}
        for turn in (3, 2, 1, 0):
            loads[turn] = [
                local.copy(act_ref.at[turn], part(act, turn)),
                local.copy(cot_ref.at[turn], part(cot, turn)),
            ]
            if turn == 3:
                loads["down"] = local.copy(down_ref, m_down)

        def units_of(turn):
            for load in loads[turn]:
                load.wait()
            if turn == 3:
                loads["units"].wait()
                loads["down"].wait()
            feed_forward_rows(
                part(act, turn), part(cot, turn), m_units, m_down,
                part(hidden, turn), part(d_units, turn), units_width,
            )

        def d_act_of(turn):
            block = part(d_units, turn)
            d_act[turn] = dot_last(block[...], m_units[...]).astype(LOW)
            if turn % 2:
                d_near[turn] = copies.send(
                    lambda: d_act.at[turn], lambda: d_core.at[turn // 2], 1, 0
                )

        def send_across(held):
            return copies.send(lambda: d_act.at[2, held], lambda: d_cross.at[held], 2, 0)

        def ffn_of(turn):
            block = part(hidden, turn)
            block[:, :features] = dot(block[...], m_down[...]).astype(LOW)
            if turn % 2:
                ffn_near[turn] = copies.send(
                    lambda: part(hidden, turn).at[:, :features],
                    lambda: ffn_in.at[turn // 2],
                    1,
                    0,
                )

        per = 256 * shards // features

        def units_grad_of(chunk):
            base = flipped(place // per, chunk) * per
            lanes = pl.ds(pl.multiple_of(base * (features // shards), 256), 256)
            block = dot_first(act[:, lanes], d_units[...]).astype(LOW)
            units_grad[pl.ds(base, per)] = block.reshape(per, -1, block.shape[1])
            for offset in units.order:
                if offset // per == chunk:
                    units.near(offset)

        for turn in (3, 2):
            units_of(turn)
            d_act_of(turn)
        d_near[3].wait_recv()
        for start in range(0, rows, slot):
            held = slice(start, start + slot)
            add_into(d_act.at[2, held], d_core.at[1, held])
            d_far.append(send_across(held))
        for turn in (1, 0):
            units_of(turn)
        for at in range(0, features, 256):
            lanes = slice(at, at + 256)
            put_shards(down_grad, lanes, dot_first(hidden[...], cot[:, lanes]).astype(LOW))
        down.near_all()
        ffn_of(3)
        ffn_of(2)
        chunks = list(range(features // 256))[::-1]
        units_grad_of(chunks[0])

        copies.sent(d_near[3])
        ffn_near[3].wait_recv()
        load = local.copy(ffn_in.at[1], d_act.at[3])
        units_grad_of(chunks[1])
        load.wait()
        add_into(d_act.at[3], part(hidden, 2).at[:, :features])
        across = copies.send(lambda: d_act.at[3], lambda: ffn_in.at[2], 2, 0)
        ffn_near[2] = across
        down.combine(down.order[0])
        for chunk in chunks[2:]:
            units_grad_of(chunk)
        d_act_of(1)
        down.combine(down.order[1])
        d_act_of(0)
        ffn_of(1)
        down.combine(down.order[2])
        copies.sent(d_near[1])
        d_act[1] = dot(part(hidden, 0)[...], m_down[...]).astype(LOW)
        for offset in down.order[3:]:
            down.combine(offset)
        copies.sent(ffn_near[3])
        copies.sent(ffn_near[1])

    pl.run_scoped(
        feed_forward,
        pltpu.VMEM(units_ref.shape, LOW),
        pltpu.VMEM(down_ref.shape, LOW),
        pltpu.VMEM((4 * rows, features), LOW),
        pltpu.VMEM((4 * rows, features), LOW),
        pltpu.VMEM((4 * rows, units_width), LOW),
        pltpu.VMEM((4 * rows, 2 * units_width), LOW),
    )

    def mixer(
        rows_ref, v_in, v_out, act_one, mixer_in, hstate, d_hstate, d_mixer, d_proj, w_out_parts
    ):
        load_rows = local.copy(all_rows_ref, rows_ref)
        load_in = local.copy(in_ref, v_in)
        load_out = local.copy(out_ref, v_out)
        gain_one, gain_two = gains_ref[0:1], gains_ref[1:2]

        load_cot = local.copy(cot_ref.at[0], d_mixer)

        def first(at):
            act_one[at] = normed(rows_ref[at].astype(F32), gain_one).astype(LOW)

        load_rows.wait()
        row_loop(rows, 64, first)
        load_in.wait()
        width = features // 4
        w_out = CollectAll(
            copies, shards, width, w_out_parts, w_out_core, w_out_cross, w_out_near, w_out_far
        )

        def columns_back(part_b, part_c, part_x):
            for part in range(4):
                at = part * width
                lanes = slice(at, at + width)
                b_now, c_now, x_now, _, convolved = mixer_columns(
                    act_one[...], v_in, gains_ref, at, width, features, slot
                )
                part_b[:, lanes] = b_now
                part_c[:, lanes] = c_now
                part_x[:, lanes] = x_now
                mixer_in[:, lanes] = (c_now * convolved).astype(LOW)
            load_out.wait()
            for start in range(0, rows, slot):
                held = slice(start, start + slot)
                hstate[held] = rows_ref[held].astype(F32) + dot(
                    mixer_in[held], v_out[...].reshape(features, features)
                )

            units.combine(units.order[0])
            down_share.append(Share(copies, local, down, lambda at: down_sum.at[at]))
            down_share[0].settle()

            d_near[1].wait_recv()
            small[0] = jnp.zeros((8, features), F32)

            def second(at):
                d_now = (
                    d_act[0, at].astype(F32) + d_core[0, at].astype(F32) + d_cross[at].astype(F32)
                )
                values = hstate[at]
                scale = rms_scale(values)
                small[0, 1:2] += jnp.sum(d_now * values * scale, axis=0, keepdims=True)
                d_values = d_mixer[at].astype(F32) + norm_back(d_now, values, scale, gain_two)
                d_hstate[at] = d_values
                d_mixer[at] = d_values.astype(LOW)

            for copy in d_far:
                copy.wait_recv()
            load_cot.wait()
            row_loop(rows, 64, second)

            for turn in (3, 1):
                w_out.compute(turn, mixer_in, d_mixer)
                w_out.to_core(turn)
            for turn in (2, 0):
                w_out.compute(turn, mixer_in, d_mixer)

            per = shards * width // features
            for part in range(4):
                at = part * width
                lanes = slice(at, at + width)
                block = v_out[part * per : (part + 1) * per].reshape(width, features)
                d_mixin = dot_last(d_mixer[...], block)
                taps = [gains_ref[2 + k : 3 + k, lanes] for k in range(3)]
                for start in range(0, rows, slot):
                    held = slice(start, start + slot)
                    d_mix = d_mixin[held]
                    b_now, c_now, x_now = part_b[held, lanes], part_c[held, lanes], part_x[held, lanes]
                    product = b_now * x_now
                    before = [shifted(product, 2), shifted(product, 1), product]
                    convolved = taps[0] * before[0] + taps[1] * before[1] + taps[2] * before[2]
                    d_conv = d_mix * c_now
                    for k in range(3):
                        small[0, 2 + k : 3 + k, lanes] += jnp.sum(
                            d_conv * before[k], axis=0, keepdims=True
                        )
                    d_product = (
                        taps[2] * d_conv
                        + taps[1] * shifted(d_conv, -1)
                        + taps[0] * shifted(d_conv, -2)
                    )
                    d_proj[held, lanes] = (d_product * x_now).astype(LOW)
                    d_proj[held, features + at : features + at + width] = (d_mix * convolved).astype(LOW)
                    d_proj[held, 2 * features + at : 2 * features + at + width] = (
                        d_product * b_now
                    ).astype(LOW)
                if part == 0:
                    w_out.to_cross()
                if part == 2:
                    units.combine(units.order[1])

        pl.run_scoped(columns_back, *[pltpu.VMEM((rows, features), F32)] * 3)

        def finish(w_in_parts):
            w_in = CollectAll(
                copies, shards, 3 * width, w_in_parts, w_in_core, w_in_cross, w_in_near, w_in_far
            )
            for turn in (3, 1):
                w_in.compute(turn, act_one, d_proj)
                w_in.to_core(turn)
            for turn in (2, 0):
                w_in.compute(turn, act_one, d_proj)
            w_in.to_cross()
            units.combine(units.order[2])

            def rows_back(start):
                held = slice(start, start + slot)
                d_now = dot_last(d_proj[held], v_in[...].reshape(features, 3 * features))
                values = rows_ref[held].astype(F32)
                scale = rms_scale(values)
                small[0, 0:1] += jnp.sum(d_now * values * scale, axis=0, keepdims=True)
                d_hstate[held] += norm_back(d_now, values, scale, gain_one)

            hops = [(0, 1), *[(0, bit) for bit in bits], (1, 0), (2, 0)]
            flight, summed = [], []

            def small_hop():
                step = len(flight)
                if len(summed) < step:
                    flight[-1].wait_recv()
                    small[step] = small[step - 1] + small_in[step - 1]
                    summed.append(step)
                if step < len(hops):
                    flight.append(copies.send(small.at[step], small_in.at[step], *hops[step]))

            def columns(target, width):
                return lambda at: target.at[:, pl.ds(pl.multiple_of(at * width, width), width)]

            starts = list(range(0, rows, slot))
            for start in starts[:-1]:
                rows_back(start)
            w_out.near_all()
            rows_back(starts[-1])
            d_out = local.copy(d_hstate, d_rows_ref)
            small_hop()

            ffn_near[1].wait_recv()
            ffn_near[2].wait_recv()
            for copy in d_far:
                copies.sent(copy)
            loads = [
                local.copy(ffn_in.at[0], d_act.at[0]),
                local.copy(ffn_in.at[2], d_act.at[2]),
            ]
            for load in loads:
                load.wait()
            small_hop()
            add_into(hstate, d_act.at[1], d_act.at[0], d_act.at[2])
            put_out = local.copy(hstate, outputs_ref)
            small_hop()
            for offset in units.order[3:]:
                units.combine(offset)
            w_in.near_all()
            small_hop()
            units_share = Share(copies, local, units, lambda at: units_sum.at[at])
            w_out.combine_all()
            small_hop()
            for offset in w_in.collect.order:
                w_in.arrive(offset)
                w_in.collect.combine(offset)
                if offset == w_in.collect.order[1]:
                    out_share = Share(copies, local, w_out.collect, columns(out_sum, width))
            while len(summed) < len(hops):
                small_hop()
            small_sum[...] = small[len(hops)]
            in_share = Share(copies, local, w_in.collect, columns(in_sum, 3 * width))
            shares = [down_share[0], units_share, out_share, in_share]
            for share in shares:
                share.forward()
            for share in shares:
                share.finish()
            put_out.wait()
            d_out.wait()
            copies.close()

        pl.run_scoped(finish, pltpu.VMEM((4, shards, part_rows, 3 * width), LOW))

    whole = (rows, features)
    part_rows = in_ref.shape[1]
    pl.run_scoped(
        mixer,
        pltpu.VMEM(whole, LOW),
        pltpu.VMEM(in_ref.shape, LOW),
        pltpu.VMEM(out_ref.shape, LOW),
        pltpu.VMEM(whole, LOW),
        pltpu.VMEM(whole, LOW),
        pltpu.VMEM(whole, F32),
        pltpu.VMEM(whole, F32),
        pltpu.VMEM(whole, LOW),
        pltpu.VMEM((rows, 3 * features), LOW),
        pltpu.VMEM((4, shards, part_rows, features // 4), LOW),
    )


def run_backward(rows, gains, m_in, m_out, m_units, m_down, act, cot, slot):
    count, features = rows.shape
    shards, part = m_in.shape[:2]
    cut = m_down.shape[0] // shards
    units = m_units.shape[1]
    half = shards // 2
    hbm = pl.BlockSpec(memory_space=pltpu.HBM)
    vmem = pl.BlockSpec(memory_space=pltpu.VMEM)
    hops = 10 * shards + 40
    depth = shards.bit_length() + 1

    def blocks(*shape):
        return [
            pltpu.VMEM((half, *shape), LOW),
            pltpu.VMEM((half if shards == 8 else half - 1, *shape), LOW),
        ]

    def quarters(width):
        return [
            pltpu.VMEM((2, shards, part, width), LOW),
            pltpu.VMEM((shards, part, width), LOW),
            *blocks(part, width),
        ]

    whole = (count, features)
    return pl.pallas_call(
        functools.partial(backward_kernel, slot),
        out_shape=[
            jax.ShapeDtypeStruct(*shape)
            for shape in (
                (whole, F32),
                (whole, F32),
                ((4, cut, features), LOW),
                ((4, part, units), LOW),
                ((part, 3 * features), LOW),
                ((part, features), LOW),
                ((8, features), F32),
                ((3, *whole), LOW),
            )
        ],
        in_specs=[hbm, vmem] + [hbm] * 6,
        out_specs=[hbm] * 6 + [vmem, hbm],
        scratch_shapes=[
            pltpu.VMEM((4, *whole), LOW),
            pltpu.VMEM((2, *whole), LOW),
            pltpu.VMEM(whole, LOW),
            pltpu.VMEM((shards, cut, features), LOW),
            *blocks(cut, features),
            pltpu.VMEM((shards, part, units), LOW),
            *blocks(part, units),
            *quarters(features // 4),
            *quarters(3 * features // 4),
            pltpu.VMEM((depth + 1, 8, features), F32),
            pltpu.VMEM((depth, 8, features), F32),
            pltpu.SemaphoreType.DMA((hops,)),
            pltpu.SemaphoreType.DMA((hops,)),
            pltpu.SemaphoreType.DMA((48,)),
        ],
        compiler_params=pltpu.CompilerParams(
            collective_id=1, has_side_effects=True, vmem_limit_bytes=127 << 19
        ),
        name="backward",
    )(rows, gains, m_in, m_out, m_units, m_down, act, cot)


def finish_kernel(
    cut, units_ref, down_ref, in_ref, out_ref, rows_ref, d_rows_ref,
    gate_out, up_out, down_out, in_out, out_out, rows_out, d_rows_out,
):
    half = units_ref.shape[2] // 2
    for side, target in enumerate((gate_out, up_out)):
        for at in range(half // cut):
            for quarter in range(4):
                start = (4 * at + quarter) * cut
                target[:, start : start + cut] = units_ref[
                    quarter, :, side * half + at * cut : side * half + (at + 1) * cut
                ].astype(F32)
    down_out[...] = down_ref[...].astype(F32)
    in_out[...] = in_ref[...].astype(F32)
    out_out[...] = out_ref[...].astype(F32)
    rows_out[...] = rows_ref[...]
    d_rows_out[...] = d_rows_ref[...]


def run_finish(units, down, w_in, w_out, outputs, d_rows):
    part, columns = units.shape[1:]
    cut, features = down.shape[1:]
    down = down.reshape(4 * cut, features)
    steps = 4 if part % 64 == 0 and cut % 16 == 0 else 1

    def rows(array):
        return pl.BlockSpec((array.shape[0] // steps, array.shape[1]), lambda at: (at, 0))

    wide = jax.ShapeDtypeStruct((part, 2 * columns), F32)
    narrow = (down, w_in, w_out, outputs, d_rows)
    outs = [wide, wide, *[jax.ShapeDtypeStruct(array.shape, F32) for array in narrow]]
    return pl.pallas_call(
        functools.partial(finish_kernel, cut),
        grid=(steps,),
        out_shape=outs,
        in_specs=[
            pl.BlockSpec((4, part // steps, columns), lambda at: (0, at, 0)),
            *[rows(array) for array in narrow],
        ],
        out_specs=[rows(out) for out in outs],
        compiler_params=pltpu.CompilerParams(vmem_limit_bytes=62 << 20),
        name="finish",
    )(units, *narrow)


def on_device(
    inputs, cotangent, lengths, norm_one, w_in, conv_w, w_out, norm_two, w_gate, w_up, w_down
):
    micro_count, tok_rows, features = inputs.shape
    shards = lax.axis_size("fsdp")
    place = lax.axis_index("fsdp")
    all_rows = micro_count * tok_rows
    cut = w_down.shape[0] // 4
    part = w_in.shape[0]
    part_ff = shards * cut

    small = jnp.concatenate([norm_one[None], norm_two[None], conv_w, jnp.zeros_like(conv_w)])
    rows_low = inputs.reshape(all_rows, features)
    m_in, m_out, m_units, m_down, act_all, cot_all, gains = run_forward(
        lengths, rows_low, cotangent.reshape(all_rows, features), small.astype(F32),
        w_in, w_out, w_gate, w_up, w_down.reshape(4, cut, features), tok_rows,
    )

    outputs, d_rows, down_sum, units_sum, in_sum, out_sum, small_sum, _ = run_backward(
        rows_low, gains, m_in, m_out, m_units.reshape(features, 2 * part_ff),
        m_down.reshape(part_ff, features), act_all, cot_all, tok_rows,
    )
    d_gate, d_up, d_down, d_in, d_out, outputs, d_rows = run_finish(
        units_sum, down_sum, in_sum, out_sum, outputs, d_rows
    )
    small_own = lax.dynamic_slice_in_dim(small_sum, place * part, part, 1)
    return (
        outputs.reshape(inputs.shape),
        d_rows.reshape(inputs.shape),
        small_own[0],
        d_in,
        small_own[2:5],
        d_out,
        small_own[1],
        d_gate,
        d_up,
        d_down,
    )


def solution(mesh):
    return jax.shard_map(
        on_device,
        mesh=mesh,
        in_specs=(
            P(None, ("rep", "fsdp"), None),
            P(None, ("rep", "fsdp"), None),
            P(),
            P("fsdp"),
            P("fsdp", None),
            P(None, "fsdp"),
            P("fsdp", None),
            P("fsdp"),
            P("fsdp", None),
            P("fsdp", None),
            P("fsdp", None),
        ),
        out_specs=(
            P(None, ("rep", "fsdp"), None),
            P(None, ("rep", "fsdp"), None),
            P("fsdp"),
            P("fsdp", None),
            P(None, "fsdp"),
            P("fsdp", None),
            P("fsdp"),
            P("fsdp", None),
            P("fsdp", None),
            P("fsdp", None),
        ),
        check_vma=False,
    )
```

```python
import functools

import jax
import jax.numpy as jnp
from jax import lax
from jax.experimental import pallas as pl
from jax.experimental.pallas import tpu as pltpu
from jax.sharding import PartitionSpec as P

EPSILON = 1e-05
LOW = jnp.bfloat16
F32 = jnp.float32
MESH = pl.DeviceIdType.MESH


def rms_scale(values):
    return lax.rsqrt(jnp.mean(values * values, axis=-1, keepdims=True) + EPSILON)


def dot(left, right):
    return jnp.dot(left, right, preferred_element_type=F32)


def dot_last(left, right):
    return lax.dot_general(left, right, (((1,), (1,)), ((), ())), preferred_element_type=F32)


def dot_first(left, right):
    return lax.dot_general(left, right, (((0,), (0,)), ((), ())), preferred_element_type=F32)


def norm_back(d_act, values, scale, gain):
    scaled = d_act * gain
    return scale * (
        scaled - values * scale * scale * jnp.mean(scaled * values, axis=-1, keepdims=True)
    )


def flipped(index, offset):
    bit = 1
    while bit <= offset:
        if offset & bit:
            index = index + bit - 2 * bit * ((index // bit) % 2)
        bit *= 2
    return index


class Copy:
    def __init__(self, copies, at, source, target, bits):
        self.copies, self.at, self.bits = copies, at, bits
        self.source, self.target = source, target

    def made(self):
        return pltpu.make_async_remote_copy(
            src_ref=self.source() if callable(self.source) else self.source,
            dst_ref=self.target() if callable(self.target) else self.target,
            send_sem=self.copies.sems[0].at[self.at],
            recv_sem=self.copies.sems[1].at[self.at],
            device_id=self.copies.peer(*self.bits),
            device_id_type=MESH,
        )

    def start(self):
        if self.only is None:
            self.made().start()
        else:
            pl.when(self.only)(lambda: self.made().start())

    def wait_recv(self):
        self.made().wait_recv()

    def wait_send(self):
        if self.only is None:
            self.made().wait_send()
        else:
            pl.when(self.only)(lambda: self.made().wait_send())


class Copies:
    def __init__(self, send_sems, recv_sems):
        self.sems = send_sems, recv_sems
        self.rep = lax.axis_index("rep")
        self.place = lax.axis_index("fsdp")
        self.started = []
        self.done = []
        self.relays = lax.axis_size("fsdp") == 8
        inner = ((self.place // 2 + 1) // 2) % 2
        self.inner, self.outer = inner == 1, inner == 0

    def peer(self, rep_bits, place_bits):
        return (flipped(self.rep, rep_bits), flipped(self.place, place_bits))

    def meet(self, peers):
        barrier = pltpu.get_barrier_semaphore()
        for bits in peers:
            pl.semaphore_signal(barrier, inc=1, device_id=self.peer(*bits), device_id_type=MESH)
        pl.semaphore_wait(barrier, len(peers))

    def send(self, source, target, rep_bits, place_bits):
        copy = self.plan(source, target, rep_bits, place_bits, None)
        copy.start()
        return copy

    def plan(self, source, target, rep_bits, place_bits, only):
        copy = Copy(self, len(self.started), source, target, (rep_bits, place_bits))
        copy.only = only
        self.started.append(copy)
        return copy

    def sent(self, copy):
        copy.wait_send()
        copy.source = copy.target
        self.done.append(copy)

    def close(self):
        for copy in self.started:
            if not any(copy is other for other in self.done):
                copy.wait_send()


class Local:
    def __init__(self, sems):
        self.sems = sems
        self.started = []

    def copy(self, source, target):
        copy = pltpu.make_async_copy(source, target, self.sems.at[len(self.started)])
        copy.start()
        self.started.append(copy)
        return copy


class Spread:
    def __init__(self, copies, locals_, shards, source, target, at=None):
        self.copies = copies
        self.target = target
        self.at = at if at is not None else (lambda shard: target.at[shard])
        self.source = source
        self.locals = locals_
        self.far = list(range(2, shards, 2))
        self.near = [1] + [offset + 1 for offset in self.far]

    def start(self):
        copies = self.copies
        here = self.at(copies.place)
        self.arriving = {}
        for offset in self.far:
            only = copies.inner if copies.relays and offset == 6 else None
            self.arriving[offset] = copies.plan(self.source, here, 0, offset, only)
            self.arriving[offset].start()
        self.arriving[1] = copies.send(self.source, here, 0, 1)
        if copies.relays:
            block = lambda: self.at(flipped(copies.place, 4))
            self.relay = copies.plan(block, block, 0, 2, copies.inner)
        if self.locals is not None:
            self.own = self.locals.copy(self.source, here)

    def arrive(self, offset):
        copies = self.copies
        if copies.relays and offset == 6:
            pl.when(copies.inner)(lambda: self.arriving[6].wait_recv())
            pl.when(copies.outer)(lambda: self.relay.wait_recv())
        else:
            self.arriving[offset].wait_recv()
        if copies.relays and offset == 4:
            self.relay.start()
        if offset % 2 == 0:
            block = self.at(flipped(copies.place, offset))
            self.arriving[offset + 1] = copies.send(block, block, 0, 1)

    def finish(self):
        for offset in self.near:
            self.arriving[offset].wait_recv()
        if self.locals is not None:
            self.own.wait()


class SpreadAll(Spread):
    def __init__(self, copies, locals_, shards, source, target, width):
        self.width = width
        self.whole = source
        self.local_all = locals_
        rep = copies.rep
        super().__init__(
            copies,
            None,
            shards,
            source.at[:, self.columns(rep)],
            target,
            lambda shard: target.at[shard, :, self.columns(rep)],
        )
        self.across = {}
        self.core = []

    def columns(self, rep):
        return pl.ds(pl.multiple_of(rep * self.width, self.width), self.width)

    def start(self):
        super().start()
        self.own = self.local_all.copy(self.whole, self.target.at[self.copies.place])

    def arrive(self, offset):
        super().arrive(offset)
        block = self.at(flipped(self.copies.place, offset))
        self.across[offset] = self.copies.send(block, block, 2, 0)
        self.core.append(self.copies.send(block, block, 1, 0))

    def cross(self, offset):
        copies = self.copies
        self.across[offset].wait_recv()
        shard = flipped(copies.place, offset)
        block = self.target.at[shard, :, self.columns(flipped(copies.rep, 2))]
        self.core.append(copies.send(block, block, 1, 0))

    def finish(self):
        for copy in self.core:
            copy.wait_recv()
        self.own.wait()


def row_loop(rows, step, body):
    @pl.loop(0, rows // step)
    def _(at):
        body(pl.ds(pl.multiple_of(at * step, step), step))


def normed(values, gain):
    return values * rms_scale(values) * gain


def shifted(values, by):
    rows = values.shape[0]
    at = lax.broadcasted_iota(jnp.int32, values.shape, 0)
    turned = pltpu.roll(values, by % rows, 0)
    kept = at >= by if by > 0 else at < rows + by
    return jnp.where(kept, turned, 0.0)


def mixer_columns(act, m_in, gains, at, width, features, slot):
    lanes = pl.ds(at, width)
    parts = []
    for base in (0, features, 2 * features):
        block = m_in[:, :, base + at : base + at + width].reshape(features, width)
        parts.append(dot(act, block))
    part_b, part_c, part_x = parts
    taps = [gains[2 + k : 3 + k, at : at + width] for k in range(3)]
    product = part_b * part_x
    convolved = []
    for start in range(0, act.shape[0], slot):
        rows = product[start : start + slot]
        convolved.append(
            taps[0] * shifted(rows, 2) + taps[1] * shifted(rows, 1) + taps[2] * rows
        )
    return part_b, part_c, part_x, product, jnp.concatenate(convolved)


def own_columns(rep, wide, target):
    half = target.shape[1] // 2
    shards = lax.axis_size("fsdp")
    cut = half // shards

    def lay(quarter):
        for at in range(shards):
            start = (4 * at + quarter) * cut
            for side in range(2):
                target[:, side * half + at * cut : side * half + (at + 1) * cut] = wide[
                    side, :, start : start + cut
                ]

    for quarter in range(4):
        pl.when(rep == quarter)(functools.partial(lay, quarter))


def forward_kernel(
    slot,
    lengths_ref, rows_ref, cot_ref, small_ref, in_ref, out_ref, gate_ref, up_ref, down_ref,
    all_in, all_out, all_units, all_down, all_act, all_cot, kept_low, kept_parts, kept_state, gains_ref,
    small_all, v_in, v_out, act_one, mixer_in, act_two, cot_live, wide, units_own, down_own,
    parts, state,
    send_sems, recv_sems, local_sems,
):
    rows, features = rows_ref.shape
    shards = all_units.shape[0]
    copies = Copies(send_sems, recv_sems)
    local = Local(local_sems)
    far = list(range(2, shards, 2))
    copies.meet([(0, offset) for offset in [*far, 1]] + [(1, 0), (2, 0)])

    small = Spread(copies, local, shards, small_ref, small_all)
    w_in = SpreadAll(copies, local, shards, in_ref, v_in, in_ref.shape[1] // 4)
    w_out = SpreadAll(copies, local, shards, out_ref, v_out, out_ref.shape[1] // 4)
    units = Spread(copies, local, shards, units_own, all_units)
    down = Spread(copies, local, shards, down_own, all_down)

    small.start()
    w_in.start()
    w_out.start()
    loads = [local.copy(gate_ref, wide.at[0]), local.copy(up_ref, wide.at[1])]
    loads.append(local.copy(down_ref.at[copies.rep], down_own))
    for offset in far:
        small.arrive(offset)
    w_in.arrive(1)
    w_in.arrive(far[0])
    for load in loads:
        load.wait()
    own_columns(copies.rep, wide, units_own)
    for offset in far[1:]:
        w_in.arrive(offset)
    w_out.arrive(1)
    for offset in far:
        w_out.arrive(offset)
    units.start()
    small.finish()
    gains_ref[...] = jnp.concatenate([small_all[at] for at in range(shards)], axis=1)
    gain_one = gains_ref[0:1]
    for offset in far:
        w_in.arrive(offset + 1)
    for offset in far:
        w_out.arrive(offset + 1)

    slot_id = copies.rep * shards + copies.place
    for micro in range(rows // slot):
        length = lengths_ref[micro, slot_id]
        for start in range(0, slot, 64):
            held = slice(micro * slot + start, micro * slot + start + 64)
            at = start + lax.broadcasted_iota(jnp.int32, (64, features), 0)
            cot_live[held] = jnp.where(at < length, cot_ref[held].astype(F32), 0.0).astype(LOW)
    own_cot = local.copy(cot_live, all_cot.at[0])
    cot_core = copies.send(cot_live, all_cot.at[1], 1, 0)
    cot_across = copies.send(cot_live, all_cot.at[2], 2, 0)

    def first(at):
        act_one[at] = normed(rows_ref[at].astype(F32), gain_one).astype(LOW)

    row_loop(rows, 64, first)
    units.arrive(far[0])
    down.start()
    order = [1, *far, *[offset + 1 for offset in far]]
    for offset in order:
        w_in.cross(offset)
    for offset in far[1:-1]:
        units.arrive(offset)
    for offset in order:
        w_out.cross(offset)
    w_in.finish()

    width = features // 4
    for part in range(4):
        at = part * width
        part_b, part_c, part_x, _, convolved = mixer_columns(
            act_one[...], v_in, gains_ref, at, width, features, slot
        )
        for index, values in enumerate((part_b, part_c, part_x)):
            parts[index, :, at : at + width] = values
        mixer_in[:, at : at + width] = (part_c * convolved).astype(LOW)
        if part == 1:
            units.arrive(far[-1])
    down.arrive(far[0])
    keeps = [
        local.copy(v_in, all_in),
        local.copy(act_one, kept_low.at[0]),
        local.copy(mixer_in, kept_low.at[1]),
        local.copy(parts, kept_parts),
    ]
    w_out.finish()
    keeps.append(local.copy(v_out, all_out))
    spread = []
    for start in range(0, rows, slot):
        held = slice(start, start + slot)
        hstate = rows_ref[held].astype(F32) + dot(
            mixer_in[held], v_out[...].reshape(features, features)
        )
        state[held] = hstate
        act_two[held] = normed(hstate, gains_ref[1:2]).astype(LOW)
        block = act_two.at[held]
        spread.append(
            (
                held,
                copies.send(block, all_act.at[2, held], 2, 0),
                copies.send(block, all_act.at[1, held], 1, 0),
                local.copy(block, all_act.at[0, held]),
            )
        )
    keeps.append(local.copy(state, kept_state))
    for offset in far[1:]:
        down.arrive(offset)
    cot_across.wait_recv()
    corner = [copies.send(all_cot.at[2], all_cot.at[3], 1, 0)]
    for held, across, _, _ in spread:
        across.wait_recv()
        corner.append(copies.send(all_act.at[2, held], all_act.at[3, held], 1, 0))
    units.finish()
    down.finish()
    cot_core.wait_recv()
    for _, _, core, own in spread:
        core.wait_recv()
        own.wait()
    for copy in corner:
        copy.wait_recv()
    own_cot.wait()
    for keep in keeps:
        keep.wait()
    copies.close()


def run_forward(lengths, rows, cot, small, w_in, w_out, w_gate, w_up, w_down, slot):
    shards = lax.axis_size("fsdp")
    count, features = rows.shape
    part = w_in.shape[0]
    down = w_down.shape[1:]
    units = (part, 2 * shards * down[0])
    shapes = [
        (shards, *w_in.shape),
        (shards, *w_out.shape),
        (shards, *units),
        (shards, *down),
        (4, count, features),
        (4, count, features),
        (2, count, features),
    ]
    hbm = pl.BlockSpec(memory_space=pltpu.HBM)
    vmem = pl.BlockSpec(memory_space=pltpu.VMEM)
    smem = pl.BlockSpec(memory_space=pltpu.SMEM)
    hops = 12 * shards + 24
    return pl.pallas_call(
        functools.partial(forward_kernel, slot),
        out_shape=[jax.ShapeDtypeStruct(shape, LOW) for shape in shapes]
        + [
            jax.ShapeDtypeStruct(shape, F32)
            for shape in ((3, count, features), (count, features), (8, features))
        ],
        in_specs=[smem, vmem, vmem, vmem, hbm, hbm, hbm, hbm, hbm],
        out_specs=[hbm] * 9 + [vmem],
        scratch_shapes=[
            pltpu.VMEM((shards, 8, part), F32),
            pltpu.VMEM((shards, *w_in.shape), LOW),
            pltpu.VMEM((shards, *w_out.shape), LOW),
            pltpu.VMEM((count, features), LOW),
            pltpu.VMEM((count, features), LOW),
            pltpu.VMEM((count, features), LOW),
            pltpu.VMEM((count, features), LOW),
            pltpu.VMEM((2, *w_gate.shape), LOW),
            pltpu.VMEM(units, LOW),
            pltpu.VMEM(down, LOW),
            pltpu.VMEM((3, count, features), F32),
            pltpu.VMEM((count, features), F32),
            pltpu.SemaphoreType.DMA((hops,)),
            pltpu.SemaphoreType.DMA((hops,)),
            pltpu.SemaphoreType.DMA((24,)),
        ],
        compiler_params=pltpu.CompilerParams(
            collective_id=0, has_side_effects=True, vmem_limit_bytes=56 << 20
        ),
        name="forward",
    )(lengths, rows, cot, small, w_in, w_out, w_gate, w_up, w_down)


def add_into(target, *others):
    rows = target.shape[-2]
    step = next((size for size in (64, 48, 16) if rows % size == 0), rows)
    kind = target.dtype if len(others) == 1 else F32

    @pl.loop(0, rows // step)
    def _(at):
        held = pl.ds(pl.multiple_of(at * step, step), step)
        total = target[held].astype(kind)
        for other in others:
            total = total + other[held].astype(kind)
        target[held] = total.astype(target.dtype)


class Collect:
    def __init__(self, copies, shards, sent_at, own_at, near_in, far_in):
        self.copies = copies
        self.sent_at, self.own_at = sent_at, own_at
        self.near_in, self.far_in = near_in, far_in
        self.order = list(range(shards - 2, -1, -2))
        self.arriving = {}
        self.far = {}

    def near(self, offset):
        copies = self.copies
        self.arriving[offset] = copies.send(
            lambda: self.sent_at(offset + 1), lambda: self.near_in.at[offset // 2], 0, 1
        )

    def near_all(self):
        for offset in self.order:
            self.near(offset)

    def combine(self, offset):
        copies = self.copies
        self.arriving[offset].wait_recv()
        own = self.own_at(offset)
        add_into(own, self.near_in.at[offset // 2])
        if not offset:
            return
        source = lambda: self.own_at(offset)
        target = lambda: self.far_in.at[offset // 2 - 1]
        if copies.relays and offset == 6:
            self.far[6] = copies.plan(source, target, 0, 6, copies.inner)
            self.relay = copies.plan(source, lambda: self.far_in.at[3], 0, 2, copies.outer)
            self.far[6].start()
            self.relay.start()
            return
        if copies.relays and offset == 4:

            @pl.when(copies.inner)
            def _():
                self.relay.wait_recv()
                add_into(self.own_at(4), self.far_in.at[3])

        self.far[offset] = copies.send(source, target, 0, offset)

    def combine_all(self):
        for offset in self.order:
            self.combine(offset)

    def total(self):
        copies = self.copies
        relayed = [6] if copies.relays else []
        for offset, copy in self.far.items():
            if offset not in relayed:
                copy.wait_recv()
        if not relayed:
            add_into(self.own_at(0), *[self.far_in.at[k] for k in range(len(self.far))])
            return self.own_at(0)

        @pl.when(copies.inner)
        def _():
            self.far[6].wait_recv()
            add_into(self.own_at(0), *[self.far_in.at[k] for k in range(3)])

        @pl.when(copies.outer)
        def _():
            add_into(self.own_at(0), *[self.far_in.at[k] for k in range(2)])

        return self.own_at(0)


class Share:
    def __init__(self, copies, local, collect, target_at):
        self.copies = copies
        self.target_at = target_at
        collect.total()
        source = lambda: collect.own_at(0)
        here = lambda: target_at(copies.rep)
        self.across = copies.send(source, here, 2, 0)
        self.core = [copies.send(source, here, 1, 0)]
        self.own = local.copy(source(), here())

    def settle(self):
        self.own.wait()
        self.own = None

    def forward(self):
        self.across.wait_recv()
        block = lambda: self.target_at(flipped(self.copies.rep, 2))
        self.core.append(self.copies.send(block, block, 1, 0))

    def finish(self):
        for copy in self.core:
            copy.wait_recv()
        if self.own is not None:
            self.own.wait()


class CollectAll:
    def __init__(self, copies, shards, width, parts, core_in, cross_in, near_in, far_in):
        self.copies = copies
        self.width = width
        self.parts, self.core_in, self.cross_in = parts, core_in, cross_in
        place = copies.place
        self.collect = Collect(
            copies,
            shards,
            lambda offset: parts.at[0, flipped(place, offset)],
            lambda offset: parts.at[0, flipped(place, offset)],
            near_in,
            far_in,
        )
        self.core = {}
        self.cross = {}
        self.near_ready = False
        self.order = [o + 1 for o in self.collect.order] + self.collect.order

    def compute(self, turn, left, right):
        rep = flipped(self.copies.rep, turn)
        shards, rows, _ = self.parts.shape[1:]
        for at in range(0, self.width, 256):
            columns = pl.ds(pl.multiple_of(rep * self.width + at, 256), 256)
            block = dot_first(left[...], right[:, columns]).astype(LOW)
            self.parts[turn, :, :, at : at + 256] = block.reshape(shards, rows, 256)

    def to_core(self, turn):
        self.core[turn - 1] = self.copies.send(
            lambda: self.parts.at[turn], lambda: self.core_in.at[turn // 2], 1, 0
        )

    def to_cross(self):
        self.core[2].wait_recv()
        place = self.copies.place
        for offset in self.order:
            block = self.parts.at[2, flipped(place, offset)]
            add_into(block, self.core_in.at[1, flipped(place, offset)])
            self.cross_one(offset)

    def cross_one(self, offset):
        place = self.copies.place
        self.cross[offset] = self.copies.send(
            lambda: self.parts.at[2, flipped(place, offset)],
            lambda: self.cross_in.at[flipped(place, offset)],
            2,
            0,
        )

    def arrive(self, offset):
        if not self.near_ready:
            self.core[0].wait_recv()
            self.near_ready = True
        self.cross[offset].wait_recv()
        shard = flipped(self.copies.place, offset)
        add_into(self.parts.at[0, shard], self.core_in.at[0, shard], self.cross_in.at[shard])

    def near_all(self):
        for offset in self.collect.order:
            self.arrive(offset + 1)
            self.collect.near(offset)

    def combine_all(self):
        for offset in self.collect.order:
            self.arrive(offset)
            self.collect.combine(offset)


def feed_forward_rows(act, cot, units, down, hidden, d_units, width):
    act_rows, cot_rows = act[...], cot[...]
    step = 256

    def columns(at, size):
        lanes, up_lanes = pl.ds(at, size), pl.ds(width + at, size)
        gate_pre = dot(act_rows, units[:, lanes])
        up_pre = dot(act_rows, units[:, up_lanes])
        d_hidden = dot_last(cot_rows, down[lanes])
        sigmoid_g = jax.nn.sigmoid(gate_pre)
        silu_g = gate_pre * sigmoid_g
        hidden[:, lanes] = (silu_g * up_pre).astype(LOW)
        d_units[:, lanes] = (
            d_hidden * up_pre * sigmoid_g * (1.0 + gate_pre * (1.0 - sigmoid_g))
        ).astype(LOW)
        d_units[:, up_lanes] = (d_hidden * silu_g).astype(LOW)

    @pl.loop(0, width // step)
    def _(at):
        columns(pl.multiple_of(at * step, 128), step)

    if width % step:
        columns(width - width % step, width % step)


def put_shards(target, columns, block):
    shards, rows = target.shape[:2]
    if rows % 16 == 0:
        target[:, :, columns] = block.reshape(shards, rows, block.shape[1])
    else:
        for shard in range(shards):
            target[shard, :, columns] = block[shard * rows : (shard + 1) * rows]


def backward_kernel(
    slot,
    all_rows_ref, gains_ref, in_ref, out_ref, units_ref, down_ref, act_ref, cot_ref,
    kept_low, kept_parts, kept_state,
    outputs_ref, d_rows_ref, down_sum, units_sum, in_sum, out_sum, small_sum, ffn_in,
    d_act, d_core, d_cross, down_grad, down_near, down_far, units_grad, units_near, units_far,
    w_out_core, w_out_cross, w_out_near, w_out_far,
    w_in_core, w_in_cross, w_in_near, w_in_far,
    small, small_in, send_sems, recv_sems, local_sems,
):
    rows, features = all_rows_ref.shape
    shards = units_grad.shape[0]
    units_width = down_ref.shape[0]
    copies = Copies(send_sems, recv_sems)
    local = Local(local_sems)
    place = copies.place
    far = list(range(2, shards, 2))
    bits = [1 << k for k in range(1, shards.bit_length() - 1)]
    copies.meet([(0, offset) for offset in [*far, 1]] + [(1, 0), (2, 0)])

    def collector(grad, near, far_in):
        at = lambda offset: grad.at[flipped(place, offset)]
        return Collect(copies, shards, at, at, near, far_in)

    down = collector(down_grad, down_near, down_far)
    units = collector(units_grad, units_near, units_far)
    d_near, d_far, ffn_near, down_share = {}, [], {}, []

    def feed_forward(m_units, m_down, act, cot, hidden, d_units):
        part = lambda ref, turn: ref.at[turn * rows : (turn + 1) * rows]
        loads = {"units": local.copy(units_ref, m_units)}
        for turn in (3, 2, 1, 0):
            loads[turn] = [
                local.copy(act_ref.at[turn], part(act, turn)),
                local.copy(cot_ref.at[turn], part(cot, turn)),
            ]
            if turn == 3:
                loads["down"] = local.copy(down_ref, m_down)

        def units_of(turn):
            for load in loads[turn]:
                load.wait()
            if turn == 3:
                loads["units"].wait()
                loads["down"].wait()
            feed_forward_rows(
                part(act, turn), part(cot, turn), m_units, m_down,
                part(hidden, turn), part(d_units, turn), units_width,
            )

        def d_act_of(turn):
            block = part(d_units, turn)
            d_act[turn] = dot_last(block[...], m_units[...]).astype(LOW)
            if turn % 2:
                d_near[turn] = copies.send(
                    lambda: d_act.at[turn], lambda: d_core.at[turn // 2], 1, 0
                )

        def send_across(held):
            return copies.send(lambda: d_act.at[2, held], lambda: d_cross.at[held], 2, 0)

        def ffn_of(turn):
            block = part(hidden, turn)
            block[:, :features] = dot(block[...], m_down[...]).astype(LOW)
            if turn % 2:
                ffn_near[turn] = copies.send(
                    lambda: part(hidden, turn).at[:, :features],
                    lambda: ffn_in.at[turn // 2],
                    1,
                    0,
                )

        per = 256 * shards // features

        def units_grad_of(chunk):
            base = flipped(place // per, chunk) * per
            lanes = pl.ds(pl.multiple_of(base * (features // shards), 256), 256)
            block = dot_first(act[:, lanes], d_units[...]).astype(LOW)
            units_grad[pl.ds(base, per)] = block.reshape(per, -1, block.shape[1])
            for offset in units.order:
                if offset // per == chunk:
                    units.near(offset)

        for turn in (3, 2):
            units_of(turn)
            d_act_of(turn)
        d_near[3].wait_recv()
        for start in range(0, rows, slot):
            held = slice(start, start + slot)
            add_into(d_act.at[2, held], d_core.at[1, held])
            d_far.append(send_across(held))
        for turn in (1, 0):
            units_of(turn)
        wide = 512 if shards == 8 else 256
        for at in range(0, features, wide):
            lanes = slice(at, at + wide)
            put_shards(down_grad, lanes, dot_first(hidden[...], cot[:, lanes]).astype(LOW))
        down.near_all()
        ffn_of(3)
        ffn_of(2)
        chunks = list(range(features // 256))[::-1]
        units_grad_of(chunks[0])

        copies.sent(d_near[3])
        ffn_near[3].wait_recv()
        load = local.copy(ffn_in.at[1], d_act.at[3])
        units_grad_of(chunks[1])
        load.wait()
        add_into(d_act.at[3], part(hidden, 2).at[:, :features])
        across = copies.send(lambda: d_act.at[3], lambda: ffn_in.at[2], 2, 0)
        ffn_near[2] = across
        down.combine(down.order[0])
        for chunk in chunks[2:]:
            units_grad_of(chunk)
        d_act_of(1)
        down.combine(down.order[1])
        d_act_of(0)
        ffn_of(1)
        down.combine(down.order[2])
        copies.sent(d_near[1])
        d_act[1] = dot(part(hidden, 0)[...], m_down[...]).astype(LOW)
        for offset in down.order[3:]:
            down.combine(offset)
        copies.sent(ffn_near[3])
        copies.sent(ffn_near[1])

    pl.run_scoped(
        feed_forward,
        pltpu.VMEM(units_ref.shape, LOW),
        pltpu.VMEM(down_ref.shape, LOW),
        pltpu.VMEM((4 * rows, features), LOW),
        pltpu.VMEM((4 * rows, features), LOW),
        pltpu.VMEM((4 * rows, units_width), LOW),
        pltpu.VMEM((4 * rows, 2 * units_width), LOW),
    )

    def mixer(
        rows_ref, v_in, v_out, act_one, mixer_in, hstate, d_hstate, d_mixer, d_proj, w_out_parts
    ):
        gain_one, gain_two = gains_ref[0:1], gains_ref[1:2]
        load_state = local.copy(kept_state, hstate)
        load_cot = local.copy(cot_ref.at[0], d_mixer)
        load_mixer = local.copy(kept_low.at[1], mixer_in)
        load_out = local.copy(out_ref, v_out)

        width = features // 4
        w_out = CollectAll(
            copies, shards, width, w_out_parts, w_out_core, w_out_cross, w_out_near, w_out_far
        )

        def columns_back(part_b, part_c, part_x):
            load_parts = [
                local.copy(kept_parts.at[index], target)
                for index, target in enumerate((part_b, part_c, part_x))
            ]
            load_act = local.copy(kept_low.at[0], act_one)
            load_in = local.copy(in_ref, v_in)
            load_rows = local.copy(all_rows_ref, rows_ref)
            load_state.wait()

            d_near[1].wait_recv()
            small[0] = jnp.zeros((8, features), F32)

            def second(at):
                d_now = (
                    d_act[0, at].astype(F32) + d_core[0, at].astype(F32) + d_cross[at].astype(F32)
                )
                values = hstate[at]
                scale = rms_scale(values)
                small[0, 1:2] += jnp.sum(d_now * values * scale, axis=0, keepdims=True)
                d_values = d_mixer[at].astype(F32) + norm_back(d_now, values, scale, gain_two)
                d_hstate[at] = d_values
                d_mixer[at] = d_values.astype(LOW)

            for copy in d_far:
                copy.wait_recv()
            load_cot.wait()
            row_loop(rows, 64, second)
            load_mixer.wait()
            load_out.wait()
            for load in load_parts:
                load.wait()

            for turn in (3, 1):
                w_out.compute(turn, mixer_in, d_mixer)
                w_out.to_core(turn)
            for turn in (2, 0):
                w_out.compute(turn, mixer_in, d_mixer)

            per = shards * width // features
            for part in range(4):
                at = part * width
                lanes = slice(at, at + width)
                block = v_out[part * per : (part + 1) * per].reshape(width, features)
                d_mixin = dot_last(d_mixer[...], block)
                taps = [gains_ref[2 + k : 3 + k, lanes] for k in range(3)]
                for start in range(0, rows, slot):
                    held = slice(start, start + slot)
                    d_mix = d_mixin[held]
                    b_now, c_now, x_now = part_b[held, lanes], part_c[held, lanes], part_x[held, lanes]
                    product = b_now * x_now
                    before = [shifted(product, 2), shifted(product, 1), product]
                    convolved = taps[0] * before[0] + taps[1] * before[1] + taps[2] * before[2]
                    d_conv = d_mix * c_now
                    for k in range(3):
                        small[0, 2 + k : 3 + k, lanes] += jnp.sum(
                            d_conv * before[k], axis=0, keepdims=True
                        )
                    d_product = (
                        taps[2] * d_conv
                        + taps[1] * shifted(d_conv, -1)
                        + taps[0] * shifted(d_conv, -2)
                    )
                    d_proj[held, lanes] = (d_product * x_now).astype(LOW)
                    d_proj[held, features + at : features + at + width] = (d_mix * convolved).astype(LOW)
                    d_proj[held, 2 * features + at : 2 * features + at + width] = (
                        d_product * b_now
                    ).astype(LOW)
                if part == 0:
                    w_out.to_cross()
                if part == 1:
                    units.combine(units.order[0])
                    down_share.append(Share(copies, local, down, lambda at: down_sum.at[at]))
                    down_share[0].settle()

            load_act.wait()
            load_in.wait()
            load_rows.wait()

        pl.run_scoped(columns_back, *[pltpu.VMEM((rows, features), F32)] * 3)

        def finish(w_in_parts):
            w_in = CollectAll(
                copies, shards, 3 * width, w_in_parts, w_in_core, w_in_cross, w_in_near, w_in_far
            )
            w_in.compute(3, act_one, d_proj)
            w_in.to_core(3)
            w_in.compute(2, act_one, d_proj)
            w_in.to_cross()
            w_in.compute(1, act_one, d_proj)
            w_in.to_core(1)
            w_in.compute(0, act_one, d_proj)
            units.combine(units.order[1])

            def rows_back(start):
                held = slice(start, start + slot)
                d_now = dot_last(d_proj[held], v_in[...].reshape(features, 3 * features))
                values = rows_ref[held].astype(F32)
                scale = rms_scale(values)
                small[0, 0:1] += jnp.sum(d_now * values * scale, axis=0, keepdims=True)
                d_hstate[held] += norm_back(d_now, values, scale, gain_one)

            hops = [(0, 1), *[(0, bit) for bit in bits], (1, 0), (2, 0)]
            flight, summed = [], []

            def small_hop():
                step = len(flight)
                if len(summed) < step:
                    flight[-1].wait_recv()
                    small[step] = small[step - 1] + small_in[step - 1]
                    summed.append(step)
                if step < len(hops):
                    flight.append(copies.send(small.at[step], small_in.at[step], *hops[step]))

            def columns(target, width):
                return lambda at: target.at[:, pl.ds(pl.multiple_of(at * width, width), width)]

            starts = list(range(0, rows, slot))
            for start in starts[:-1]:
                rows_back(start)
            units.combine(units.order[2])
            w_out.near_all()
            rows_back(starts[-1])
            d_out = local.copy(d_hstate, d_rows_ref)
            small_hop()

            ffn_near[1].wait_recv()
            ffn_near[2].wait_recv()
            for copy in d_far:
                copies.sent(copy)
            loads = [
                local.copy(ffn_in.at[0], d_act.at[0]),
                local.copy(ffn_in.at[2], d_act.at[2]),
            ]
            for load in loads:
                load.wait()
            small_hop()
            add_into(hstate, d_act.at[1], d_act.at[0], d_act.at[2])
            put_out = local.copy(hstate, outputs_ref)
            small_hop()
            for offset in units.order[3:]:
                units.combine(offset)
            w_in.near_all()
            small_hop()
            units_share = Share(copies, local, units, lambda at: units_sum.at[at])
            w_out.combine_all()
            small_hop()
            for offset in w_in.collect.order:
                w_in.arrive(offset)
                w_in.collect.combine(offset)
                if offset == w_in.collect.order[1]:
                    out_share = Share(copies, local, w_out.collect, columns(out_sum, width))
            while len(summed) < len(hops):
                small_hop()
            small_sum[...] = small[len(hops)]
            in_share = Share(copies, local, w_in.collect, columns(in_sum, 3 * width))
            shares = [down_share[0], units_share, out_share, in_share]
            for share in shares:
                share.forward()
            for share in shares:
                share.finish()
            put_out.wait()
            d_out.wait()
            copies.close()

        pl.run_scoped(finish, pltpu.VMEM((4, shards, part_rows, 3 * width), LOW))

    whole = (rows, features)
    part_rows = in_ref.shape[1]
    pl.run_scoped(
        mixer,
        pltpu.VMEM(whole, LOW),
        pltpu.VMEM(in_ref.shape, LOW),
        pltpu.VMEM(out_ref.shape, LOW),
        pltpu.VMEM(whole, LOW),
        pltpu.VMEM(whole, LOW),
        pltpu.VMEM(whole, F32),
        pltpu.VMEM(whole, F32),
        pltpu.VMEM(whole, LOW),
        pltpu.VMEM((rows, 3 * features), LOW),
        pltpu.VMEM((4, shards, part_rows, features // 4), LOW),
    )


def run_backward(rows, gains, m_in, m_out, m_units, m_down, act, cot, kept, slot):
    count, features = rows.shape
    shards, part = m_in.shape[:2]
    cut = m_down.shape[0] // shards
    units = m_units.shape[1]
    half = shards // 2
    hbm = pl.BlockSpec(memory_space=pltpu.HBM)
    vmem = pl.BlockSpec(memory_space=pltpu.VMEM)
    hops = 10 * shards + 40
    depth = shards.bit_length() + 1

    def blocks(*shape):
        return [
            pltpu.VMEM((half, *shape), LOW),
            pltpu.VMEM((half if shards == 8 else half - 1, *shape), LOW),
        ]

    def quarters(width):
        return [
            pltpu.VMEM((2, shards, part, width), LOW),
            pltpu.VMEM((shards, part, width), LOW),
            *blocks(part, width),
        ]

    whole = (count, features)
    return pl.pallas_call(
        functools.partial(backward_kernel, slot),
        out_shape=[
            jax.ShapeDtypeStruct(*shape)
            for shape in (
                (whole, F32),
                (whole, F32),
                ((4, cut, features), LOW),
                ((4, part, units), LOW),
                ((part, 3 * features), LOW),
                ((part, features), LOW),
                ((8, features), F32),
                ((3, *whole), LOW),
            )
        ],
        in_specs=[hbm, vmem] + [hbm] * 9,
        out_specs=[hbm] * 6 + [vmem, hbm],
        scratch_shapes=[
            pltpu.VMEM((4, *whole), LOW),
            pltpu.VMEM((2, *whole), LOW),
            pltpu.VMEM(whole, LOW),
            pltpu.VMEM((shards, cut, features), LOW),
            *blocks(cut, features),
            pltpu.VMEM((shards, part, units), LOW),
            *blocks(part, units),
            *quarters(features // 4),
            *quarters(3 * features // 4),
            pltpu.VMEM((depth + 1, 8, features), F32),
            pltpu.VMEM((depth, 8, features), F32),
            pltpu.SemaphoreType.DMA((hops,)),
            pltpu.SemaphoreType.DMA((hops,)),
            pltpu.SemaphoreType.DMA((48,)),
        ],
        compiler_params=pltpu.CompilerParams(
            collective_id=1, has_side_effects=True, vmem_limit_bytes=127 << 19
        ),
        name="backward",
    )(rows, gains, m_in, m_out, m_units, m_down, act, cot, *kept)


def finish_kernel(
    cut, units_ref, down_ref, in_ref, out_ref, rows_ref, d_rows_ref,
    gate_out, up_out, down_out, in_out, out_out, rows_out, d_rows_out,
):
    half = units_ref.shape[2] // 2
    for side, target in enumerate((gate_out, up_out)):
        for at in range(half // cut):
            for quarter in range(4):
                start = (4 * at + quarter) * cut
                target[:, start : start + cut] = units_ref[
                    quarter, :, side * half + at * cut : side * half + (at + 1) * cut
                ].astype(F32)
    down_out[...] = down_ref[...].astype(F32)
    in_out[...] = in_ref[...].astype(F32)
    out_out[...] = out_ref[...].astype(F32)
    rows_out[...] = rows_ref[...]
    d_rows_out[...] = d_rows_ref[...]


def run_finish(units, down, w_in, w_out, outputs, d_rows):
    part, columns = units.shape[1:]
    cut, features = down.shape[1:]
    down = down.reshape(4 * cut, features)
    steps = 4 if part % 64 == 0 and cut % 16 == 0 else 1

    def rows(array):
        return pl.BlockSpec((array.shape[0] // steps, array.shape[1]), lambda at: (at, 0))

    wide = jax.ShapeDtypeStruct((part, 2 * columns), F32)
    narrow = (down, w_in, w_out, outputs, d_rows)
    outs = [wide, wide, *[jax.ShapeDtypeStruct(array.shape, F32) for array in narrow]]
    return pl.pallas_call(
        functools.partial(finish_kernel, cut),
        grid=(steps,),
        out_shape=outs,
        in_specs=[
            pl.BlockSpec((4, part // steps, columns), lambda at: (0, at, 0)),
            *[rows(array) for array in narrow],
        ],
        out_specs=[rows(out) for out in outs],
        compiler_params=pltpu.CompilerParams(vmem_limit_bytes=62 << 20),
        name="finish",
    )(units, *narrow)


def on_device(
    inputs, cotangent, lengths, norm_one, w_in, conv_w, w_out, norm_two, w_gate, w_up, w_down
):
    micro_count, tok_rows, features = inputs.shape
    shards = lax.axis_size("fsdp")
    place = lax.axis_index("fsdp")
    all_rows = micro_count * tok_rows
    cut = w_down.shape[0] // 4
    part = w_in.shape[0]
    part_ff = shards * cut

    small = jnp.concatenate([norm_one[None], norm_two[None], conv_w, jnp.zeros_like(conv_w)])
    rows_low = inputs.reshape(all_rows, features)
    m_in, m_out, m_units, m_down, act_all, cot_all, *kept, gains = run_forward(
        lengths, rows_low, cotangent.reshape(all_rows, features), small.astype(F32),
        w_in, w_out, w_gate, w_up, w_down.reshape(4, cut, features), tok_rows,
    )

    outputs, d_rows, down_sum, units_sum, in_sum, out_sum, small_sum, _ = run_backward(
        rows_low, gains, m_in, m_out, m_units.reshape(features, 2 * part_ff),
        m_down.reshape(part_ff, features), act_all, cot_all, kept, tok_rows,
    )
    d_gate, d_up, d_down, d_in, d_out, outputs, d_rows = run_finish(
        units_sum, down_sum, in_sum, out_sum, outputs, d_rows
    )
    small_own = lax.dynamic_slice_in_dim(small_sum, place * part, part, 1)
    return (
        outputs.reshape(inputs.shape),
        d_rows.reshape(inputs.shape),
        small_own[0],
        d_in,
        small_own[2:5],
        d_out,
        small_own[1],
        d_gate,
        d_up,
        d_down,
    )


def solution(mesh):
    return jax.shard_map(
        on_device,
        mesh=mesh,
        in_specs=(
            P(None, ("rep", "fsdp"), None),
            P(None, ("rep", "fsdp"), None),
            P(),
            P("fsdp"),
            P("fsdp", None),
            P(None, "fsdp"),
            P("fsdp", None),
            P("fsdp"),
            P("fsdp", None),
            P("fsdp", None),
            P("fsdp", None),
        ),
        out_specs=(
            P(None, ("rep", "fsdp"), None),
            P(None, ("rep", "fsdp"), None),
            P("fsdp"),
            P("fsdp", None),
            P(None, "fsdp"),
            P("fsdp", None),
            P("fsdp"),
            P("fsdp", None),
            P("fsdp", None),
            P("fsdp", None),
        ),
        check_vma=False,
    )
```

```python
import functools

import jax
import jax.numpy as jnp
from jax import lax
from jax.experimental import pallas as pl
from jax.experimental.pallas import tpu as pltpu
from jax.sharding import PartitionSpec as P

EPSILON = 1e-05
LOW = jnp.bfloat16
F32 = jnp.float32
MESH = pl.DeviceIdType.MESH


def rms_scale(values):
    return lax.rsqrt(jnp.mean(values * values, axis=-1, keepdims=True) + EPSILON)


def dot(left, right):
    return jnp.dot(left, right, preferred_element_type=F32)


def dot_last(left, right):
    return lax.dot_general(left, right, (((1,), (1,)), ((), ())), preferred_element_type=F32)


def dot_first(left, right):
    return lax.dot_general(left, right, (((0,), (0,)), ((), ())), preferred_element_type=F32)


def norm_back(d_act, values, scale, gain):
    scaled = d_act * gain
    return scale * (
        scaled - values * scale * scale * jnp.mean(scaled * values, axis=-1, keepdims=True)
    )


def flipped(index, offset):
    bit = 1
    while bit <= offset:
        if offset & bit:
            index = index + bit - 2 * bit * ((index // bit) % 2)
        bit *= 2
    return index


class Copy:
    def __init__(self, copies, at, source, target, bits):
        self.copies, self.at, self.bits = copies, at, bits
        self.source, self.target = source, target

    def made(self):
        return pltpu.make_async_remote_copy(
            src_ref=self.source() if callable(self.source) else self.source,
            dst_ref=self.target() if callable(self.target) else self.target,
            send_sem=self.copies.sems[0].at[self.at],
            recv_sem=self.copies.sems[1].at[self.at],
            device_id=self.copies.peer(*self.bits),
            device_id_type=MESH,
        )

    def start(self):
        if self.only is None:
            self.made().start()
        else:
            pl.when(self.only)(lambda: self.made().start())

    def wait_recv(self):
        self.made().wait_recv()

    def wait_send(self):
        if self.only is None:
            self.made().wait_send()
        else:
            pl.when(self.only)(lambda: self.made().wait_send())


class Copies:
    def __init__(self, send_sems, recv_sems):
        self.sems = send_sems, recv_sems
        self.rep = lax.axis_index("rep")
        self.place = lax.axis_index("fsdp")
        self.started = []
        self.done = []
        self.relays = lax.axis_size("fsdp") == 8
        inner = ((self.place // 2 + 1) // 2) % 2
        self.inner, self.outer = inner == 1, inner == 0

    def peer(self, rep_bits, place_bits):
        return (flipped(self.rep, rep_bits), flipped(self.place, place_bits))

    def meet(self, peers):
        barrier = pltpu.get_barrier_semaphore()
        for bits in peers:
            pl.semaphore_signal(barrier, inc=1, device_id=self.peer(*bits), device_id_type=MESH)
        pl.semaphore_wait(barrier, len(peers))

    def send(self, source, target, rep_bits, place_bits):
        copy = self.plan(source, target, rep_bits, place_bits, None)
        copy.start()
        return copy

    def plan(self, source, target, rep_bits, place_bits, only):
        copy = Copy(self, len(self.started), source, target, (rep_bits, place_bits))
        copy.only = only
        self.started.append(copy)
        return copy

    def sent(self, copy):
        copy.wait_send()
        copy.source = copy.target
        self.done.append(copy)

    def close(self):
        for copy in self.started:
            if not any(copy is other for other in self.done):
                copy.wait_send()


class Local:
    def __init__(self, sems):
        self.sems = sems
        self.started = []

    def copy(self, source, target):
        copy = pltpu.make_async_copy(source, target, self.sems.at[len(self.started)])
        copy.start()
        self.started.append(copy)
        return copy


class Spread:
    def __init__(self, copies, locals_, shards, source, target, at=None):
        self.copies = copies
        self.target = target
        self.at = at if at is not None else (lambda shard: target.at[shard])
        self.source = source
        self.locals = locals_
        self.far = list(range(2, shards, 2))
        self.near = [1] + [offset + 1 for offset in self.far]

    def start(self):
        copies = self.copies
        here = self.at(copies.place)
        self.arriving = {}
        for offset in self.far:
            only = copies.inner if copies.relays and offset == 6 else None
            self.arriving[offset] = copies.plan(self.source, here, 0, offset, only)
            self.arriving[offset].start()
        self.arriving[1] = copies.send(self.source, here, 0, 1)
        if copies.relays:
            block = lambda: self.at(flipped(copies.place, 4))
            self.relay = copies.plan(block, block, 0, 2, copies.inner)
        if self.locals is not None:
            self.own = self.locals.copy(self.source, here)

    def arrive(self, offset):
        copies = self.copies
        if copies.relays and offset == 6:
            pl.when(copies.inner)(lambda: self.arriving[6].wait_recv())
            pl.when(copies.outer)(lambda: self.relay.wait_recv())
        else:
            self.arriving[offset].wait_recv()
        if copies.relays and offset == 4:
            self.relay.start()
        if offset % 2 == 0:
            block = self.at(flipped(copies.place, offset))
            self.arriving[offset + 1] = copies.send(block, block, 0, 1)

    def finish(self):
        for offset in self.near:
            self.arriving[offset].wait_recv()
        if self.locals is not None:
            self.own.wait()


class SpreadAll(Spread):
    def __init__(self, copies, locals_, shards, source, target, width):
        self.width = width
        self.whole = source
        self.local_all = locals_
        rep = copies.rep
        super().__init__(
            copies,
            None,
            shards,
            source.at[:, self.columns(rep)],
            target,
            lambda shard: target.at[shard, :, self.columns(rep)],
        )
        self.across = {}
        self.core = []

    def columns(self, rep):
        return pl.ds(pl.multiple_of(rep * self.width, self.width), self.width)

    def start(self):
        super().start()
        self.own = self.local_all.copy(self.whole, self.target.at[self.copies.place])

    def arrive(self, offset):
        super().arrive(offset)
        block = self.at(flipped(self.copies.place, offset))
        self.across[offset] = self.copies.send(block, block, 2, 0)
        self.core.append(self.copies.send(block, block, 1, 0))

    def cross(self, offset):
        copies = self.copies
        self.across[offset].wait_recv()
        shard = flipped(copies.place, offset)
        block = self.target.at[shard, :, self.columns(flipped(copies.rep, 2))]
        self.core.append(copies.send(block, block, 1, 0))

    def finish(self):
        for copy in self.core:
            copy.wait_recv()
        self.own.wait()


def row_loop(rows, step, body):
    @pl.loop(0, rows // step)
    def _(at):
        body(pl.ds(pl.multiple_of(at * step, step), step))


def normed(values, gain):
    return values * rms_scale(values) * gain


def shifted(values, by):
    rows = values.shape[0]
    at = lax.broadcasted_iota(jnp.int32, values.shape, 0)
    turned = pltpu.roll(values, by % rows, 0)
    kept = at >= by if by > 0 else at < rows + by
    return jnp.where(kept, turned, 0.0)


def mixer_columns(act, m_in, gains, at, width, features, slot):
    lanes = pl.ds(at, width)
    parts = []
    for base in (0, features, 2 * features):
        block = m_in[:, :, base + at : base + at + width].reshape(features, width)
        parts.append(dot(act, block))
    part_b, part_c, part_x = parts
    taps = [gains[2 + k : 3 + k, at : at + width] for k in range(3)]
    product = part_b * part_x
    convolved = []
    for start in range(0, act.shape[0], slot):
        rows = product[start : start + slot]
        convolved.append(
            taps[0] * shifted(rows, 2) + taps[1] * shifted(rows, 1) + taps[2] * rows
        )
    return part_b, part_c, part_x, product, jnp.concatenate(convolved)


def own_columns(rep, wide, target):
    half = target.shape[1] // 2
    shards = lax.axis_size("fsdp")
    cut = half // shards

    def lay(quarter):
        for at in range(shards):
            start = (4 * at + quarter) * cut
            for side in range(2):
                target[:, side * half + at * cut : side * half + (at + 1) * cut] = wide[
                    side, :, start : start + cut
                ]

    for quarter in range(4):
        pl.when(rep == quarter)(functools.partial(lay, quarter))


def forward_kernel(
    slot,
    lengths_ref, rows_ref, cot_ref, small_ref, in_ref, out_ref, gate_ref, up_ref, down_ref,
    all_in, all_out, all_units, all_down, all_act, all_cot, kept_low, kept_parts, kept_state, gains_ref,
    small_all, v_in, v_out, act_one, mixer_in, act_two, cot_live, wide, units_own, down_own,
    parts, state,
    send_sems, recv_sems, local_sems,
):
    rows, features = rows_ref.shape
    shards = all_units.shape[0]
    copies = Copies(send_sems, recv_sems)
    local = Local(local_sems)
    far = list(range(2, shards, 2))
    loads = [local.copy(gate_ref, wide.at[0]), local.copy(up_ref, wide.at[1])]
    loads.append(local.copy(down_ref.at[copies.rep], down_own))
    copies.meet([(0, offset) for offset in [*far, 1]] + [(1, 0), (2, 0)])

    small = Spread(copies, local, shards, small_ref, small_all)
    w_in = SpreadAll(copies, local, shards, in_ref, v_in, in_ref.shape[1] // 4)
    w_out = SpreadAll(copies, local, shards, out_ref, v_out, out_ref.shape[1] // 4)
    units = Spread(copies, local, shards, units_own, all_units)
    down = Spread(copies, local, shards, down_own, all_down)

    small.start()
    w_in.start()
    w_out.start()
    for offset in far:
        small.arrive(offset)
    w_in.arrive(1)
    w_in.arrive(far[0])
    for load in loads:
        load.wait()
    own_columns(copies.rep, wide, units_own)
    for offset in far[1:]:
        w_in.arrive(offset)
    w_out.arrive(1)
    for offset in far:
        w_out.arrive(offset)
    units.start()
    small.finish()
    gains_ref[...] = jnp.concatenate([small_all[at] for at in range(shards)], axis=1)
    gain_one = gains_ref[0:1]
    for offset in far:
        w_in.arrive(offset + 1)
    for offset in far:
        w_out.arrive(offset + 1)

    slot_id = copies.rep * shards + copies.place
    for micro in range(rows // slot):
        length = lengths_ref[micro, slot_id]
        for start in range(0, slot, 64):
            held = slice(micro * slot + start, micro * slot + start + 64)
            at = start + lax.broadcasted_iota(jnp.int32, (64, features), 0)
            cot_live[held] = jnp.where(at < length, cot_ref[held].astype(F32), 0.0).astype(LOW)
    own_cot = local.copy(cot_live, all_cot.at[0])
    cot_core = copies.send(cot_live, all_cot.at[1], 1, 0)
    cot_across = copies.send(cot_live, all_cot.at[2], 2, 0)

    def first(at):
        act_one[at] = normed(rows_ref[at].astype(F32), gain_one).astype(LOW)

    row_loop(rows, 64, first)
    units.arrive(far[0])
    down.start()
    order = [1, *far, *[offset + 1 for offset in far]]
    for offset in order:
        w_in.cross(offset)
    for offset in far[1:-1]:
        units.arrive(offset)
    for offset in order:
        w_out.cross(offset)
    w_in.finish()

    width = features // 4
    for part in range(4):
        at = part * width
        part_b, part_c, part_x, _, convolved = mixer_columns(
            act_one[...], v_in, gains_ref, at, width, features, slot
        )
        for index, values in enumerate((part_b, part_c, part_x)):
            parts[index, :, at : at + width] = values
        mixer_in[:, at : at + width] = (part_c * convolved).astype(LOW)
        if part == 1:
            units.arrive(far[-1])
    down.arrive(far[0])
    keeps = [
        local.copy(v_in, all_in),
        local.copy(act_one, kept_low.at[0]),
        local.copy(mixer_in, kept_low.at[1]),
        local.copy(parts, kept_parts),
    ]
    w_out.finish()
    keeps.append(local.copy(v_out, all_out))
    spread = []
    for start in range(0, rows, slot):
        held = slice(start, start + slot)
        hstate = rows_ref[held].astype(F32) + dot(
            mixer_in[held], v_out[...].reshape(features, features)
        )
        state[held] = hstate
        act_two[held] = normed(hstate, gains_ref[1:2]).astype(LOW)
        block = act_two.at[held]
        spread.append(
            (
                held,
                copies.send(block, all_act.at[2, held], 2, 0),
                copies.send(block, all_act.at[1, held], 1, 0),
                local.copy(block, all_act.at[0, held]),
            )
        )
    keeps.append(local.copy(state, kept_state))
    for offset in far[1:]:
        down.arrive(offset)
    cot_across.wait_recv()
    corner = [copies.send(all_cot.at[2], all_cot.at[3], 1, 0)]
    for held, across, _, _ in spread:
        across.wait_recv()
        corner.append(copies.send(all_act.at[2, held], all_act.at[3, held], 1, 0))
    units.finish()
    down.finish()
    cot_core.wait_recv()
    for _, _, core, own in spread:
        core.wait_recv()
        own.wait()
    for copy in corner:
        copy.wait_recv()
    own_cot.wait()
    for keep in keeps:
        keep.wait()
    copies.close()


def run_forward(lengths, rows, cot, small, w_in, w_out, w_gate, w_up, w_down, slot):
    shards = lax.axis_size("fsdp")
    count, features = rows.shape
    part = w_in.shape[0]
    down = w_down.shape[1:]
    units = (part, 2 * shards * down[0])
    shapes = [
        (shards, *w_in.shape),
        (shards, *w_out.shape),
        (shards, *units),
        (shards, *down),
        (4, count, features),
        (4, count, features),
        (2, count, features),
    ]
    hbm = pl.BlockSpec(memory_space=pltpu.HBM)
    vmem = pl.BlockSpec(memory_space=pltpu.VMEM)
    smem = pl.BlockSpec(memory_space=pltpu.SMEM)
    hops = 12 * shards + 24
    return pl.pallas_call(
        functools.partial(forward_kernel, slot),
        out_shape=[jax.ShapeDtypeStruct(shape, LOW) for shape in shapes]
        + [
            jax.ShapeDtypeStruct(shape, F32)
            for shape in ((3, count, features), (count, features), (8, features))
        ],
        in_specs=[smem, vmem, vmem, vmem, hbm, hbm, hbm, hbm, hbm],
        out_specs=[hbm] * 9 + [vmem],
        scratch_shapes=[
            pltpu.VMEM((shards, 8, part), F32),
            pltpu.VMEM((shards, *w_in.shape), LOW),
            pltpu.VMEM((shards, *w_out.shape), LOW),
            pltpu.VMEM((count, features), LOW),
            pltpu.VMEM((count, features), LOW),
            pltpu.VMEM((count, features), LOW),
            pltpu.VMEM((count, features), LOW),
            pltpu.VMEM((2, *w_gate.shape), LOW),
            pltpu.VMEM(units, LOW),
            pltpu.VMEM(down, LOW),
            pltpu.VMEM((3, count, features), F32),
            pltpu.VMEM((count, features), F32),
            pltpu.SemaphoreType.DMA((hops,)),
            pltpu.SemaphoreType.DMA((hops,)),
            pltpu.SemaphoreType.DMA((24,)),
        ],
        compiler_params=pltpu.CompilerParams(
            collective_id=0, has_side_effects=True, vmem_limit_bytes=56 << 20
        ),
        name="forward",
    )(lengths, rows, cot, small, w_in, w_out, w_gate, w_up, w_down)


def add_into(target, *others):
    rows = target.shape[-2]
    step = next((size for size in (64, 48, 16) if rows % size == 0), rows)
    kind = target.dtype if len(others) == 1 else F32

    @pl.loop(0, rows // step)
    def _(at):
        held = pl.ds(pl.multiple_of(at * step, step), step)
        total = target[held].astype(kind)
        for other in others:
            total = total + other[held].astype(kind)
        target[held] = total.astype(target.dtype)


class Collect:
    def __init__(self, copies, shards, sent_at, own_at, near_in, far_in):
        self.copies = copies
        self.sent_at, self.own_at = sent_at, own_at
        self.near_in, self.far_in = near_in, far_in
        self.order = list(range(shards - 2, -1, -2))
        self.arriving = {}
        self.far = {}

    def near(self, offset):
        copies = self.copies
        self.arriving[offset] = copies.send(
            lambda: self.sent_at(offset + 1), lambda: self.near_in.at[offset // 2], 0, 1
        )

    def near_all(self):
        for offset in self.order:
            self.near(offset)

    def combine(self, offset):
        copies = self.copies
        self.arriving[offset].wait_recv()
        own = self.own_at(offset)
        add_into(own, self.near_in.at[offset // 2])
        if not offset:
            return
        source = lambda: self.own_at(offset)
        target = lambda: self.far_in.at[offset // 2 - 1]
        if copies.relays and offset == 6:
            self.far[6] = copies.plan(source, target, 0, 6, copies.inner)
            self.relay = copies.plan(source, lambda: self.far_in.at[3], 0, 2, copies.outer)
            self.far[6].start()
            self.relay.start()
            return
        if copies.relays and offset == 4:

            @pl.when(copies.inner)
            def _():
                self.relay.wait_recv()
                add_into(self.own_at(4), self.far_in.at[3])

        self.far[offset] = copies.send(source, target, 0, offset)

    def combine_all(self):
        for offset in self.order:
            self.combine(offset)

    def total(self):
        copies = self.copies
        relayed = [6] if copies.relays else []
        for offset, copy in self.far.items():
            if offset not in relayed:
                copy.wait_recv()
        if not relayed:
            add_into(self.own_at(0), *[self.far_in.at[k] for k in range(len(self.far))])
            return self.own_at(0)

        @pl.when(copies.inner)
        def _():
            self.far[6].wait_recv()
            add_into(self.own_at(0), *[self.far_in.at[k] for k in range(3)])

        @pl.when(copies.outer)
        def _():
            add_into(self.own_at(0), *[self.far_in.at[k] for k in range(2)])

        return self.own_at(0)


class Share:
    def __init__(self, copies, local, collect, target_at):
        self.copies = copies
        self.target_at = target_at
        collect.total()
        source = lambda: collect.own_at(0)
        here = lambda: target_at(copies.rep)
        self.across = copies.send(source, here, 2, 0)
        self.core = [copies.send(source, here, 1, 0)]
        self.own = local.copy(source(), here())

    def settle(self):
        self.own.wait()
        self.own = None

    def forward(self):
        self.across.wait_recv()
        block = lambda: self.target_at(flipped(self.copies.rep, 2))
        self.core.append(self.copies.send(block, block, 1, 0))

    def finish(self):
        for copy in self.core:
            copy.wait_recv()
        if self.own is not None:
            self.own.wait()


class CollectAll:
    def __init__(self, copies, shards, width, parts, core_in, cross_in, near_in, far_in):
        self.copies = copies
        self.width = width
        self.parts, self.core_in, self.cross_in = parts, core_in, cross_in
        place = copies.place
        self.collect = Collect(
            copies,
            shards,
            lambda offset: parts.at[0, flipped(place, offset)],
            lambda offset: parts.at[0, flipped(place, offset)],
            near_in,
            far_in,
        )
        self.core = {}
        self.cross = {}
        self.near_ready = False
        self.order = [o + 1 for o in self.collect.order] + self.collect.order

    def compute(self, turn, left, right):
        rep = flipped(self.copies.rep, turn)
        shards, rows, _ = self.parts.shape[1:]
        for at in range(0, self.width, 256):
            columns = pl.ds(pl.multiple_of(rep * self.width + at, 256), 256)
            block = dot_first(left[...], right[:, columns]).astype(LOW)
            self.parts[turn, :, :, at : at + 256] = block.reshape(shards, rows, 256)

    def to_core(self, turn):
        self.core[turn - 1] = self.copies.send(
            lambda: self.parts.at[turn], lambda: self.core_in.at[turn // 2], 1, 0
        )

    def to_cross(self):
        self.core[2].wait_recv()
        place = self.copies.place
        for offset in self.order:
            block = self.parts.at[2, flipped(place, offset)]
            add_into(block, self.core_in.at[1, flipped(place, offset)])
            self.cross_one(offset)

    def cross_one(self, offset):
        place = self.copies.place
        self.cross[offset] = self.copies.send(
            lambda: self.parts.at[2, flipped(place, offset)],
            lambda: self.cross_in.at[flipped(place, offset)],
            2,
            0,
        )

    def arrive(self, offset):
        if not self.near_ready:
            self.core[0].wait_recv()
            self.near_ready = True
        self.cross[offset].wait_recv()
        shard = flipped(self.copies.place, offset)
        add_into(self.parts.at[0, shard], self.core_in.at[0, shard], self.cross_in.at[shard])

    def near_all(self):
        for offset in self.collect.order:
            self.arrive(offset + 1)
            self.collect.near(offset)

    def combine_all(self):
        for offset in self.collect.order:
            self.arrive(offset)
            self.collect.combine(offset)


def feed_forward_rows(act, cot, units, down, hidden, d_units, width):
    act_rows, cot_rows = act[...], cot[...]
    step = 256

    def columns(at, size):
        lanes, up_lanes = pl.ds(at, size), pl.ds(width + at, size)
        gate_pre = dot(act_rows, units[:, lanes])
        up_pre = dot(act_rows, units[:, up_lanes])
        d_hidden = dot_last(cot_rows, down[lanes])
        sigmoid_g = jax.nn.sigmoid(gate_pre)
        silu_g = gate_pre * sigmoid_g
        hidden[:, lanes] = (silu_g * up_pre).astype(LOW)
        d_units[:, lanes] = (
            d_hidden * up_pre * sigmoid_g * (1.0 + gate_pre * (1.0 - sigmoid_g))
        ).astype(LOW)
        d_units[:, up_lanes] = (d_hidden * silu_g).astype(LOW)

    @pl.loop(0, width // step)
    def _(at):
        columns(pl.multiple_of(at * step, 128), step)

    if width % step:
        columns(width - width % step, width % step)


def put_shards(target, columns, block):
    shards, rows = target.shape[:2]
    if rows % 16 == 0:
        target[:, :, columns] = block.reshape(shards, rows, block.shape[1])
    else:
        for shard in range(shards):
            target[shard, :, columns] = block[shard * rows : (shard + 1) * rows]


def backward_kernel(
    slot,
    all_rows_ref, gains_ref, in_ref, out_ref, units_ref, down_ref, act_ref, cot_ref,
    kept_low, kept_parts, kept_state,
    outputs_ref, d_rows_ref, down_sum, units_sum, in_sum, out_sum, small_sum, ffn_in,
    d_act, d_core, d_cross, down_grad, down_near, down_far, units_grad, units_near, units_far,
    w_out_core, w_out_cross, w_out_near, w_out_far,
    w_in_core, w_in_cross, w_in_near, w_in_far,
    small, small_in, send_sems, recv_sems, local_sems,
):
    rows, features = all_rows_ref.shape
    shards = units_grad.shape[0]
    units_width = down_ref.shape[0]
    copies = Copies(send_sems, recv_sems)
    local = Local(local_sems)
    place = copies.place
    far = list(range(2, shards, 2))
    bits = [1 << k for k in range(1, shards.bit_length() - 1)]
    peers = [(0, offset) for offset in [*far, 1]] + [(1, 0), (2, 0)]

    def collector(grad, near, far_in):
        at = lambda offset: grad.at[flipped(place, offset)]
        return Collect(copies, shards, at, at, near, far_in)

    down = collector(down_grad, down_near, down_far)
    units = collector(units_grad, units_near, units_far)
    d_near, d_far, ffn_near, down_share = {}, [], {}, []

    def feed_forward(m_units, m_down, act, cot, hidden, d_units):
        part = lambda ref, turn: ref.at[turn * rows : (turn + 1) * rows]
        loads = {"units": local.copy(units_ref, m_units)}
        for turn in (3, 2, 1, 0):
            loads[turn] = [
                local.copy(act_ref.at[turn], part(act, turn)),
                local.copy(cot_ref.at[turn], part(cot, turn)),
            ]
            if turn == 3:
                loads["down"] = local.copy(down_ref, m_down)

        copies.meet(peers)

        def units_of(turn):
            for load in loads[turn]:
                load.wait()
            if turn == 3:
                loads["units"].wait()
                loads["down"].wait()
            feed_forward_rows(
                part(act, turn), part(cot, turn), m_units, m_down,
                part(hidden, turn), part(d_units, turn), units_width,
            )

        def d_act_of(turn):
            block = part(d_units, turn)
            d_act[turn] = dot_last(block[...], m_units[...]).astype(LOW)
            if turn % 2:
                d_near[turn] = copies.send(
                    lambda: d_act.at[turn], lambda: d_core.at[turn // 2], 1, 0
                )

        def send_across(held):
            return copies.send(lambda: d_act.at[2, held], lambda: d_cross.at[held], 2, 0)

        def ffn_of(turn):
            block = part(hidden, turn)
            block[:, :features] = dot(block[...], m_down[...]).astype(LOW)
            if turn % 2:
                ffn_near[turn] = copies.send(
                    lambda: part(hidden, turn).at[:, :features],
                    lambda: ffn_in.at[turn // 2],
                    1,
                    0,
                )

        per = 256 * shards // features

        def units_grad_of(chunk):
            base = flipped(place // per, chunk) * per
            lanes = pl.ds(pl.multiple_of(base * (features // shards), 256), 256)
            block = dot_first(act[:, lanes], d_units[...]).astype(LOW)
            units_grad[pl.ds(base, per)] = block.reshape(per, -1, block.shape[1])
            for offset in units.order:
                if offset // per == chunk:
                    units.near(offset)

        for turn in (3, 2):
            units_of(turn)
            d_act_of(turn)
        d_near[3].wait_recv()
        for start in range(0, rows, slot):
            held = slice(start, start + slot)
            add_into(d_act.at[2, held], d_core.at[1, held])
            d_far.append(send_across(held))
        for turn in (1, 0):
            units_of(turn)
        wide = 512 if shards == 8 else 256
        for at in range(0, features, wide):
            lanes = slice(at, at + wide)
            put_shards(down_grad, lanes, dot_first(hidden[...], cot[:, lanes]).astype(LOW))
        down.near_all()
        ffn_of(3)
        ffn_of(2)
        chunks = list(range(features // 256))[::-1]
        units_grad_of(chunks[0])

        copies.sent(d_near[3])
        ffn_near[3].wait_recv()
        load = local.copy(ffn_in.at[1], d_act.at[3])
        units_grad_of(chunks[1])
        load.wait()
        add_into(d_act.at[3], part(hidden, 2).at[:, :features])
        across = copies.send(lambda: d_act.at[3], lambda: ffn_in.at[2], 2, 0)
        ffn_near[2] = across
        down.combine(down.order[0])
        for chunk in chunks[2:]:
            units_grad_of(chunk)
        d_act_of(1)
        down.combine(down.order[1])
        d_act_of(0)
        ffn_of(1)
        down.combine(down.order[2])
        copies.sent(d_near[1])
        d_act[1] = dot(part(hidden, 0)[...], m_down[...]).astype(LOW)
        for offset in down.order[3:]:
            down.combine(offset)
        copies.sent(ffn_near[3])
        copies.sent(ffn_near[1])

    pl.run_scoped(
        feed_forward,
        pltpu.VMEM(units_ref.shape, LOW),
        pltpu.VMEM(down_ref.shape, LOW),
        pltpu.VMEM((4 * rows, features), LOW),
        pltpu.VMEM((4 * rows, features), LOW),
        pltpu.VMEM((4 * rows, units_width), LOW),
        pltpu.VMEM((4 * rows, 2 * units_width), LOW),
    )

    def mixer(
        rows_ref, v_in, v_out, act_one, mixer_in, hstate, d_hstate, d_mixer, d_proj, w_out_parts
    ):
        gain_one, gain_two = gains_ref[0:1], gains_ref[1:2]
        load_state = local.copy(kept_state, hstate)
        load_cot = local.copy(cot_ref.at[0], d_mixer)
        load_mixer = local.copy(kept_low.at[1], mixer_in)
        load_out = local.copy(out_ref, v_out)

        width = features // 4
        w_out = CollectAll(
            copies, shards, width, w_out_parts, w_out_core, w_out_cross, w_out_near, w_out_far
        )

        def columns_back(part_b, part_c, part_x):
            load_parts = [
                local.copy(kept_parts.at[index], target)
                for index, target in enumerate((part_b, part_c, part_x))
            ]
            load_act = local.copy(kept_low.at[0], act_one)
            load_in = local.copy(in_ref, v_in)
            load_rows = local.copy(all_rows_ref, rows_ref)
            load_state.wait()

            d_near[1].wait_recv()
            small[0] = jnp.zeros((8, features), F32)

            def second(at):
                d_now = (
                    d_act[0, at].astype(F32) + d_core[0, at].astype(F32) + d_cross[at].astype(F32)
                )
                values = hstate[at]
                scale = rms_scale(values)
                small[0, 1:2] += jnp.sum(d_now * values * scale, axis=0, keepdims=True)
                d_values = d_mixer[at].astype(F32) + norm_back(d_now, values, scale, gain_two)
                d_hstate[at] = d_values
                d_mixer[at] = d_values.astype(LOW)

            for copy in d_far:
                copy.wait_recv()
            load_cot.wait()
            row_loop(rows, 64, second)
            load_mixer.wait()
            load_out.wait()
            for load in load_parts:
                load.wait()

            for turn in (3, 1):
                w_out.compute(turn, mixer_in, d_mixer)
                w_out.to_core(turn)
            for turn in (2, 0):
                w_out.compute(turn, mixer_in, d_mixer)

            per = shards * width // features
            for part in range(4):
                at = part * width
                lanes = slice(at, at + width)
                block = v_out[part * per : (part + 1) * per].reshape(width, features)
                d_mixin = dot_last(d_mixer[...], block)
                taps = [gains_ref[2 + k : 3 + k, lanes] for k in range(3)]
                for start in range(0, rows, slot):
                    held = slice(start, start + slot)
                    d_mix = d_mixin[held]
                    b_now, c_now, x_now = part_b[held, lanes], part_c[held, lanes], part_x[held, lanes]
                    product = b_now * x_now
                    before = [shifted(product, 2), shifted(product, 1), product]
                    convolved = taps[0] * before[0] + taps[1] * before[1] + taps[2] * before[2]
                    d_conv = d_mix * c_now
                    for k in range(3):
                        small[0, 2 + k : 3 + k, lanes] += jnp.sum(
                            d_conv * before[k], axis=0, keepdims=True
                        )
                    d_product = (
                        taps[2] * d_conv
                        + taps[1] * shifted(d_conv, -1)
                        + taps[0] * shifted(d_conv, -2)
                    )
                    d_proj[held, lanes] = (d_product * x_now).astype(LOW)
                    d_proj[held, features + at : features + at + width] = (d_mix * convolved).astype(LOW)
                    d_proj[held, 2 * features + at : 2 * features + at + width] = (
                        d_product * b_now
                    ).astype(LOW)
                if part == 0:
                    w_out.to_cross()
                if part == 1:
                    units.combine(units.order[0])
                    down_share.append(Share(copies, local, down, lambda at: down_sum.at[at]))
                    down_share[0].settle()

            load_act.wait()
            load_in.wait()
            load_rows.wait()

        pl.run_scoped(columns_back, *[pltpu.VMEM((rows, features), F32)] * 3)

        def finish(w_in_parts):
            w_in = CollectAll(
                copies, shards, 3 * width, w_in_parts, w_in_core, w_in_cross, w_in_near, w_in_far
            )
            w_in.compute(3, act_one, d_proj)
            w_in.to_core(3)
            w_in.compute(2, act_one, d_proj)
            w_in.to_cross()
            w_in.compute(1, act_one, d_proj)
            w_in.to_core(1)
            w_in.compute(0, act_one, d_proj)
            units.combine(units.order[1])

            def rows_back(start):
                held = slice(start, start + slot)
                d_now = dot_last(d_proj[held], v_in[...].reshape(features, 3 * features))
                values = rows_ref[held].astype(F32)
                scale = rms_scale(values)
                small[0, 0:1] += jnp.sum(d_now * values * scale, axis=0, keepdims=True)
                d_hstate[held] += norm_back(d_now, values, scale, gain_one)

            hops = [(0, 1), *[(0, bit) for bit in bits], (1, 0), (2, 0)]
            flight, summed = [], []

            def small_hop():
                step = len(flight)
                if len(summed) < step:
                    flight[-1].wait_recv()
                    small[step] = small[step - 1] + small_in[step - 1]
                    summed.append(step)
                if step < len(hops):
                    flight.append(copies.send(small.at[step], small_in.at[step], *hops[step]))

            def columns(target, width):
                return lambda at: target.at[:, pl.ds(pl.multiple_of(at * width, width), width)]

            starts = list(range(0, rows, slot))
            for start in starts[:-1]:
                rows_back(start)
            units.combine(units.order[2])
            w_out.near_all()
            rows_back(starts[-1])
            d_out = local.copy(d_hstate, d_rows_ref)
            small_hop()

            ffn_near[1].wait_recv()
            ffn_near[2].wait_recv()
            for copy in d_far:
                copies.sent(copy)
            loads = [
                local.copy(ffn_in.at[0], d_act.at[0]),
                local.copy(ffn_in.at[2], d_act.at[2]),
            ]
            for load in loads:
                load.wait()
            small_hop()
            add_into(hstate, d_act.at[1], d_act.at[0], d_act.at[2])
            put_out = local.copy(hstate, outputs_ref)
            small_hop()
            for offset in units.order[3:]:
                units.combine(offset)
            w_in.near_all()
            small_hop()
            units_share = Share(copies, local, units, lambda at: units_sum.at[at])
            w_out.combine_all()
            small_hop()
            for offset in w_in.collect.order:
                w_in.arrive(offset)
                w_in.collect.combine(offset)
                if offset == w_in.collect.order[1]:
                    out_share = Share(copies, local, w_out.collect, columns(out_sum, width))
            while len(summed) < len(hops):
                small_hop()
            small_sum[...] = small[len(hops)]
            in_share = Share(copies, local, w_in.collect, columns(in_sum, 3 * width))
            shares = [down_share[0], units_share, out_share, in_share]
            for share in shares:
                share.forward()
            for share in shares:
                share.finish()
            put_out.wait()
            d_out.wait()
            copies.close()

        pl.run_scoped(finish, pltpu.VMEM((4, shards, part_rows, 3 * width), LOW))

    whole = (rows, features)
    part_rows = in_ref.shape[1]
    pl.run_scoped(
        mixer,
        pltpu.VMEM(whole, LOW),
        pltpu.VMEM(in_ref.shape, LOW),
        pltpu.VMEM(out_ref.shape, LOW),
        pltpu.VMEM(whole, LOW),
        pltpu.VMEM(whole, LOW),
        pltpu.VMEM(whole, F32),
        pltpu.VMEM(whole, F32),
        pltpu.VMEM(whole, LOW),
        pltpu.VMEM((rows, 3 * features), LOW),
        pltpu.VMEM((4, shards, part_rows, features // 4), LOW),
    )


def run_backward(rows, gains, m_in, m_out, m_units, m_down, act, cot, kept, slot):
    count, features = rows.shape
    shards, part = m_in.shape[:2]
    cut = m_down.shape[0] // shards
    units = m_units.shape[1]
    half = shards // 2
    hbm = pl.BlockSpec(memory_space=pltpu.HBM)
    vmem = pl.BlockSpec(memory_space=pltpu.VMEM)
    hops = 10 * shards + 40
    depth = shards.bit_length() + 1

    def blocks(*shape):
        return [
            pltpu.VMEM((half, *shape), LOW),
            pltpu.VMEM((half if shards == 8 else half - 1, *shape), LOW),
        ]

    def quarters(width):
        return [
            pltpu.VMEM((2, shards, part, width), LOW),
            pltpu.VMEM((shards, part, width), LOW),
            *blocks(part, width),
        ]

    whole = (count, features)
    return pl.pallas_call(
        functools.partial(backward_kernel, slot),
        out_shape=[
            jax.ShapeDtypeStruct(*shape)
            for shape in (
                (whole, F32),
                (whole, F32),
                ((4, cut, features), LOW),
                ((4, part, units), LOW),
                ((part, 3 * features), LOW),
                ((part, features), LOW),
                ((8, features), F32),
                ((3, *whole), LOW),
            )
        ],
        in_specs=[hbm, vmem] + [hbm] * 9,
        out_specs=[hbm] * 6 + [vmem, hbm],
        scratch_shapes=[
            pltpu.VMEM((4, *whole), LOW),
            pltpu.VMEM((2, *whole), LOW),
            pltpu.VMEM(whole, LOW),
            pltpu.VMEM((shards, cut, features), LOW),
            *blocks(cut, features),
            pltpu.VMEM((shards, part, units), LOW),
            *blocks(part, units),
            *quarters(features // 4),
            *quarters(3 * features // 4),
            pltpu.VMEM((depth + 1, 8, features), F32),
            pltpu.VMEM((depth, 8, features), F32),
            pltpu.SemaphoreType.DMA((hops,)),
            pltpu.SemaphoreType.DMA((hops,)),
            pltpu.SemaphoreType.DMA((48,)),
        ],
        compiler_params=pltpu.CompilerParams(
            collective_id=1, has_side_effects=True, vmem_limit_bytes=127 << 19
        ),
        name="backward",
    )(rows, gains, m_in, m_out, m_units, m_down, act, cot, *kept)


def finish_kernel(
    cut, units_ref, down_ref, in_ref, out_ref, rows_ref, d_rows_ref, small_ref,
    gate_out, up_out, down_out, in_out, out_out, rows_out, d_rows_out, one_out, conv_out, two_out,
):
    half = units_ref.shape[2] // 2
    for side, target in enumerate((gate_out, up_out)):
        for at in range(half // cut):
            for quarter in range(4):
                start = (4 * at + quarter) * cut
                target[:, start : start + cut] = units_ref[
                    quarter, :, side * half + at * cut : side * half + (at + 1) * cut
                ].astype(F32)
    down_out[...] = down_ref[...].astype(F32)
    in_out[...] = in_ref[...].astype(F32)
    out_out[...] = out_ref[...].astype(F32)
    rows_out[...] = rows_ref[...]
    d_rows_out[...] = d_rows_ref[...]
    part = one_out.shape[1]
    start = lax.axis_index("fsdp") * part if small_ref.shape[1] > part else 0
    lanes = pl.ds(pl.multiple_of(start, 128), part) if small_ref.shape[1] > part else slice(None)
    one_out[...] = small_ref[0:1, lanes]
    two_out[...] = small_ref[1:2, lanes]
    conv_out[...] = small_ref[2:5, lanes]


def run_finish(units, down, w_in, w_out, outputs, d_rows, small):
    part, columns = units.shape[1:]
    cut, features = down.shape[1:]
    down = down.reshape(4 * cut, features)
    steps = 4 if part % 64 == 0 and cut % 16 == 0 else 1

    if part % 128:
        small = lax.dynamic_slice_in_dim(small, lax.axis_index("fsdp") * part, part, 1)

    def rows(array):
        return pl.BlockSpec((array.shape[0] // steps, array.shape[1]), lambda at: (at, 0))

    def same(array):
        return pl.BlockSpec(array.shape, lambda at: (0, 0))

    wide = jax.ShapeDtypeStruct((part, 2 * columns), F32)
    narrow = (down, w_in, w_out, outputs, d_rows)
    outs = [wide, wide, *[jax.ShapeDtypeStruct(array.shape, F32) for array in narrow]]
    sums = [jax.ShapeDtypeStruct((count, part), F32) for count in (1, 3, 1)]
    return pl.pallas_call(
        functools.partial(finish_kernel, cut),
        grid=(steps,),
        out_shape=[*outs, *sums],
        in_specs=[
            pl.BlockSpec((4, part // steps, columns), lambda at: (0, at, 0)),
            *[rows(array) for array in narrow],
            same(small),
        ],
        out_specs=[*[rows(out) for out in outs], *[same(out) for out in sums]],
        compiler_params=pltpu.CompilerParams(vmem_limit_bytes=62 << 20),
        name="finish",
    )(units, *narrow, small)


def on_device(
    inputs, cotangent, lengths, norm_one, w_in, conv_w, w_out, norm_two, w_gate, w_up, w_down
):
    micro_count, tok_rows, features = inputs.shape
    shards = lax.axis_size("fsdp")
    all_rows = micro_count * tok_rows
    cut = w_down.shape[0] // 4
    part = w_in.shape[0]
    part_ff = shards * cut

    small = jnp.concatenate([norm_one[None], norm_two[None], conv_w, jnp.zeros_like(conv_w)])
    rows_low = inputs.reshape(all_rows, features)
    m_in, m_out, m_units, m_down, act_all, cot_all, *kept, gains = run_forward(
        lengths, rows_low, cotangent.reshape(all_rows, features), small.astype(F32),
        w_in, w_out, w_gate, w_up, w_down.reshape(4, cut, features), tok_rows,
    )

    outputs, d_rows, down_sum, units_sum, in_sum, out_sum, small_sum, _ = run_backward(
        rows_low, gains, m_in, m_out, m_units.reshape(features, 2 * part_ff),
        m_down.reshape(part_ff, features), act_all, cot_all, kept, tok_rows,
    )
    d_gate, d_up, d_down, d_in, d_out, outputs, d_rows, d_one, d_conv, d_two = run_finish(
        units_sum, down_sum, in_sum, out_sum, outputs, d_rows, small_sum
    )
    return (
        outputs.reshape(inputs.shape),
        d_rows.reshape(inputs.shape),
        d_one[0],
        d_in,
        d_conv,
        d_out,
        d_two[0],
        d_gate,
        d_up,
        d_down,
    )


def solution(mesh):
    return jax.shard_map(
        on_device,
        mesh=mesh,
        in_specs=(
            P(None, ("rep", "fsdp"), None),
            P(None, ("rep", "fsdp"), None),
            P(),
            P("fsdp"),
            P("fsdp", None),
            P(None, "fsdp"),
            P("fsdp", None),
            P("fsdp"),
            P("fsdp", None),
            P("fsdp", None),
            P("fsdp", None),
        ),
        out_specs=(
            P(None, ("rep", "fsdp"), None),
            P(None, ("rep", "fsdp"), None),
            P("fsdp"),
            P("fsdp", None),
            P(None, "fsdp"),
            P("fsdp", None),
            P("fsdp"),
            P("fsdp", None),
            P("fsdp", None),
            P("fsdp", None),
        ),
        check_vma=False,
    )
```

```python
import functools

import jax
import jax.numpy as jnp
from jax import lax
from jax.experimental import pallas as pl
from jax.experimental.pallas import tpu as pltpu
from jax.sharding import PartitionSpec as P

EPSILON = 1e-05
LOW = jnp.bfloat16
F32 = jnp.float32
MESH = pl.DeviceIdType.MESH


def rms_scale(values):
    return lax.rsqrt(jnp.mean(values * values, axis=-1, keepdims=True) + EPSILON)


def dot(left, right):
    return jnp.dot(left, right, preferred_element_type=F32)


def dot_last(left, right):
    return lax.dot_general(left, right, (((1,), (1,)), ((), ())), preferred_element_type=F32)


def dot_first(left, right):
    return lax.dot_general(left, right, (((0,), (0,)), ((), ())), preferred_element_type=F32)


def norm_back(d_act, values, scale, gain):
    scaled = d_act * gain
    return scale * (
        scaled - values * scale * scale * jnp.mean(scaled * values, axis=-1, keepdims=True)
    )


def flipped(index, offset):
    bit = 1
    while bit <= offset:
        if offset & bit:
            index = index + bit - 2 * bit * ((index // bit) % 2)
        bit *= 2
    return index


class Copy:
    def __init__(self, copies, at, source, target, bits):
        self.copies, self.at, self.bits = copies, at, bits
        self.source, self.target = source, target

    def made(self):
        return pltpu.make_async_remote_copy(
            src_ref=self.source() if callable(self.source) else self.source,
            dst_ref=self.target() if callable(self.target) else self.target,
            send_sem=self.copies.sems[0].at[self.at],
            recv_sem=self.copies.sems[1].at[self.at],
            device_id=self.copies.peer(*self.bits),
            device_id_type=MESH,
        )

    def start(self):
        if self.only is None:
            self.made().start()
        else:
            pl.when(self.only)(lambda: self.made().start())

    def wait_recv(self):
        self.made().wait_recv()

    def wait_send(self):
        if self.only is None:
            self.made().wait_send()
        else:
            pl.when(self.only)(lambda: self.made().wait_send())


class Copies:
    def __init__(self, send_sems, recv_sems):
        self.sems = send_sems, recv_sems
        self.rep = lax.axis_index("rep")
        self.place = lax.axis_index("fsdp")
        self.started = []
        self.done = []
        self.relays = lax.axis_size("fsdp") == 8
        inner = ((self.place // 2 + 1) // 2) % 2
        self.inner, self.outer = inner == 1, inner == 0

    def peer(self, rep_bits, place_bits):
        return (flipped(self.rep, rep_bits), flipped(self.place, place_bits))

    def meet(self, peers):
        barrier = pltpu.get_barrier_semaphore()
        for bits in peers:
            pl.semaphore_signal(barrier, inc=1, device_id=self.peer(*bits), device_id_type=MESH)
        pl.semaphore_wait(barrier, len(peers))

    def send(self, source, target, rep_bits, place_bits):
        copy = self.plan(source, target, rep_bits, place_bits, None)
        copy.start()
        return copy

    def plan(self, source, target, rep_bits, place_bits, only):
        copy = Copy(self, len(self.started), source, target, (rep_bits, place_bits))
        copy.only = only
        self.started.append(copy)
        return copy

    def sent(self, copy):
        copy.wait_send()
        copy.source = copy.target
        self.done.append(copy)

    def close(self):
        for copy in self.started:
            if not any(copy is other for other in self.done):
                copy.wait_send()


class Local:
    def __init__(self, sems):
        self.sems = sems
        self.started = []

    def copy(self, source, target):
        copy = pltpu.make_async_copy(source, target, self.sems.at[len(self.started)])
        copy.start()
        self.started.append(copy)
        return copy


class Spread:
    def __init__(self, copies, locals_, shards, source, target, at=None):
        self.copies = copies
        self.target = target
        self.at = at if at is not None else (lambda shard: target.at[shard])
        self.source = source
        self.locals = locals_
        self.far = list(range(2, shards, 2))
        self.near = [1] + [offset + 1 for offset in self.far]

    def start(self):
        copies = self.copies
        here = self.at(copies.place)
        self.arriving = {}
        for offset in self.far:
            only = copies.inner if copies.relays and offset == 6 else None
            self.arriving[offset] = copies.plan(self.source, here, 0, offset, only)
            self.arriving[offset].start()
        self.arriving[1] = copies.send(self.source, here, 0, 1)
        if copies.relays:
            block = lambda: self.at(flipped(copies.place, 4))
            self.relay = copies.plan(block, block, 0, 2, copies.inner)
        if self.locals is not None:
            self.own = self.locals.copy(self.source, here)

    def arrive(self, offset):
        copies = self.copies
        if copies.relays and offset == 6:
            pl.when(copies.inner)(lambda: self.arriving[6].wait_recv())
            pl.when(copies.outer)(lambda: self.relay.wait_recv())
        else:
            self.arriving[offset].wait_recv()
        if copies.relays and offset == 4:
            self.relay.start()
        if offset % 2 == 0:
            block = self.at(flipped(copies.place, offset))
            self.arriving[offset + 1] = copies.send(block, block, 0, 1)

    def finish(self):
        for offset in self.near:
            self.arriving[offset].wait_recv()
        if self.locals is not None:
            self.own.wait()


class SpreadAll(Spread):
    def __init__(self, copies, locals_, shards, source, target, width):
        self.width = width
        self.whole = source
        self.local_all = locals_
        rep = copies.rep
        super().__init__(
            copies,
            None,
            shards,
            source.at[:, self.columns(rep)],
            target,
            lambda shard: target.at[shard, :, self.columns(rep)],
        )
        self.across = {}
        self.core = []

    def columns(self, rep):
        return pl.ds(pl.multiple_of(rep * self.width, self.width), self.width)

    def start(self):
        super().start()
        self.own = self.local_all.copy(self.whole, self.target.at[self.copies.place])

    def arrive(self, offset):
        super().arrive(offset)
        block = self.at(flipped(self.copies.place, offset))
        self.across[offset] = self.copies.send(block, block, 2, 0)
        self.core.append(self.copies.send(block, block, 1, 0))

    def cross(self, offset):
        copies = self.copies
        self.across[offset].wait_recv()
        shard = flipped(copies.place, offset)
        block = self.target.at[shard, :, self.columns(flipped(copies.rep, 2))]
        self.core.append(copies.send(block, block, 1, 0))

    def finish(self):
        for copy in self.core:
            copy.wait_recv()
        self.own.wait()


def row_loop(rows, step, body):
    @pl.loop(0, rows // step)
    def _(at):
        body(pl.ds(pl.multiple_of(at * step, step), step))


def normed(values, gain):
    return values * rms_scale(values) * gain


def shifted(values, by):
    rows = values.shape[0]
    at = lax.broadcasted_iota(jnp.int32, values.shape, 0)
    turned = pltpu.roll(values, by % rows, 0)
    kept = at >= by if by > 0 else at < rows + by
    return jnp.where(kept, turned, 0.0)


def mixer_columns(act, m_in, gains, at, width, features, slot):
    lanes = pl.ds(at, width)
    parts = []
    for base in (0, features, 2 * features):
        block = m_in[:, :, base + at : base + at + width].reshape(features, width)
        parts.append(dot(act, block))
    part_b, part_c, part_x = parts
    taps = [gains[2 + k : 3 + k, at : at + width] for k in range(3)]
    product = part_b * part_x
    convolved = []
    for start in range(0, act.shape[0], slot):
        rows = product[start : start + slot]
        convolved.append(
            taps[0] * shifted(rows, 2) + taps[1] * shifted(rows, 1) + taps[2] * rows
        )
    return part_b, part_c, part_x, product, jnp.concatenate(convolved)


def own_columns(rep, wide, target):
    half = target.shape[1] // 2
    shards = lax.axis_size("fsdp")
    cut = half // shards

    def lay(quarter):
        for at in range(shards):
            start = (4 * at + quarter) * cut
            for side in range(2):
                target[:, side * half + at * cut : side * half + (at + 1) * cut] = wide[
                    side, :, start : start + cut
                ]

    for quarter in range(4):
        pl.when(rep == quarter)(functools.partial(lay, quarter))


def forward_kernel(
    slot,
    lengths_ref, rows_ref, cot_ref, small_ref, in_ref, out_ref, gate_ref, up_ref, down_ref,
    all_in, all_out, all_units, all_down, all_act, all_cot, kept_low, kept_parts, kept_state, gains_ref,
    small_all, v_in, v_out, act_one, mixer_in, act_two, cot_live, wide, units_own, down_own,
    parts, state,
    send_sems, recv_sems, local_sems,
):
    rows, features = rows_ref.shape
    shards = all_units.shape[0]
    copies = Copies(send_sems, recv_sems)
    local = Local(local_sems)
    far = list(range(2, shards, 2))
    loads = [local.copy(gate_ref, wide.at[0]), local.copy(up_ref, wide.at[1])]
    loads.append(local.copy(down_ref.at[copies.rep], down_own))
    copies.meet([(0, offset) for offset in [*far, 1]] + [(1, 0), (2, 0)])

    small = Spread(copies, local, shards, small_ref, small_all)
    w_in = SpreadAll(copies, local, shards, in_ref, v_in, in_ref.shape[1] // 4)
    w_out = SpreadAll(copies, local, shards, out_ref, v_out, out_ref.shape[1] // 4)
    units = Spread(copies, local, shards, units_own, all_units)
    down = Spread(copies, local, shards, down_own, all_down)

    small.start()
    w_in.start()
    w_out.start()
    for offset in far:
        small.arrive(offset)
    w_in.arrive(1)
    w_in.arrive(far[0])
    for load in loads:
        load.wait()
    own_columns(copies.rep, wide, units_own)
    for offset in far[1:]:
        w_in.arrive(offset)
    w_out.arrive(1)
    for offset in far:
        w_out.arrive(offset)
    units.start()
    small.finish()
    gains_ref[...] = jnp.concatenate([small_all[at] for at in range(shards)], axis=1)
    gain_one = gains_ref[0:1]
    for offset in far:
        w_in.arrive(offset + 1)
    for offset in far:
        w_out.arrive(offset + 1)

    slot_id = copies.rep * shards + copies.place
    for micro in range(rows // slot):
        length = lengths_ref[micro, slot_id]
        for start in range(0, slot, 64):
            held = slice(micro * slot + start, micro * slot + start + 64)
            at = start + lax.broadcasted_iota(jnp.int32, (64, features), 0)
            cot_live[held] = jnp.where(at < length, cot_ref[held].astype(F32), 0.0).astype(LOW)
    own_cot = local.copy(cot_live, all_cot.at[0])
    cot_core = copies.send(cot_live, all_cot.at[1], 1, 0)
    cot_across = copies.send(cot_live, all_cot.at[2], 2, 0)

    def first(at):
        act_one[at] = normed(rows_ref[at].astype(F32), gain_one).astype(LOW)

    row_loop(rows, 64, first)
    units.arrive(far[0])
    down.start()
    order = [1, *far, *[offset + 1 for offset in far]]
    for offset in order:
        w_in.cross(offset)
    for offset in far[1:-1]:
        units.arrive(offset)
    for offset in order:
        w_out.cross(offset)
    w_in.finish()

    width = features // 4
    for part in range(4):
        at = part * width
        part_b, part_c, part_x, _, convolved = mixer_columns(
            act_one[...], v_in, gains_ref, at, width, features, slot
        )
        for index, values in enumerate((part_b, part_c, part_x)):
            parts[index, :, at : at + width] = values
        mixer_in[:, at : at + width] = (part_c * convolved).astype(LOW)
        if part == 1:
            units.arrive(far[-1])
    down.arrive(far[0])
    keeps = [
        local.copy(v_in, all_in),
        local.copy(act_one, kept_low.at[0]),
        local.copy(mixer_in, kept_low.at[1]),
        local.copy(parts, kept_parts),
    ]
    w_out.finish()
    keeps.append(local.copy(v_out, all_out))
    spread = []
    for start in range(0, rows, slot):
        held = slice(start, start + slot)
        hstate = rows_ref[held].astype(F32) + dot(
            mixer_in[held], v_out[...].reshape(features, features)
        )
        state[held] = hstate
        act_two[held] = normed(hstate, gains_ref[1:2]).astype(LOW)
        block = act_two.at[held]
        spread.append(
            (
                held,
                copies.send(block, all_act.at[2, held], 2, 0),
                copies.send(block, all_act.at[1, held], 1, 0),
                local.copy(block, all_act.at[0, held]),
            )
        )
    keeps.append(local.copy(state, kept_state))
    for offset in far[1:]:
        down.arrive(offset)
    cot_across.wait_recv()
    corner = [copies.send(all_cot.at[2], all_cot.at[3], 1, 0)]
    for held, across, _, _ in spread:
        across.wait_recv()
        corner.append(copies.send(all_act.at[2, held], all_act.at[3, held], 1, 0))
    units.finish()
    down.finish()
    cot_core.wait_recv()
    for _, _, core, own in spread:
        core.wait_recv()
        own.wait()
    for copy in corner:
        copy.wait_recv()
    own_cot.wait()
    for keep in keeps:
        keep.wait()
    copies.close()


def run_forward(lengths, rows, cot, small, w_in, w_out, w_gate, w_up, w_down, slot):
    shards = lax.axis_size("fsdp")
    count, features = rows.shape
    part = w_in.shape[0]
    down = w_down.shape[1:]
    units = (part, 2 * shards * down[0])
    shapes = [
        (shards, *w_in.shape),
        (shards, *w_out.shape),
        (shards, *units),
        (shards, *down),
        (4, count, features),
        (4, count, features),
        (2, count, features),
    ]
    hbm = pl.BlockSpec(memory_space=pltpu.HBM)
    vmem = pl.BlockSpec(memory_space=pltpu.VMEM)
    smem = pl.BlockSpec(memory_space=pltpu.SMEM)
    hops = 12 * shards + 24
    return pl.pallas_call(
        functools.partial(forward_kernel, slot),
        out_shape=[jax.ShapeDtypeStruct(shape, LOW) for shape in shapes]
        + [
            jax.ShapeDtypeStruct(shape, F32)
            for shape in ((3, count, features), (count, features), (8, features))
        ],
        in_specs=[smem, vmem, vmem, vmem, hbm, hbm, hbm, hbm, hbm],
        out_specs=[hbm] * 9 + [vmem],
        scratch_shapes=[
            pltpu.VMEM((shards, 8, part), F32),
            pltpu.VMEM((shards, *w_in.shape), LOW),
            pltpu.VMEM((shards, *w_out.shape), LOW),
            pltpu.VMEM((count, features), LOW),
            pltpu.VMEM((count, features), LOW),
            pltpu.VMEM((count, features), LOW),
            pltpu.VMEM((count, features), LOW),
            pltpu.VMEM((2, *w_gate.shape), LOW),
            pltpu.VMEM(units, LOW),
            pltpu.VMEM(down, LOW),
            pltpu.VMEM((3, count, features), F32),
            pltpu.VMEM((count, features), F32),
            pltpu.SemaphoreType.DMA((hops,)),
            pltpu.SemaphoreType.DMA((hops,)),
            pltpu.SemaphoreType.DMA((24,)),
        ],
        compiler_params=pltpu.CompilerParams(
            collective_id=0, has_side_effects=True, vmem_limit_bytes=56 << 20
        ),
        name="forward",
    )(lengths, rows, cot, small, w_in, w_out, w_gate, w_up, w_down)


def add_into(target, *others):
    rows = target.shape[-2]
    step = next((size for size in (64, 48, 16) if rows % size == 0), rows)
    kind = target.dtype if len(others) == 1 else F32

    @pl.loop(0, rows // step)
    def _(at):
        held = pl.ds(pl.multiple_of(at * step, step), step)
        total = target[held].astype(kind)
        for other in others:
            total = total + other[held].astype(kind)
        target[held] = total.astype(target.dtype)


class Collect:
    def __init__(self, copies, shards, sent_at, own_at, near_in, far_in):
        self.copies = copies
        self.sent_at, self.own_at = sent_at, own_at
        self.near_in, self.far_in = near_in, far_in
        self.order = list(range(shards - 2, -1, -2))
        self.arriving = {}
        self.far = {}

    def near(self, offset, lanes=slice(None)):
        copy = self.copies.send(
            lambda: self.sent_at(offset + 1).at[:, lanes],
            lambda: self.near_in.at[offset // 2, :, lanes],
            0,
            1,
        )
        self.arriving.setdefault(offset, []).append(copy)

    def near_all(self):
        for offset in self.order:
            self.near(offset)

    def combine(self, offset):
        copies = self.copies
        for copy in self.arriving[offset]:
            copy.wait_recv()
        own = self.own_at(offset)
        add_into(own, self.near_in.at[offset // 2])
        if not offset:
            return
        source = lambda: self.own_at(offset)
        target = lambda: self.far_in.at[offset // 2 - 1]
        if copies.relays and offset == 6:
            self.far[6] = copies.plan(source, target, 0, 6, copies.inner)
            self.relay = copies.plan(source, lambda: self.far_in.at[3], 0, 2, copies.outer)
            self.far[6].start()
            self.relay.start()
            return
        if copies.relays and offset == 4:

            @pl.when(copies.inner)
            def _():
                self.relay.wait_recv()
                add_into(self.own_at(4), self.far_in.at[3])

        self.far[offset] = copies.send(source, target, 0, offset)

    def combine_all(self):
        for offset in self.order:
            self.combine(offset)

    def total(self):
        copies = self.copies
        relayed = [6] if copies.relays else []
        for offset, copy in self.far.items():
            if offset not in relayed:
                copy.wait_recv()
        if not relayed:
            add_into(self.own_at(0), *[self.far_in.at[k] for k in range(len(self.far))])
            return self.own_at(0)

        @pl.when(copies.inner)
        def _():
            self.far[6].wait_recv()
            add_into(self.own_at(0), *[self.far_in.at[k] for k in range(3)])

        @pl.when(copies.outer)
        def _():
            add_into(self.own_at(0), *[self.far_in.at[k] for k in range(2)])

        return self.own_at(0)


class Share:
    def __init__(self, copies, local, collect, target_at):
        self.copies = copies
        self.target_at = target_at
        collect.total()
        source = lambda: collect.own_at(0)
        here = lambda: target_at(copies.rep)
        self.across = copies.send(source, here, 2, 0)
        self.core = [copies.send(source, here, 1, 0)]
        self.own = local.copy(source(), here())

    def settle(self):
        self.own.wait()
        self.own = None

    def forward(self):
        self.across.wait_recv()
        block = lambda: self.target_at(flipped(self.copies.rep, 2))
        self.core.append(self.copies.send(block, block, 1, 0))

    def finish(self):
        for copy in self.core:
            copy.wait_recv()
        if self.own is not None:
            self.own.wait()


class CollectAll:
    def __init__(self, copies, shards, width, parts, core_in, cross_in, near_in, far_in):
        self.copies = copies
        self.width = width
        self.parts, self.core_in, self.cross_in = parts, core_in, cross_in
        place = copies.place
        self.collect = Collect(
            copies,
            shards,
            lambda offset: parts.at[0, flipped(place, offset)],
            lambda offset: parts.at[0, flipped(place, offset)],
            near_in,
            far_in,
        )
        self.core = {}
        self.cross = {}
        self.near_ready = False
        self.order = [o + 1 for o in self.collect.order] + self.collect.order

    def compute(self, turn, left, right):
        rep = flipped(self.copies.rep, turn)
        shards, rows, _ = self.parts.shape[1:]
        for at in range(0, self.width, 256):
            columns = pl.ds(pl.multiple_of(rep * self.width + at, 256), 256)
            block = dot_first(left[...], right[:, columns]).astype(LOW)
            self.parts[turn, :, :, at : at + 256] = block.reshape(shards, rows, 256)

    def to_core(self, turn):
        self.core[turn - 1] = self.copies.send(
            lambda: self.parts.at[turn], lambda: self.core_in.at[turn // 2], 1, 0
        )

    def to_cross(self):
        self.core[2].wait_recv()
        place = self.copies.place
        for offset in self.order:
            block = self.parts.at[2, flipped(place, offset)]
            add_into(block, self.core_in.at[1, flipped(place, offset)])
            self.cross_one(offset)

    def cross_one(self, offset):
        place = self.copies.place
        self.cross[offset] = self.copies.send(
            lambda: self.parts.at[2, flipped(place, offset)],
            lambda: self.cross_in.at[flipped(place, offset)],
            2,
            0,
        )

    def arrive(self, offset):
        if not self.near_ready:
            self.core[0].wait_recv()
            self.near_ready = True
        self.cross[offset].wait_recv()
        shard = flipped(self.copies.place, offset)
        add_into(self.parts.at[0, shard], self.core_in.at[0, shard], self.cross_in.at[shard])

    def near_all(self):
        for offset in self.collect.order:
            self.arrive(offset + 1)
            self.collect.near(offset)

    def combine_all(self):
        for offset in self.collect.order:
            self.arrive(offset)
            self.collect.combine(offset)


def feed_forward_rows(act, cot, units, down, hidden, d_units, width):
    act_rows, cot_rows = act[...], cot[...]
    step = 256

    def columns(at, size):
        lanes, up_lanes = pl.ds(at, size), pl.ds(width + at, size)
        gate_pre = dot(act_rows, units[:, lanes])
        up_pre = dot(act_rows, units[:, up_lanes])
        d_hidden = dot_last(cot_rows, down[lanes])
        sigmoid_g = jax.nn.sigmoid(gate_pre)
        silu_g = gate_pre * sigmoid_g
        hidden[:, lanes] = (silu_g * up_pre).astype(LOW)
        d_units[:, lanes] = (
            d_hidden * up_pre * sigmoid_g * (1.0 + gate_pre * (1.0 - sigmoid_g))
        ).astype(LOW)
        d_units[:, up_lanes] = (d_hidden * silu_g).astype(LOW)

    @pl.loop(0, width // step)
    def _(at):
        columns(pl.multiple_of(at * step, 128), step)

    if width % step:
        columns(width - width % step, width % step)


def put_shards(target, columns, block):
    shards, rows = target.shape[:2]
    if rows % 16 == 0:
        target[:, :, columns] = block.reshape(shards, rows, block.shape[1])
    else:
        for shard in range(shards):
            target[shard, :, columns] = block[shard * rows : (shard + 1) * rows]


def backward_kernel(
    slot,
    all_rows_ref, gains_ref, in_ref, out_ref, units_ref, down_ref, act_ref, cot_ref,
    kept_low, kept_parts, kept_state,
    outputs_ref, d_rows_ref, down_sum, units_sum, in_sum, out_sum, small_sum, ffn_in,
    d_act, d_core, d_cross, down_grad, down_near, down_far, units_grad, units_near, units_far,
    w_out_core, w_out_cross, w_out_near, w_out_far,
    w_in_core, w_in_cross, w_in_near, w_in_far,
    small, small_in, send_sems, recv_sems, local_sems,
):
    rows, features = all_rows_ref.shape
    shards = units_grad.shape[0]
    units_width = down_ref.shape[0]
    copies = Copies(send_sems, recv_sems)
    local = Local(local_sems)
    place = copies.place
    far = list(range(2, shards, 2))
    bits = [1 << k for k in range(1, shards.bit_length() - 1)]
    peers = [(0, offset) for offset in [*far, 1]] + [(1, 0), (2, 0)]

    def collector(grad, near, far_in):
        at = lambda offset: grad.at[flipped(place, offset)]
        return Collect(copies, shards, at, at, near, far_in)

    down = collector(down_grad, down_near, down_far)
    units = collector(units_grad, units_near, units_far)
    d_near, d_far, ffn_near, down_share = {}, [], {}, []

    def feed_forward(m_units, m_down, act, cot, hidden, d_units):
        part = lambda ref, turn: ref.at[turn * rows : (turn + 1) * rows]
        loads = {"units": local.copy(units_ref, m_units)}
        for turn in (3, 2, 1, 0):
            loads[turn] = [
                local.copy(act_ref.at[turn], part(act, turn)),
                local.copy(cot_ref.at[turn], part(cot, turn)),
            ]
            if turn == 3:
                loads["down"] = local.copy(down_ref, m_down)

        copies.meet(peers)

        def units_of(turn):
            for load in loads[turn]:
                load.wait()
            if turn == 3:
                loads["units"].wait()
                loads["down"].wait()
            feed_forward_rows(
                part(act, turn), part(cot, turn), m_units, m_down,
                part(hidden, turn), part(d_units, turn), units_width,
            )

        def d_act_of(turn):
            block = part(d_units, turn)
            d_act[turn] = dot_last(block[...], m_units[...]).astype(LOW)
            if turn % 2:
                d_near[turn] = copies.send(
                    lambda: d_act.at[turn], lambda: d_core.at[turn // 2], 1, 0
                )

        def send_across(held):
            return copies.send(lambda: d_act.at[2, held], lambda: d_cross.at[held], 2, 0)

        def ffn_of(turn):
            block = part(hidden, turn)
            block[:, :features] = dot(block[...], m_down[...]).astype(LOW)
            if turn % 2:
                ffn_near[turn] = copies.send(
                    lambda: part(hidden, turn).at[:, :features],
                    lambda: ffn_in.at[turn // 2],
                    1,
                    0,
                )

        per = 256 * shards // features

        def units_grad_of(chunk):
            base = flipped(place // per, chunk) * per
            lanes = pl.ds(pl.multiple_of(base * (features // shards), 256), 256)
            block = dot_first(act[:, lanes], d_units[...]).astype(LOW)
            units_grad[pl.ds(base, per)] = block.reshape(per, -1, block.shape[1])
            for offset in units.order:
                if offset // per == chunk:
                    units.near(offset)

        for turn in (3, 2):
            units_of(turn)
            d_act_of(turn)
        d_near[3].wait_recv()
        for start in range(0, rows, slot):
            held = slice(start, start + slot)
            add_into(d_act.at[2, held], d_core.at[1, held])
            d_far.append(send_across(held))
        for turn in (1, 0):
            units_of(turn)
        wide = 512 if shards == 8 else 256
        for at in range(0, features, wide):
            lanes = slice(at, at + wide)
            put_shards(down_grad, lanes, dot_first(hidden[...], cot[:, lanes]).astype(LOW))
            for offset in down.order:
                down.near(offset, lanes)
        ffn_of(3)
        ffn_of(2)
        chunks = list(range(features // 256))[::-1]
        units_grad_of(chunks[0])

        copies.sent(d_near[3])
        ffn_near[3].wait_recv()
        load = local.copy(ffn_in.at[1], d_act.at[3])
        units_grad_of(chunks[1])
        load.wait()
        add_into(d_act.at[3], part(hidden, 2).at[:, :features])
        across = copies.send(lambda: d_act.at[3], lambda: ffn_in.at[2], 2, 0)
        ffn_near[2] = across
        down.combine(down.order[0])
        for chunk in chunks[2:]:
            units_grad_of(chunk)
        d_act_of(1)
        down.combine(down.order[1])
        d_act_of(0)
        ffn_of(1)
        down.combine(down.order[2])
        copies.sent(d_near[1])
        d_act[1] = dot(part(hidden, 0)[...], m_down[...]).astype(LOW)
        for offset in down.order[3:]:
            down.combine(offset)
        copies.sent(ffn_near[3])
        copies.sent(ffn_near[1])

    pl.run_scoped(
        feed_forward,
        pltpu.VMEM(units_ref.shape, LOW),
        pltpu.VMEM(down_ref.shape, LOW),
        pltpu.VMEM((4 * rows, features), LOW),
        pltpu.VMEM((4 * rows, features), LOW),
        pltpu.VMEM((4 * rows, units_width), LOW),
        pltpu.VMEM((4 * rows, 2 * units_width), LOW),
    )

    def mixer(
        rows_ref, v_in, v_out, act_one, mixer_in, hstate, d_hstate, d_mixer, d_proj, w_out_parts
    ):
        gain_one, gain_two = gains_ref[0:1], gains_ref[1:2]
        load_state = local.copy(kept_state, hstate)
        load_cot = local.copy(cot_ref.at[0], d_mixer)
        load_mixer = local.copy(kept_low.at[1], mixer_in)
        load_out = local.copy(out_ref, v_out)

        width = features // 4
        w_out = CollectAll(
            copies, shards, width, w_out_parts, w_out_core, w_out_cross, w_out_near, w_out_far
        )

        def columns_back(part_b, part_c, part_x):
            load_parts = [
                local.copy(kept_parts.at[index], target)
                for index, target in enumerate((part_b, part_c, part_x))
            ]
            load_act = local.copy(kept_low.at[0], act_one)
            load_in = local.copy(in_ref, v_in)
            load_rows = local.copy(all_rows_ref, rows_ref)
            load_state.wait()

            d_near[1].wait_recv()
            small[0] = jnp.zeros((8, features), F32)

            def second(at):
                d_now = (
                    d_act[0, at].astype(F32) + d_core[0, at].astype(F32) + d_cross[at].astype(F32)
                )
                values = hstate[at]
                scale = rms_scale(values)
                small[0, 1:2] += jnp.sum(d_now * values * scale, axis=0, keepdims=True)
                d_values = d_mixer[at].astype(F32) + norm_back(d_now, values, scale, gain_two)
                d_hstate[at] = d_values
                d_mixer[at] = d_values.astype(LOW)

            for copy in d_far:
                copy.wait_recv()
            load_cot.wait()
            row_loop(rows, 64, second)
            load_mixer.wait()
            load_out.wait()
            for load in load_parts:
                load.wait()

            for turn in (3, 1):
                w_out.compute(turn, mixer_in, d_mixer)
                w_out.to_core(turn)
            for turn in (2, 0):
                w_out.compute(turn, mixer_in, d_mixer)

            per = shards * width // features
            for part in range(4):
                at = part * width
                lanes = slice(at, at + width)
                block = v_out[part * per : (part + 1) * per].reshape(width, features)
                d_mixin = dot_last(d_mixer[...], block)
                taps = [gains_ref[2 + k : 3 + k, lanes] for k in range(3)]
                for start in range(0, rows, slot):
                    held = slice(start, start + slot)
                    d_mix = d_mixin[held]
                    b_now, c_now, x_now = part_b[held, lanes], part_c[held, lanes], part_x[held, lanes]
                    product = b_now * x_now
                    before = [shifted(product, 2), shifted(product, 1), product]
                    convolved = taps[0] * before[0] + taps[1] * before[1] + taps[2] * before[2]
                    d_conv = d_mix * c_now
                    for k in range(3):
                        small[0, 2 + k : 3 + k, lanes] += jnp.sum(
                            d_conv * before[k], axis=0, keepdims=True
                        )
                    d_product = (
                        taps[2] * d_conv
                        + taps[1] * shifted(d_conv, -1)
                        + taps[0] * shifted(d_conv, -2)
                    )
                    d_proj[held, lanes] = (d_product * x_now).astype(LOW)
                    d_proj[held, features + at : features + at + width] = (d_mix * convolved).astype(LOW)
                    d_proj[held, 2 * features + at : 2 * features + at + width] = (
                        d_product * b_now
                    ).astype(LOW)
                if part == 0:
                    w_out.to_cross()
                if part == 1:
                    units.combine(units.order[0])
                    down_share.append(Share(copies, local, down, lambda at: down_sum.at[at]))
                    down_share[0].settle()

            load_act.wait()
            load_in.wait()
            load_rows.wait()

        pl.run_scoped(columns_back, *[pltpu.VMEM((rows, features), F32)] * 3)

        def finish(w_in_parts):
            w_in = CollectAll(
                copies, shards, 3 * width, w_in_parts, w_in_core, w_in_cross, w_in_near, w_in_far
            )
            w_in.compute(3, act_one, d_proj)
            w_in.to_core(3)
            w_in.compute(2, act_one, d_proj)
            w_in.to_cross()
            w_in.compute(1, act_one, d_proj)
            w_in.to_core(1)
            w_in.compute(0, act_one, d_proj)
            units.combine(units.order[1])

            def rows_back(start):
                held = slice(start, start + slot)
                d_now = dot_last(d_proj[held], v_in[...].reshape(features, 3 * features))
                values = rows_ref[held].astype(F32)
                scale = rms_scale(values)
                small[0, 0:1] += jnp.sum(d_now * values * scale, axis=0, keepdims=True)
                d_hstate[held] += norm_back(d_now, values, scale, gain_one)

            hops = [(0, 1), *[(0, bit) for bit in bits], (1, 0), (2, 0)]
            flight, summed = [], []

            def small_hop():
                step = len(flight)
                if len(summed) < step:
                    flight[-1].wait_recv()
                    small[step] = small[step - 1] + small_in[step - 1]
                    summed.append(step)
                if step < len(hops):
                    flight.append(copies.send(small.at[step], small_in.at[step], *hops[step]))

            def columns(target, width):
                return lambda at: target.at[:, pl.ds(pl.multiple_of(at * width, width), width)]

            starts = list(range(0, rows, slot))
            for start in starts[:-1]:
                rows_back(start)
            units.combine(units.order[2])
            w_out.near_all()
            rows_back(starts[-1])
            d_out = local.copy(d_hstate, d_rows_ref)
            small_hop()

            ffn_near[1].wait_recv()
            ffn_near[2].wait_recv()
            for copy in d_far:
                copies.sent(copy)
            loads = [
                local.copy(ffn_in.at[0], d_act.at[0]),
                local.copy(ffn_in.at[2], d_act.at[2]),
            ]
            for load in loads:
                load.wait()
            small_hop()
            add_into(hstate, d_act.at[1], d_act.at[0], d_act.at[2])
            put_out = local.copy(hstate, outputs_ref)
            small_hop()
            for offset in units.order[3:]:
                units.combine(offset)
            w_in.near_all()
            small_hop()
            units_share = Share(copies, local, units, lambda at: units_sum.at[at])
            w_out.combine_all()
            small_hop()
            for offset in w_in.collect.order:
                w_in.arrive(offset)
                w_in.collect.combine(offset)
                if offset == w_in.collect.order[1]:
                    out_share = Share(copies, local, w_out.collect, columns(out_sum, width))
            while len(summed) < len(hops):
                small_hop()
            small_sum[...] = small[len(hops)]
            in_share = Share(copies, local, w_in.collect, columns(in_sum, 3 * width))
            shares = [down_share[0], units_share, out_share, in_share]
            for share in shares:
                share.forward()
            for share in shares:
                share.finish()
            put_out.wait()
            d_out.wait()
            copies.close()

        pl.run_scoped(finish, pltpu.VMEM((4, shards, part_rows, 3 * width), LOW))

    whole = (rows, features)
    part_rows = in_ref.shape[1]
    pl.run_scoped(
        mixer,
        pltpu.VMEM(whole, LOW),
        pltpu.VMEM(in_ref.shape, LOW),
        pltpu.VMEM(out_ref.shape, LOW),
        pltpu.VMEM(whole, LOW),
        pltpu.VMEM(whole, LOW),
        pltpu.VMEM(whole, F32),
        pltpu.VMEM(whole, F32),
        pltpu.VMEM(whole, LOW),
        pltpu.VMEM((rows, 3 * features), LOW),
        pltpu.VMEM((4, shards, part_rows, features // 4), LOW),
    )


def run_backward(rows, gains, m_in, m_out, m_units, m_down, act, cot, kept, slot):
    count, features = rows.shape
    shards, part = m_in.shape[:2]
    cut = m_down.shape[0] // shards
    units = m_units.shape[1]
    half = shards // 2
    hbm = pl.BlockSpec(memory_space=pltpu.HBM)
    vmem = pl.BlockSpec(memory_space=pltpu.VMEM)
    hops = 10 * shards + 40
    depth = shards.bit_length() + 1

    def blocks(*shape):
        return [
            pltpu.VMEM((half, *shape), LOW),
            pltpu.VMEM((half if shards == 8 else half - 1, *shape), LOW),
        ]

    def quarters(width):
        return [
            pltpu.VMEM((2, shards, part, width), LOW),
            pltpu.VMEM((shards, part, width), LOW),
            *blocks(part, width),
        ]

    whole = (count, features)
    return pl.pallas_call(
        functools.partial(backward_kernel, slot),
        out_shape=[
            jax.ShapeDtypeStruct(*shape)
            for shape in (
                (whole, F32),
                (whole, F32),
                ((4, cut, features), LOW),
                ((4, part, units), LOW),
                ((part, 3 * features), LOW),
                ((part, features), LOW),
                ((8, features), F32),
                ((3, *whole), LOW),
            )
        ],
        in_specs=[hbm, vmem] + [hbm] * 9,
        out_specs=[hbm] * 6 + [vmem, hbm],
        scratch_shapes=[
            pltpu.VMEM((4, *whole), LOW),
            pltpu.VMEM((2, *whole), LOW),
            pltpu.VMEM(whole, LOW),
            pltpu.VMEM((shards, cut, features), LOW),
            *blocks(cut, features),
            pltpu.VMEM((shards, part, units), LOW),
            *blocks(part, units),
            *quarters(features // 4),
            *quarters(3 * features // 4),
            pltpu.VMEM((depth + 1, 8, features), F32),
            pltpu.VMEM((depth, 8, features), F32),
            pltpu.SemaphoreType.DMA((hops,)),
            pltpu.SemaphoreType.DMA((hops,)),
            pltpu.SemaphoreType.DMA((48,)),
        ],
        compiler_params=pltpu.CompilerParams(
            collective_id=1, has_side_effects=True, vmem_limit_bytes=127 << 19
        ),
        name="backward",
    )(rows, gains, m_in, m_out, m_units, m_down, act, cot, *kept)


def finish_kernel(
    cut, units_ref, down_ref, in_ref, out_ref, rows_ref, d_rows_ref, small_ref,
    gate_out, up_out, down_out, in_out, out_out, rows_out, d_rows_out, one_out, conv_out, two_out,
):
    half = units_ref.shape[2] // 2
    for side, target in enumerate((gate_out, up_out)):
        for at in range(half // cut):
            for quarter in range(4):
                start = (4 * at + quarter) * cut
                target[:, start : start + cut] = units_ref[
                    quarter, :, side * half + at * cut : side * half + (at + 1) * cut
                ].astype(F32)
    down_out[...] = down_ref[...].astype(F32)
    in_out[...] = in_ref[...].astype(F32)
    out_out[...] = out_ref[...].astype(F32)
    rows_out[...] = rows_ref[...]
    d_rows_out[...] = d_rows_ref[...]
    part = one_out.shape[1]
    start = lax.axis_index("fsdp") * part if small_ref.shape[1] > part else 0
    lanes = pl.ds(pl.multiple_of(start, 128), part) if small_ref.shape[1] > part else slice(None)
    one_out[...] = small_ref[0:1, lanes]
    two_out[...] = small_ref[1:2, lanes]
    conv_out[...] = small_ref[2:5, lanes]


def run_finish(units, down, w_in, w_out, outputs, d_rows, small):
    part, columns = units.shape[1:]
    cut, features = down.shape[1:]
    down = down.reshape(4 * cut, features)
    steps = 4 if part % 64 == 0 and cut % 16 == 0 else 1

    if part % 128:
        small = lax.dynamic_slice_in_dim(small, lax.axis_index("fsdp") * part, part, 1)

    def rows(array):
        return pl.BlockSpec((array.shape[0] // steps, array.shape[1]), lambda at: (at, 0))

    def same(array):
        return pl.BlockSpec(array.shape, lambda at: (0, 0))

    wide = jax.ShapeDtypeStruct((part, 2 * columns), F32)
    narrow = (down, w_in, w_out, outputs, d_rows)
    outs = [wide, wide, *[jax.ShapeDtypeStruct(array.shape, F32) for array in narrow]]
    sums = [jax.ShapeDtypeStruct((count, part), F32) for count in (1, 3, 1)]
    return pl.pallas_call(
        functools.partial(finish_kernel, cut),
        grid=(steps,),
        out_shape=[*outs, *sums],
        in_specs=[
            pl.BlockSpec((4, part // steps, columns), lambda at: (0, at, 0)),
            *[rows(array) for array in narrow],
            same(small),
        ],
        out_specs=[*[rows(out) for out in outs], *[same(out) for out in sums]],
        compiler_params=pltpu.CompilerParams(vmem_limit_bytes=62 << 20),
        name="finish",
    )(units, *narrow, small)


def on_device(
    inputs, cotangent, lengths, norm_one, w_in, conv_w, w_out, norm_two, w_gate, w_up, w_down
):
    micro_count, tok_rows, features = inputs.shape
    shards = lax.axis_size("fsdp")
    all_rows = micro_count * tok_rows
    cut = w_down.shape[0] // 4
    part = w_in.shape[0]
    part_ff = shards * cut

    small = jnp.concatenate([norm_one[None], norm_two[None], conv_w, jnp.zeros_like(conv_w)])
    rows_low = inputs.reshape(all_rows, features)
    m_in, m_out, m_units, m_down, act_all, cot_all, *kept, gains = run_forward(
        lengths, rows_low, cotangent.reshape(all_rows, features), small.astype(F32),
        w_in, w_out, w_gate, w_up, w_down.reshape(4, cut, features), tok_rows,
    )

    outputs, d_rows, down_sum, units_sum, in_sum, out_sum, small_sum, _ = run_backward(
        rows_low, gains, m_in, m_out, m_units.reshape(features, 2 * part_ff),
        m_down.reshape(part_ff, features), act_all, cot_all, kept, tok_rows,
    )
    d_gate, d_up, d_down, d_in, d_out, outputs, d_rows, d_one, d_conv, d_two = run_finish(
        units_sum, down_sum, in_sum, out_sum, outputs, d_rows, small_sum
    )
    return (
        outputs.reshape(inputs.shape),
        d_rows.reshape(inputs.shape),
        d_one[0],
        d_in,
        d_conv,
        d_out,
        d_two[0],
        d_gate,
        d_up,
        d_down,
    )


def solution(mesh):
    return jax.shard_map(
        on_device,
        mesh=mesh,
        in_specs=(
            P(None, ("rep", "fsdp"), None),
            P(None, ("rep", "fsdp"), None),
            P(),
            P("fsdp"),
            P("fsdp", None),
            P(None, "fsdp"),
            P("fsdp", None),
            P("fsdp"),
            P("fsdp", None),
            P("fsdp", None),
            P("fsdp", None),
        ),
        out_specs=(
            P(None, ("rep", "fsdp"), None),
            P(None, ("rep", "fsdp"), None),
            P("fsdp"),
            P("fsdp", None),
            P(None, "fsdp"),
            P("fsdp", None),
            P("fsdp"),
            P("fsdp", None),
            P("fsdp", None),
            P("fsdp", None),
        ),
        check_vma=False,
    )
```
